256 devices in a mesh: gx: 4 (over y), gy: 8 (over x, core), gz: 8 (over z).
Axes of the slice: x: 4, y: 4, z: 8, core: 2. Of those that a mesh axis runs over, the one named last changes fastest.
Arguments:
- earlier_edge_voltage: float32 [6, 32, 128, 2048], P(None, 'gx', 'gy', 'gz'), may hold values from -6 to 6
- coil_drive_current: float32 [6, 32, 128, 2048], P(None, 'gx', 'gy', 'gz'), may hold values from -18 to 18
- sigma_omega_cellwise: float32 [32, 128, 2048], P('gx', 'gy', 'gz'), may hold values from 0.2 to 3
- subdomain_inverse_full: bfloat16 [4, 8, 8, 16, 512, 512], P('gx', 'gy', 'gz'), may hold values from -0.25 to 0.25
- subdomain_inverse_main: float32 [4, 8, 8, 16, 512], P('gx', 'gy', 'gz'), may hold values from 0.25 to 1.75
- subdomain_layer_counts: int32 [4, 8, 8, 16], P('gx', 'gy', 'gz'), may hold values from 1 to 19, 256 in all within a row
- heat_layer_lookup: int32 [8, 32], P('gz'), may hold values from 1 to 24, 256 in all within a row
- warming_amount: float32 [4, 8, 8, 24, 32, 128], P('gx', 'gy', 'gz'), may hold values from 0 to 2
- heat_spreading_coef: float32 [4, 8, 8, 24, 32, 128], P('gx', 'gy', 'gz'), may hold values from 0.25 to 1
Outputs:
- field_new: float32 [6, 32, 128, 2048], P(None, 'gx', 'gy', 'gz')
- renewed_heat_rise: float32 [4, 8, 8, 24, 32, 128], P('gx', 'gy', 'gz')
- renewed_sigma_omega: float32 [32, 128, 2048], P('gx', 'gy', 'gz')
The draws below stay inside these ranges and needn't reach their ends.
Inputs may be any that keep to these rules, and one draw needn't show every extreme that they name: `subdomain_layer_counts`: each device's 16 segment lengths sum to 256, and every device has a segment of exactly 19 planes. `heat_layer_lookup`: each row sums to 256, and every row has a slab of exactly 24 planes.
All inputs are finite; a program needn't handle non-finite values.
Results may differ from the reference program's by a relative error of at most 0.013.
Values sent between devices are 32-bit elements; how exact they have to be, the bound alone decides.
No kernel may reach another device: no remote copies, remote signals or barrier semaphores. Data moves between devices by JAX's collectives and lax.ppermute only.
A program may use at most 128 MiB of HBM per device.

```python
import math
import jax
import jax.numpy as jnp
import numpy as np
from jax import lax

CX = 8
CY = 16
CZ = 256
NSEG = 16
BLK = 512
SWEEPS = 2
SECTIONS = 4
MAXSEG = 19
NTH = 32
LAYER_CAP_HEAT = 24
VOXELS_ALONG_X = 32
VOXELS_ALONG_Y = 128
NZ = 2048
N_GX = 4
N_GY = 8
N_GZ = 8


def level_of(stream_key, extent, pieces, least, top_value):
    level, own = 1.0, jax.random.fold_in(stream_key, 6)
    for axis_at, blocks in pieces:
        heights = jnp.exp(jax.random.uniform(jax.random.fold_in(own, axis_at), (blocks,), jnp.float32, least / len(pieces), top_value / len(pieces)))
        level = level * jnp.repeat(heights, extent[axis_at] // blocks).reshape([-1 if axis == axis_at else 1 for axis in range(len(extent))])
    return level


def profile(number_of, total, limit, slope):
    loads = [(1 << 20) // math.isqrt(rank ** slope) + 1 for rank in range(2, number_of + 1)]
    spare, counts = total - limit - (number_of - 1), [1] * (number_of - 1)
    while spare > 0:
        movable = [i for i in range(number_of - 1) if counts[i] < limit]
        mass, left = sum([loads[i] for i in movable]), spare
        for i in movable:
            more = min(limit - counts[i], max(1, left * loads[i] // mass), spare)
            counts[i] = counts[i] + more
            spare = spare - more
    return np.array([limit] + counts)


def ragged(key, count, total, limit, lean):
    if count == 2:
        one = jax.random.randint(key, (), max(1, total - limit), min(limit, total - 1) + 1)
        return jnp.stack([one, total - one])
    lengths = jnp.asarray(profile(count, total, limit, lean), jnp.int32)
    couples = (count - 1) // 2
    giver, taker = lengths[1:1 + 2 * couples:2], lengths[2:2 + 2 * couples:2]
    slack = jnp.minimum(giver - 1, limit - taker)
    passed = jax.random.randint(jax.random.fold_in(key, 1), (couples,), 0, 1 << 20) % (slack + 1)
    lengths = lengths.at[1:1 + 2 * couples:2].set(giver - passed).at[2:2 + 2 * couples:2].set(taker + passed)
    return lengths[jax.random.permutation(jax.random.fold_in(key, 2), count)]


def normal_values(rng, dims, deviation, bound, shards=(), kind=jnp.bfloat16):
    loudness = level_of(rng, dims, shards, -0.22, 0.18) if shards else 1.0
    result = jax.random.normal(rng, dims, jnp.float32) * deviation * loudness
    return jnp.minimum(jnp.maximum(result, -bound), bound).astype(kind)


def setup_inputs(seed: int = 0) -> dict:
    key_list = jax.random.split(jax.random.key(seed), 10)
    earlier_edge_voltage = normal_values(key_list[0], (6, VOXELS_ALONG_X, VOXELS_ALONG_Y, NZ), 1.0, 6.0, ((1, 4), (2, 8), (3, 8)), jnp.float32)
    coil_drive_current = normal_values(key_list[1], (6, VOXELS_ALONG_X, VOXELS_ALONG_Y, NZ), 3.0, 18.0, ((1, 4), (2, 8), (3, 8)), jnp.float32)
    sigma_omega_cellwise = jnp.clip(jnp.exp(math.log(3.0) - 2.7080502 * jax.random.uniform(key_list[2], (VOXELS_ALONG_X, VOXELS_ALONG_Y, NZ), jnp.float32) ** level_of(key_list[2], (VOXELS_ALONG_X, VOXELS_ALONG_Y, NZ), ((0, 4), (1, 8), (2, 8)), -0.2, 0.2)), 0.2, 3.0)
    subdomain_inverse_full = normal_values(key_list[3], (N_GX, N_GY, N_GZ, NSEG, BLK, BLK), BLK ** -0.5, 0.25, ((0, 4), (1, 8), (2, 8)))
    subdomain_inverse_main = jnp.clip(1.0 + 0.15 * jax.random.normal(key_list[4], (N_GX, N_GY, N_GZ, NSEG, BLK), jnp.float32), 0.25, 1.75)
    subdomain_layer_counts = jax.vmap(lambda own: ragged(own, NSEG, CZ, MAXSEG, 1))(jax.random.split(key_list[5], N_GX * N_GY * N_GZ)).reshape((N_GX, N_GY, N_GZ, NSEG)).astype(jnp.int32)
    heat_layer_lookup = jax.vmap(lambda own: ragged(own, NTH, CZ, LAYER_CAP_HEAT, 2))(jax.random.split(key_list[6], N_GZ)).reshape((N_GZ, NTH)).astype(jnp.int32)
    warming_amount = jnp.clip(2.0 * jax.random.uniform(key_list[7], (N_GX, N_GY, N_GZ, LAYER_CAP_HEAT, VOXELS_ALONG_X, VOXELS_ALONG_Y), jnp.float32) ** level_of(key_list[7], (N_GX, N_GY, N_GZ, LAYER_CAP_HEAT, VOXELS_ALONG_X, VOXELS_ALONG_Y), ((0, 4), (1, 8), (2, 8)), -0.2, 0.2), 0.0, 2.0)
    heat_spreading_coef = jnp.clip(jnp.exp(math.log(1.0) - 1.3862944 * jax.random.uniform(key_list[8], (N_GX, N_GY, N_GZ, LAYER_CAP_HEAT, VOXELS_ALONG_X, VOXELS_ALONG_Y), jnp.float32) ** level_of(key_list[8], (N_GX, N_GY, N_GZ, LAYER_CAP_HEAT, VOXELS_ALONG_X, VOXELS_ALONG_Y), ((0, 4), (1, 8), (2, 8)), -0.2, 0.2)), 0.25, 1.0)
    return {"earlier_edge_voltage": earlier_edge_voltage, "coil_drive_current": coil_drive_current, "sigma_omega_cellwise": sigma_omega_cellwise, "subdomain_inverse_full": subdomain_inverse_full, "subdomain_inverse_main": subdomain_inverse_main, "subdomain_layer_counts": subdomain_layer_counts, "heat_layer_lookup": heat_layer_lookup, "warming_amount": warming_amount, "heat_spreading_coef": heat_spreading_coef}


mass_shift = 1.0
solver_scale = 0.2
coupling_scale = 0.05
time_step = 2.5
heat_drop = 0.15


def curl_curl(padded, conduct):
    size_x = padded.shape[1] - 2
    size_y = padded.shape[2] - 2
    size_z = padded.shape[3] - 2
    vector_parts_count = padded.reshape(2, 3, size_x + 2, size_y + 2, size_z + 2)
    field_x = vector_parts_count[:, 0]
    field_y = vector_parts_count[:, 1]
    field_z = vector_parts_count[:, 2]

    def wide_cut(array, shift_x, shift_y, shift_z):
        return array[:, shift_x:shift_x + size_x + 1, shift_y:shift_y + size_y + 1, shift_z:shift_z + size_z + 1]

    def core_cut(array, shift_x, shift_y, shift_z):
        return array[:, shift_x:shift_x + size_x, shift_y:shift_y + size_y, shift_z:shift_z + size_z]

    face_x = wide_cut(field_z, 0, 1, 0) - wide_cut(field_z, 0, 0, 0) - wide_cut(field_y, 0, 0, 1) + wide_cut(field_y, 0, 0, 0)
    face_y = wide_cut(field_x, 0, 0, 1) - wide_cut(field_x, 0, 0, 0) - wide_cut(field_z, 1, 0, 0) + wide_cut(field_z, 0, 0, 0)
    face_z = wide_cut(field_y, 1, 0, 0) - wide_cut(field_y, 0, 0, 0) - wide_cut(field_x, 0, 1, 0) + wide_cut(field_x, 0, 0, 0)
    curl_x = core_cut(face_z, 1, 1, 1) - core_cut(face_z, 1, 0, 1) - core_cut(face_y, 1, 1, 1) + core_cut(face_y, 1, 1, 0)
    curl_y = core_cut(face_x, 1, 1, 1) - core_cut(face_x, 1, 1, 0) - core_cut(face_z, 1, 1, 1) + core_cut(face_z, 0, 1, 1)
    curl_z = core_cut(face_y, 1, 1, 1) - core_cut(face_y, 0, 1, 1) - core_cut(face_x, 1, 1, 1) + core_cut(face_x, 1, 0, 1)
    curl_all = jnp.stack([curl_x, curl_y, curl_z], axis=1)
    center = vector_parts_count[:, :, 1:-1, 1:-1, 1:-1]
    real_part = curl_all[0] + mass_shift * center[0] - conduct * center[1]
    imag_part = curl_all[1] + mass_shift * center[1] + conduct * center[0]
    return jnp.concatenate([real_part, imag_part], axis=0)


def block_correction(residual, solvers, diagonal, seg_len):
    seg_count = diagonal.shape[0]
    block_width = diagonal.shape[1]
    extent_x = residual.shape[1]
    extent_y = residual.shape[2]
    extent_z = residual.shape[3]
    window_planes = block_width // 24
    used_width = window_planes * 24
    column_x = extent_x // 2
    column_y = extent_y // 2
    starts = (jnp.cumsum(seg_len) - seg_len).astype(jnp.int32)
    offsets = jnp.arange(window_planes, dtype=jnp.int32)
    planes = (starts[:, None] - 1 + offsets[None, :]).astype(jnp.int32)
    inside = (offsets[None, :] <= seg_len[:, None] + 1) & (planes >= 0) & (planes < extent_z)
    plane_rows = jnp.transpose(residual, (3, 0, 1, 2)).reshape(extent_z, 6 * extent_x * extent_y)
    picked = plane_rows[jnp.clip(planes, 0, extent_z - 1)] * inside[:, :, None].astype(jnp.float32)
    picked = picked.reshape(seg_count, window_planes, 6, column_x, 2, column_y, 2)
    picked = jnp.transpose(picked, (0, 3, 5, 1, 2, 4, 6)).reshape(seg_count, column_x * column_y, used_width)
    vectors = jnp.pad(picked, ((0, 0), (0, 0), (0, block_width - used_width))).astype(jnp.bfloat16)
    product = jnp.einsum("sij,scj->sci", solvers.astype(jnp.float32), vectors.astype(jnp.float32))
    solved = coupling_scale * product + solver_scale * diagonal[:, None, :] * vectors.astype(jnp.float32)
    restored = solved[:, :, :used_width].reshape(seg_count, column_x, column_y, window_planes, 6, 2, 2)
    restored = jnp.transpose(restored, (0, 3, 4, 1, 5, 2, 6)).reshape(seg_count * window_planes, 6 * extent_x * extent_y)
    plane_ids = jnp.arange(extent_z, dtype=jnp.int32)
    owner_seg = jnp.sum((starts[None, :] <= plane_ids[:, None]).astype(jnp.int32), axis=1) - 1
    seg_ids = jnp.arange(seg_count, dtype=jnp.int32)
    own_start = jnp.sum(jnp.where(owner_seg[:, None] == seg_ids[None, :], starts[None, :], 0), axis=1)
    slots = (owner_seg * window_planes + plane_ids - own_start + 1).astype(jnp.int32)
    gathered = restored[slots]
    return jnp.transpose(gathered.reshape(extent_z, 6, extent_x, extent_y), (1, 2, 3, 0))


def to_devices(whole):
    shaped = whole.reshape(6, N_GX, CX, N_GY, CY, N_GZ, CZ)
    return jnp.transpose(shaped, (1, 3, 5, 0, 2, 4, 6)).reshape(N_GX * N_GY * N_GZ, 6, CX, CY, CZ)


def from_devices(device_parts):
    shaped = device_parts.reshape(N_GX, N_GY, N_GZ, 6, CX, CY, CZ)
    return jnp.transpose(shaped, (3, 0, 4, 1, 5, 2, 6)).reshape(6, VOXELS_ALONG_X, VOXELS_ALONG_Y, NZ)


def heat_rate(values, rates, joule_z):
    padded = jnp.pad(values, 1)
    beside_all = padded[2:, 1:-1, 1:-1] + padded[:-2, 1:-1, 1:-1]
    beside_all = beside_all + padded[1:-1, 2:, 1:-1] + padded[1:-1, :-2, 1:-1]
    beside_all = beside_all + padded[1:-1, 1:-1, 2:] + padded[1:-1, 1:-1, :-2]
    return rates * (beside_all - 6.0 * values) + joule_z


def reference(earlier_edge_voltage, coil_drive_current, sigma_omega_cellwise, subdomain_inverse_full, subdomain_inverse_main, subdomain_layer_counts, heat_layer_lookup, warming_amount, heat_spreading_coef):
    device_count = N_GX * N_GY * N_GZ
    solver_parts = subdomain_inverse_full.reshape(device_count, NSEG, BLK, BLK)
    diagonal_parts = subdomain_inverse_main.reshape(device_count, NSEG, BLK)
    length_parts = subdomain_layer_counts.reshape(device_count, NSEG)

    def one_device(device_items):
        return block_correction(device_items[0], device_items[1], device_items[2], device_items[3])

    vector_parts_count = earlier_edge_voltage
    for sweep_index in range(SWEEPS):
        padded = jnp.pad(vector_parts_count, ((0, 0), (1, 1), (1, 1), (1, 1)))
        residual = coil_drive_current - curl_curl(padded, sigma_omega_cellwise)
        corrections = lax.map(one_device, (to_devices(residual), solver_parts, diagonal_parts, length_parts))
        vector_parts_count = vector_parts_count + from_devices(corrections)
    joule_heat = 0.5 * sigma_omega_cellwise * jnp.sum(vector_parts_count * vector_parts_count, axis=0)

    slab_lengths = heat_layer_lookup
    slab_starts = (jnp.cumsum(slab_lengths, axis=1) - slab_lengths).astype(jnp.int32)
    offsets = jnp.arange(LAYER_CAP_HEAT, dtype=jnp.int32)
    range_ids = jnp.arange(N_GZ, dtype=jnp.int32)
    plane_index = (range_ids[:, None, None] * CZ + slab_starts[:, :, None] + offsets[None, None, :]).astype(jnp.int32)
    inside = offsets[None, None, :] < slab_lengths[:, :, None]
    local_planes = jnp.arange(CZ, dtype=jnp.int32)
    owner_slab = (jnp.sum((slab_starts[:, None, :] <= local_planes[None, :, None]).astype(jnp.int32), axis=2) - 1).astype(jnp.int32)
    owner_start = jnp.take_along_axis(slab_starts, owner_slab, axis=1)
    flat_index = ((range_ids[:, None] * NTH + owner_slab) * LAYER_CAP_HEAT + local_planes[None, :] - owner_start).reshape(NZ).astype(jnp.int32)

    def collect_onto_mesh(slabs):
        stacked = jnp.transpose(slabs, (2, 0, 1, 3, 4, 5)).reshape(N_GZ * NTH * LAYER_CAP_HEAT, VOXELS_ALONG_X, VOXELS_ALONG_Y)
        return stacked[flat_index]

    def distribute_onto_layers(whole):
        picked = whole[jnp.clip(plane_index, 0, NZ - 1)] * inside[:, :, :, None, None].astype(jnp.float32)
        return jnp.transpose(picked.reshape(N_GZ, N_GX, N_GY, LAYER_CAP_HEAT, VOXELS_ALONG_X, VOXELS_ALONG_Y), (1, 2, 0, 3, 4, 5))

    joule_z = jnp.transpose(joule_heat, (2, 0, 1))
    rates = collect_onto_mesh(heat_spreading_coef)
    section_coef = time_step / (SECTIONS * SECTIONS)
    earlier_estimate = collect_onto_mesh(warming_amount)
    current_estimate = earlier_estimate + section_coef * heat_rate(earlier_estimate, rates, joule_z)
    for section_index in range(2, SECTIONS + 1):
        following = 2.0 * current_estimate - earlier_estimate + 2.0 * section_coef * heat_rate(current_estimate, rates, joule_z)
        earlier_estimate = current_estimate
        current_estimate = following
    renewed_heat_rise = distribute_onto_layers(current_estimate)
    renewed_sigma_omega = sigma_omega_cellwise * jnp.exp(-heat_drop * jnp.transpose(current_estimate, (1, 2, 0)))
    return (vector_parts_count, renewed_heat_rise, renewed_sigma_omega)
```

```python
import functools

import jax
import jax.numpy as jnp
from jax import lax
from jax.experimental import pallas as pl
from jax.experimental.pallas import tpu as pltpu
from jax.sharding import PartitionSpec as P

SWEEPS = 2
SECTIONS = 4

mass_shift = 1.0
solver_scale = 0.2
coupling_scale = 0.05
time_step = 2.5
heat_drop = 0.15

CX, CY, CZ = 8, 16, 256
LANES = CX * CY
PLANE = 24
WINDOW = 21
MAXSEG = 19
COLS = LANES // 4
F32 = jnp.float32
HALO = 8
CHUNK = 32
XP_PLUS, XP_MINUS = 6, 7
RING = SECTIONS
VMEM = pl.BlockSpec(memory_space=pltpu.VMEM)
SMEM = pl.BlockSpec(memory_space=pltpu.SMEM)
ANY = pl.BlockSpec(memory_space=pl.ANY)


def params(mib=40):
    return pltpu.CompilerParams(vmem_limit_bytes=mib << 20)


def cost(flops, moved):
    return pl.CostEstimate(flops=flops, bytes_accessed=moved, transcendentals=0)


def lane_of(value):
    return lax.broadcasted_iota(jnp.int32, value.shape, value.ndim - 1)


def ahead(value, by):
    shift = (-by) % LANES
    return value if shift == 0 else pltpu.roll(value, shift, value.ndim - 1)


def x_slot(slot):
    return (slot // 4) * 64 + (slot % 4) * 8


def y_slot(slot):
    return (slot // 8) * 32 + slot % 8


def x_next(value, halo, slot):
    lane = lane_of(value)
    inner = jnp.where(lane < 64, ahead(value, 64), ahead(value, -56))
    return jnp.where((lane // 8) % 4 + 4 * (lane // 64) == 7, ahead(halo, x_slot(slot) - 88), inner)


def x_before(value, halo, slot):
    lane = lane_of(value)
    inner = jnp.where(lane < 64, ahead(value, 56), ahead(value, -64))
    return jnp.where((lane // 8) % 4 + 4 * (lane // 64) == 0, ahead(halo, x_slot(slot)), inner)


def y_next(value, halo, slot):
    lane = lane_of(value)
    low = (lane // 32) % 2 == 0
    inner = jnp.where(low, ahead(value, 32), ahead(value, -31))
    return jnp.where(lane % 8 + 8 * ((lane // 32) % 2) == 15, ahead(halo, y_slot(slot) - 39), inner)


def y_before(value, halo, slot):
    lane = lane_of(value)
    low = (lane // 32) % 2 == 0
    inner = jnp.where(low, ahead(value, 31), ahead(value, -32))
    return jnp.where(lane % 8 + 8 * ((lane // 32) % 2) == 0, ahead(halo, y_slot(slot)), inner)


def x_faces(parts):
    lane = lane_of(parts[0])
    own = (lane // 8) % 4 + 4 * (lane // 64)
    first = jnp.zeros_like(parts[0])
    last = first
    for slot, part in enumerate(parts):
        first = jnp.where(own == slot, ahead(part, -x_slot(slot)), first)
        last = jnp.where(own == slot, ahead(part, 88 - x_slot(slot)), last)
    return first, last


def y_faces(parts):
    lane = lane_of(parts[0])
    own = lane % 8 + 8 * ((lane // 32) % 2)
    first = jnp.zeros_like(parts[0])
    last = first
    for slot, part in enumerate(parts):
        first = jnp.where(own == slot, ahead(part, -y_slot(slot)), first)
        last = jnp.where(own == slot, ahead(part, 39 - y_slot(slot)), last)
    return first, last


def cell_rows(part):
    for dx in range(2):
        for dy in range(2):
            for a in range(CX // 2):
                yield (2 * dx + dy) * 32 + a * 8, 32 * a + 16 * dx + dy


def to_planes(source, index, target, out_index, turned):
    for to_row, from_row in cell_rows(None):
        for half in range(CZ // LANES):
            turned[half, to_row : to_row + 8, :] = source[index, half, pl.ds(from_row, 8, stride=2), :]
    for half in range(CZ // LANES):
        target[out_index, half * LANES : (half + 1) * LANES, :] = turned[half].T


def load_halves(source, loaded, index):
    for half in range(CZ // LANES):
        loaded[index, half] = source[index, :, half * LANES : (half + 1) * LANES]


def prepare_field(field, planes, first, last, loaded, turned):
    for comp in range(6):
        load_halves(field, loaded, comp)
        to_planes(loaded, comp, planes, comp, turned.at[comp % 2])

    def chunk(i, carry):
        rows = pl.ds(pl.multiple_of(i * CHUNK, CHUNK), CHUNK)
        low, high = x_faces([planes[comp, rows, :] for comp in range(6)])
        first[rows, :] = low
        last[rows, :] = high
        return carry

    lax.fori_loop(0, CZ // CHUNK, chunk, 0)


def prepare_drive(drive, conduct, diagonal, drive_planes, conduct_planes, diagonal_turned, loaded, turned):
    for comp in range(6):
        load_halves(drive, loaded, comp)
        to_planes(loaded, comp, drive_planes, comp, turned.at[comp % 2])
    load_halves(conduct, loaded, 0)
    to_planes(loaded, 0, conduct_planes, 0, turned.at[0])
    diagonal_turned[...] = diagonal[...].T


def kept(flag, value):
    return jnp.where(flag > 0, value, jnp.zeros_like(value))


def pack_y(flags, field, x_plus, x_minus, first, last):
    def chunk(i, carry):
        rows = pl.ds(pl.multiple_of(i * CHUNK, CHUNK), CHUNK)
        parts = [field[comp, rows, :] for comp in range(6)]
        parts += [kept(flags[1], x_plus[rows, :]), kept(flags[0], x_minus[rows, :])]
        low, high = y_faces(parts)
        first[rows, :] = low
        last[rows, :] = high
        return carry

    lax.fori_loop(0, CZ // CHUNK, chunk, 0)


def pack_z(flags, *refs):
    lows, highs, (first, last) = refs[:5], refs[5:10], refs[10:]
    for (field, xp, xm, yp, ym), row, out in ((lows, 0, first), (highs, 7, last)):
        for comp in range(6):
            out[comp : comp + 1, :] = field[comp, row : row + 1, :]
        out[6:7, :] = kept(flags[1], xp[row : row + 1, :])
        out[7:8, :] = kept(flags[0], xm[row : row + 1, :])
        out[8:9, :] = kept(flags[3], yp[row : row + 1, :])
        out[9:10, :] = kept(flags[2], ym[row : row + 1, :])
        out[10:16, :] = jnp.zeros((6, LANES), F32)


def curl_chunk(wide, part):
    ex, ey, ez = wide[3 * part], wide[3 * part + 1], wide[3 * part + 2]
    xp, xm, yp, ym = wide[6], wide[7], wide[8], wide[9]
    sx, sy, sz = 3 * part, 3 * part + 1, 3 * part + 2

    def here(v):
        return v[8 : 8 + CHUNK]

    def up(v):
        return v[9 : 9 + CHUNK]

    def down(v):
        return v[7 : 7 + CHUNK]

    upper = [v[8:] for v in (ex, ey, xm, ym)]
    ex_xm = x_before(upper[0], upper[2], sx)
    ey_ym = y_before(upper[1], upper[3], sy)
    ex_xm_up, ex_xm = ex_xm[1 : 1 + CHUNK], ex_xm[:CHUNK]
    ey_ym_up, ey_ym = ey_ym[1 : 1 + CHUNK], ey_ym[:CHUNK]
    lower = [v[: 8 + CHUNK] for v in (ez, xp, yp)]
    ez_xp = x_next(lower[0], lower[1], sz)
    ez_yp = y_next(lower[0], lower[2], sz)
    ez_xp_down, ez_xp = down(ez_xp), ez_xp[8:]
    ez_yp_down, ez_yp = down(ez_yp), ez_yp[8:]
    xp0, xm0, yp0, ym0 = here(xp), here(xm), here(yp), here(ym)
    ex0, ey0, ez0 = here(ex), here(ey), here(ez)
    ex_yp = y_next(ex0, yp0, sx)
    ex_ym = y_before(ex0, ym0, sx)
    ex_xm_yp = x_before(ex_yp, y_next(xm0, yp0, XP_MINUS), sx)
    ey_xp = x_next(ey0, xp0, sy)
    ey_xm = x_before(ey0, xm0, sy)
    ey_xp_ym = x_next(ey_ym, y_before(xp0, ym0, XP_PLUS), sy)
    ez_xm = x_before(ez0, xm0, sz)
    ez_ym = y_before(ez0, ym0, sz)
    kx = 4.0 * ex0 - ex_yp - ex_ym - up(ex) - down(ex)
    kx = kx + (ey_xp - ey0 - ey_xp_ym + ey_ym) + (ez_xp - ez0 - ez_xp_down + down(ez))
    ky = 4.0 * ey0 - ey_xp - ey_xm - up(ey) - down(ey)
    ky = ky + (ex_yp - ex0 - ex_xm_yp + ex_xm) + (ez_yp - ez0 - ez_yp_down + down(ez))
    kz = 4.0 * ez0 - ez_xp - ez_xm - ez_yp - ez_ym
    kz = kz + (up(ex) - ex0 - ex_xm_up + ex_xm) + (up(ey) - ey0 - ey_ym_up + ey_ym)
    return (kx, ky, kz), (ex0, ey0, ez0)


def sweep(last_sweep, flags, seg_len, field, drive, conduct, xp, xm, yp, ym, zp, zm, diagonal, solver, *rest):
    if last_sweep:
        permute, field_out, heat_out, ext, columns, solved, matrices, sems, turned = rest
    else:
        field_out, first, last, ext, columns, solved, matrices, sems = rest
    segs = matrices.shape[0]
    copies = [pltpu.make_async_copy(solver.at[s], matrices.at[s], sems.at[s]) for s in range(segs)]
    for copy in copies:
        copy.start()

    def fill(i, carry):
        rows = pl.ds(pl.multiple_of(i * CHUNK, CHUNK), CHUNK)
        to = pl.ds(pl.multiple_of(i * CHUNK + HALO, 8), CHUNK)
        for comp in range(6):
            ext[comp, to, :] = field[comp, rows, :]
        ext[6, to, :] = kept(flags[1], xp[rows, :])
        ext[7, to, :] = kept(flags[0], xm[rows, :])
        ext[8, to, :] = kept(flags[3], yp[rows, :])
        ext[9, to, :] = kept(flags[2], ym[rows, :])
        return carry

    lax.fori_loop(0, CZ // CHUNK, fill, 0)
    for comp in range(10):
        ext[comp, HALO - 1 : HALO, :] = kept(flags[4], zm[comp : comp + 1, :])
        ext[comp, HALO + CZ : HALO + CZ + 1, :] = kept(flags[5], zp[comp : comp + 1, :])

    columns[0:PLANE, :] = jnp.zeros((PLANE, LANES), F32)
    tail = columns.shape[0] - (CZ + 1) * PLANE
    columns[(CZ + 1) * PLANE :, :] = jnp.zeros((tail, LANES), F32)

    def residual(i, carry):
        base = pl.multiple_of(i * CHUNK, CHUNK)
        rows = pl.ds(base, CHUNK)
        wide = [ext[comp, pl.ds(base, CHUNK + 2 * HALO), :] for comp in range(10)]
        curl_real, real = curl_chunk(wide, 0)
        curl_imag, imag = curl_chunk(wide, 1)
        sigma = conduct[0, rows, :]
        for axis in range(3):
            both = (
                curl_real[axis] + mass_shift * real[axis] - sigma * imag[axis],
                curl_imag[axis] + mass_shift * imag[axis] + sigma * real[axis],
            )
            for part in range(2):
                comp = 3 * part + axis
                rest_of = drive[comp, rows, :] - both[part]
                for q in range(4):
                    at = (base + 1) * PLANE + comp * 4 + q
                    columns[pl.ds(at, CHUNK, stride=PLANE), :] = ahead(rest_of, 32 * q)
        return carry

    lax.fori_loop(0, CZ // CHUNK, residual, 0)

    row_of = lax.broadcasted_iota(jnp.int32, (512, LANES), 0)
    start = jnp.int32(0)
    for s in range(segs):
        length = seg_len[s]
        window = columns[pl.ds(pl.multiple_of(start * PLANE, 8), 512), :]
        window = jnp.where(row_of < (length + 2) * PLANE, window, 0.0).astype(jnp.bfloat16)
        copies[s].wait()
        product = jnp.dot(matrices[s], window, preferred_element_type=F32)
        scaled = solver_scale * diagonal[:, s : s + 1] * window.astype(F32)
        result = coupling_scale * product + scaled
        to = pl.ds(pl.multiple_of(start * PLANE, 8), MAXSEG * PLANE)
        solved[to, :] = result[PLANE : (MAXSEG + 1) * PLANE, :]
        start = start + length

    def update(i, carry):
        base = pl.multiple_of(i * CHUNK, CHUNK)
        rows = pl.ds(base, CHUNK)
        lane = lax.broadcasted_iota(jnp.int32, (CHUNK, LANES), 1)
        parts = []
        for comp in range(6):
            add = jnp.zeros((CHUNK, LANES), F32)
            for q in range(4):
                piece = solved[pl.ds(base * PLANE + comp * 4 + q, CHUNK, stride=PLANE), :]
                add = jnp.where(lane // COLS == q, ahead(piece, -32 * q), add)
            parts.append(field[comp, rows, :] + add)
        if last_sweep:
            total = parts[0] * parts[0]
            for part in parts[1:]:
                total = total + part * part
            heat = 0.5 * conduct[0, rows, :] * total
            heat_out[rows, :] = jnp.dot(
                heat, permute[...], precision=lax.Precision.HIGHEST, preferred_element_type=F32
            )
            for comp in range(6):
                ext[comp, rows, :] = parts[comp]
        else:
            for comp in range(6):
                field_out[comp, rows, :] = parts[comp]
            low, high = x_faces(parts)
            first[rows, :] = low
            last[rows, :] = high
        return carry

    lax.fori_loop(0, CZ // CHUNK, update, 0)
    if last_sweep:
        for comp in range(6):
            for half in range(CZ // LANES):
                flat = ext[comp, half * LANES : (half + 1) * LANES, :].T
                for from_row, to_row in cell_rows(None):
                    turned[comp % 2, half, pl.ds(to_row, 8, stride=2), :] = flat[from_row : from_row + 8]
                field_out[comp, :, half * LANES : (half + 1) * LANES] = turned[comp % 2, half]


def pack_heat(flags, starts, heat, below, above, out, ext):
    ext[0:8, :] = kept(flags[4], below[...])
    ext[8 : 8 + CZ, :] = heat[...]
    ext[8 + CZ : 16 + CZ, :] = kept(flags[5], above[...])
    ext[16 + CZ :, :] = jnp.zeros((ext.shape[0] - 16 - CZ, LANES), F32)
    for owner in range(out.shape[0]):
        out[owner] = ext[pl.ds(starts[owner] + 8 - (RING - 1), out.shape[1]), :]


def swap_tiles(value):
    row = lax.broadcasted_iota(jnp.int32, value.shape, value.ndim - 2)
    lane = lane_of(value)
    axis = value.ndim - 2
    for k in range(3):
        step = 1 << k
        row_bit = (row // step) % 2
        lane_bit = (lane // (16 * step)) % 2
        up = ahead(pltpu.roll(value, 8 - step, axis), -16 * step)
        down = up if step == 4 else ahead(pltpu.roll(value, step, axis), 16 * step)
        value = jnp.where(row_bit == lane_bit, value, jnp.where(row_bit == 0, up, down))
    return value


def prepare_slab(warm, rates, out):
    for plane in range(out.shape[0]):
        for which, source in enumerate((warm, rates)):
            out[plane, which] = swap_tiles(source[plane].reshape(4, 8, LANES))


def choose_planes(length, round_id, slab, *refs):
    received = refs[: 2 * (round_id - 1)]
    up_out, down_out = refs[2 * (round_id - 1) :]
    below, above = received[0::2], received[1::2]
    count = length[0]
    up_out[...] = slab[jnp.maximum(count - round_id, 0)]
    down_out[...] = slab[round_id - 1]
    for short in range(1, round_id):

        @pl.when(count == short)
        def _():
            up_out[...] = below[round_id - short - 1][...]
            down_out[...] = above[round_id - short - 1][...]


def heat_step(slab_info, slab, b1, a1, b2, a2, b3, a3, b4, a4, arrived, factor_out, warm_out, temp, rates, joule):
    count, low_open, high_open = slab_info[0], slab_info[1], slab_info[2]
    planes = temp.shape[1]
    owners = arrived.shape[0]
    for plane in range(planes - 2 * RING):
        temp[0, plane + RING] = slab[plane, 0]
        rates[plane + RING] = slab[plane, 1]
    for r, (below, above) in enumerate(((b1, a1), (b2, a2), (b3, a3), (b4, a4))):
        temp[0, RING - 1 - r] = below[0]
        rates[RING - 1 - r] = below[1]
        temp[0, RING + count + r] = above[0]
        rates[RING + count + r] = above[1]
    for owner in range(owners):
        joule[pl.ds(owners + owner, arrived.shape[1], stride=owners), :] = arrived[owner]

    group = 6
    section = time_step / (SECTIONS * SECTIONS)

    def one(step, now, before, base):
        value = temp[now, pl.ds(base - 1, group + 2)]
        mid = value[1:-1]
        lane = lane_of(mid)
        row = lax.broadcasted_iota(jnp.int32, mid.shape, 2)
        none = jnp.zeros_like(mid[:, :1])
        gx_up = jnp.concatenate([mid[:, 1:], none], axis=1)
        gx_down = jnp.concatenate([none, mid[:, :-1]], axis=1)
        gy_up = jnp.where(row == 7, 0.0, pltpu.roll(mid, 7, 2))
        gy_down = jnp.where(row == 0, 0.0, pltpu.roll(mid, 1, 2))
        total = ahead(jnp.where(lane < 16, gx_up, mid), 16)
        total = total + ahead(jnp.where(lane >= 112, gx_down, mid), -16)
        total = total + jnp.where(lane % 16 == 15, ahead(gy_up, -15), ahead(mid, 1))
        total = total + jnp.where(lane % 16 == 0, ahead(gy_down, 15), ahead(mid, -1))
        total = total + value[:-2] + value[2:]
        heat = joule[pl.ds(base * owners, group * owners), :].reshape(group, 4, 8, LANES)
        rate = rates[pl.ds(base, group)] * (total - 6.0 * mid) + heat
        if step == 1:
            temp[before, pl.ds(base, group)] = mid + section * rate
        else:
            old = temp[before, pl.ds(base, group)]
            temp[before, pl.ds(base, group)] = 2.0 * mid - old + 2.0 * section * rate

    for step in range(1, SECTIONS + 1):
        now, before = (step - 1) % 2, step % 2

        def loop(g, carry):
            one(step, now, before, 1 + g * group)
            return carry

        lax.fori_loop(0, (planes - 2) // group, loop, 0)
    final = SECTIONS % 2
    for plane in range(warm_out.shape[0]):
        result = temp[final, plane + RING]
        warm_out[plane] = result
        joule[plane * owners : (plane + 1) * owners, :] = jnp.exp(-heat_drop * result).reshape(owners, LANES)
    for owner in range(owners):
        factor_out[owner] = joule[pl.ds(owner, factor_out.shape[1], stride=owners), :]


def finish_slab(slab_info, warm, out):
    count = slab_info[0]
    for plane in range(out.shape[0]):
        out[plane] = kept(count - plane, swap_tiles(warm[plane])).reshape(32, LANES)


def finish_conduct(starts, returned, conduct, out, rows):
    for owner in range(returned.shape[0]):
        rows[pl.ds(starts[owner], returned.shape[1]), :] = returned[owner]
    for half in range(CZ // LANES):
        lanes = slice(half * LANES, (half + 1) * LANES)
        out[:, lanes] = conduct[:, lanes] * rows[half * LANES : (half + 1) * LANES, :].T


def shape(*dims):
    return jax.ShapeDtypeStruct(dims, F32)


def body(
    earlier_edge_voltage,
    coil_drive_current,
    sigma_omega_cellwise,
    subdomain_inverse_full,
    subdomain_inverse_main,
    subdomain_layer_counts,
    heat_layer_lookup,
    warming_amount,
    heat_spreading_coef,
):
    count_x, count_y, count_z = (lax.axis_size(axis) for axis in ("gx", "gy", "gz"))
    at_x, at_y, at_z = (lax.axis_index(axis) for axis in ("gx", "gy", "gz"))
    owners = count_x * count_y
    segs = subdomain_layer_counts.shape[3]
    slab_cap = warming_amount.shape[3]

    def turn(value, axis, step):
        count = lax.axis_size(axis)
        return lax.ppermute(value, axis, [(i, (i + step) % count) for i in range(count)])

    def device(slab):
        return (slab % owners) * count_z + slab // owners

    def ring(value, step):
        total = owners * count_z
        pairs = [(device(i), device((i + step) % total)) for i in range(total)]
        return lax.ppermute(value, ("gx", "gy", "gz"), pairs)

    flags = jnp.stack(
        [at_x > 0, at_x < count_x - 1, at_y > 0, at_y < count_y - 1, at_z > 0, at_z < count_z - 1]
    ).astype(jnp.int32)
    seg_len = subdomain_layer_counts[0, 0, 0]
    slab_lengths = heat_layer_lookup[0]
    slab_ids = jnp.arange(owners, dtype=jnp.int32)
    starts = jnp.sum(
        jnp.where(slab_ids[None, :] < slab_ids[:, None], slab_lengths[None, :], 0), axis=1
    ).astype(jnp.int32)
    my_owner = at_x * count_y + at_y
    my_length = jnp.sum(jnp.where(slab_ids == my_owner, slab_lengths, 0)).astype(jnp.int32)
    low_open = (my_owner > 0) | (at_z > 0)
    high_open = (my_owner < owners - 1) | (at_z < count_z - 1)
    slab_info = jnp.stack([my_length, low_open.astype(jnp.int32), high_open.astype(jnp.int32)])

    field_bytes = 6 * CZ * LANES * 4
    plane_array = shape(CZ, LANES)
    halves = pltpu.VMEM((6, 2, LANES, LANES), F32)
    turned = pltpu.VMEM((2, 2, LANES, LANES), F32)
    field, face_low, face_high = pl.pallas_call(
        prepare_field,
        out_shape=(shape(6, CZ, LANES), plane_array, plane_array),
        in_specs=[VMEM],
        out_specs=[VMEM] * 3,
        scratch_shapes=[halves, turned],
        compiler_params=params(),
        cost_estimate=cost(1 << 20, 2 * field_bytes),
        name="prepare_field",
    )(earlier_edge_voltage.reshape(6, LANES, CZ))
    drive, conduct, diagonal = pl.pallas_call(
        prepare_drive,
        out_shape=(shape(6, CZ, LANES), shape(1, CZ, LANES), shape(512, segs)),
        in_specs=[VMEM] * 3,
        out_specs=[VMEM] * 3,
        scratch_shapes=[halves, turned],
        compiler_params=params(),
        cost_estimate=cost(1 << 20, 2 * field_bytes),
        name="prepare_drive",
    )(
        coil_drive_current.reshape(6, LANES, CZ),
        sigma_omega_cellwise.reshape(1, LANES, CZ),
        subdomain_inverse_main[0, 0, 0],
    )
    slab = pl.pallas_call(
        prepare_slab,
        out_shape=shape(slab_cap, 2, 4, 8, LANES),
        in_specs=[VMEM] * 2,
        out_specs=VMEM,
        compiler_params=params(),
        cost_estimate=cost(1 << 20, 2 * field_bytes),
        name="prepare_slab",
    )(warming_amount[0, 0, 0], heat_spreading_coef[0, 0, 0])

    def halo(field, face_low, face_high):
        x_plus, x_minus = turn(face_low, "gx", -1), turn(face_high, "gx", 1)
        y_low, y_high = pl.pallas_call(
            pack_y,
            out_shape=(plane_array, plane_array),
            in_specs=[SMEM] + [VMEM] * 3,
            out_specs=[VMEM] * 2,
            compiler_params=params(),
            cost_estimate=cost(1 << 20, 2 * field_bytes),
            name="pack_y",
        )(flags, field, x_plus, x_minus)
        y_plus, y_minus = turn(y_low, "gy", -1), turn(y_high, "gy", 1)
        sides = (x_plus, x_minus, y_plus, y_minus)
        end = CZ // 8 - 1
        specs = []
        for block in (0, end):
            specs.append(pl.BlockSpec((6, 8, LANES), lambda i, block=block: (0, block, 0)))
            specs += [pl.BlockSpec((8, LANES), lambda i, block=block: (block, 0))] * 4
        z_low, z_high = pl.pallas_call(
            pack_z,
            grid=(1,),
            out_shape=(shape(16, LANES), shape(16, LANES)),
            in_specs=[SMEM] + specs,
            out_specs=[pl.BlockSpec((16, LANES), lambda i: (0, 0))] * 2,
            compiler_params=params(),
            name="pack_z",
        )(flags, field, *sides, field, *sides)
        z_plus, z_minus = turn(z_low, "gz", -1), turn(z_high, "gz", 1)
        return sides + (z_plus, z_minus)

    received = []
    for round_id in range(1, RING + 1):
        up, down = pl.pallas_call(
            lambda length, *refs, round_id=round_id: choose_planes(length, round_id, *refs),
            out_shape=(shape(2, 4, 8, LANES),) * 2,
            in_specs=[SMEM] + [VMEM] * (1 + len(received)),
            out_specs=[VMEM] * 2,
            compiler_params=params(),
            name="choose_planes",
        )(slab_info, slab, *received)
        below, above = ring(up, 1), ring(down, -1)
        received += [jnp.where(low_open, below, 0.0), jnp.where(high_open, above, 0.0)]

    solver = subdomain_inverse_full[0, 0, 0]
    for sweep_index in range(SWEEPS):
        final = sweep_index == SWEEPS - 1
        ghosts = halo(field, face_low, face_high)
        scratch = [
            pltpu.VMEM((10, CZ + 2 * HALO, LANES), F32),
            pltpu.VMEM(((CZ + 1 + WINDOW) * PLANE + 8, LANES), F32),
            pltpu.VMEM(((CZ + MAXSEG) * PLANE, LANES), F32),
            pltpu.VMEM((segs, 512, 512), jnp.bfloat16),
            pltpu.SemaphoreType.DMA((segs,)),
        ]
        inputs = [flags, seg_len, field, drive, conduct, *ghosts, diagonal, solver]
        specs = [SMEM] * 2 + [VMEM] * 10 + [ANY]
        if final:
            lane = jnp.arange(LANES, dtype=jnp.int32)
            natural = (
                (2 * ((lane // 8) % 4) + lane // 64) * 16 + 2 * (lane % 8) + (lane // 32) % 2
            )
            inputs.append((natural[:, None] == lane[None, :]).astype(F32))
            specs.append(VMEM)
            scratch.append(turned)
            outs = (shape(6, LANES, CZ), plane_array)
        else:
            outs = (shape(6, CZ, LANES), plane_array, plane_array)
        result = pl.pallas_call(
            functools.partial(sweep, final),
            out_shape=outs,
            in_specs=specs,
            out_specs=[VMEM] * len(outs),
            scratch_shapes=scratch,
            compiler_params=params(),
            cost_estimate=cost(1 << 28, 4 * field_bytes),
            name="sweep",
        )(*inputs)
        if final:
            field_new, heat = result
        else:
            field, face_low, face_high = result

    heat_above, heat_below = turn(heat[:8], "gz", -1), turn(heat[CZ - 8 :], "gz", 1)
    rows = slab_cap + 8
    outgoing = pl.pallas_call(
        pack_heat,
        out_shape=shape(owners, rows, LANES),
        in_specs=[SMEM] * 2 + [VMEM] * 3,
        out_specs=VMEM,
        scratch_shapes=[pltpu.VMEM((CZ + 16 + rows, LANES), F32)],
        compiler_params=params(),
        name="pack_heat",
    )(flags, starts, heat, heat_below, heat_above)
    arrived = lax.all_to_all(outgoing, ("gx", "gy"), split_axis=0, concat_axis=0, tiled=True)
    planes = slab_cap + 2 * RING
    factor, warm = pl.pallas_call(
        heat_step,
        out_shape=(shape(owners, slab_cap, LANES), shape(slab_cap, 4, 8, LANES)),
        in_specs=[SMEM] + [VMEM] * 10,
        out_specs=[VMEM] * 2,
        scratch_shapes=[
            pltpu.VMEM((2, planes, 4, 8, LANES), F32),
            pltpu.VMEM((planes, 4, 8, LANES), F32),
            pltpu.VMEM(((1 + rows) * owners, LANES), F32),
        ],
        compiler_params=params(),
        name="heat_step",
    )(slab_info, slab, *received, arrived)
    returned = lax.all_to_all(factor, ("gx", "gy"), split_axis=0, concat_axis=0, tiled=True)
    renewed_heat_rise = pl.pallas_call(
        finish_slab,
        out_shape=shape(slab_cap, 32, LANES),
        in_specs=[SMEM, VMEM],
        out_specs=VMEM,
        compiler_params=params(),
        name="finish_slab",
    )(slab_info, warm)
    renewed_sigma_omega = pl.pallas_call(
        finish_conduct,
        out_shape=shape(LANES, CZ),
        in_specs=[SMEM] + [VMEM] * 2,
        out_specs=VMEM,
        scratch_shapes=[pltpu.VMEM((CZ + slab_cap, LANES), F32)],
        compiler_params=params(),
        name="finish_conduct",
    )(starts, returned, sigma_omega_cellwise.reshape(LANES, CZ))
    return (
        field_new.reshape(6, CX, CY, CZ),
        renewed_heat_rise[None, None, None],
        renewed_sigma_omega.reshape(CX, CY, CZ),
    )


def solution(mesh):
    return jax.shard_map(
        body,
        mesh=mesh,
        in_specs=(
            P(None, "gx", "gy", "gz"),
            P(None, "gx", "gy", "gz"),
            P("gx", "gy", "gz"),
            P("gx", "gy", "gz", None, None, None),
            P("gx", "gy", "gz", None, None),
            P("gx", "gy", "gz", None),
            P("gz", None),
            P("gx", "gy", "gz", None, None, None),
            P("gx", "gy", "gz", None, None, None),
        ),
        out_specs=(
            P(None, "gx", "gy", "gz"),
            P("gx", "gy", "gz", None, None, None),
            P("gx", "gy", "gz"),
        ),
        check_vma=False,
    )
```

```python
import functools

import jax
import jax.numpy as jnp
from jax import lax
from jax.experimental import pallas as pl
from jax.experimental.pallas import tpu as pltpu
from jax.sharding import PartitionSpec as P

SWEEPS = 2
SECTIONS = 4

mass_shift = 1.0
solver_scale = 0.2
coupling_scale = 0.05
time_step = 2.5
heat_drop = 0.15

CX, CY, CZ = 8, 16, 256
LANES = CX * CY
PLANE = 24
WINDOW = 21
MAXSEG = 19
F32 = jnp.float32
HALO = 8
CHUNK = 32
XP_PLUS, XP_MINUS = 6, 7
X_BITS, Y_BITS = 112, 15
RING = SECTIONS
HALF = CZ // 2
CORNER = (0, 1, 16, 17)
VMEM = pl.BlockSpec(memory_space=pltpu.VMEM)
SMEM = pl.BlockSpec(memory_space=pltpu.SMEM)


def params(mib=24):
    return pltpu.CompilerParams(vmem_limit_bytes=mib << 20)


def cost(flops, moved):
    return pl.CostEstimate(flops=flops, bytes_accessed=moved, transcendentals=0)


def lane_of(value):
    return lax.broadcasted_iota(jnp.int32, value.shape, value.ndim - 1)


def ahead(value, by):
    shift = (-by) % LANES
    return value if shift == 0 else pltpu.roll(value, shift, value.ndim - 1)


def x_slot(slot):
    return 16 * slot


def y_slot(slot):
    return slot


def x_next(value, halo, slot):
    lane = lane_of(value)
    return jnp.where(lane & X_BITS == X_BITS, ahead(halo, x_slot(slot) - X_BITS), ahead(value, 16))


def x_before(value, halo, slot):
    lane = lane_of(value)
    return jnp.where(lane & X_BITS == 0, ahead(halo, x_slot(slot)), ahead(value, -16))


def y_next(value, halo, slot):
    lane = lane_of(value)
    return jnp.where(lane & Y_BITS == Y_BITS, ahead(halo, y_slot(slot) - Y_BITS), ahead(value, 1))


def y_before(value, halo, slot):
    lane = lane_of(value)
    return jnp.where(lane & Y_BITS == 0, ahead(halo, y_slot(slot)), ahead(value, -1))


def x_faces(parts):
    lane = lane_of(parts[0])
    own = lane & X_BITS
    first = jnp.zeros_like(parts[0])
    last = first
    for slot, part in enumerate(parts):
        mine = own == x_slot(slot)
        first = jnp.where(mine, ahead(part, -x_slot(slot)), first)
        last = jnp.where(mine, ahead(part, X_BITS - x_slot(slot)), last)
    return first, last


def y_faces(parts):
    lane = lane_of(parts[0])
    own = lane & Y_BITS
    first = jnp.zeros_like(parts[0])
    last = first
    for slot, part in enumerate(parts):
        mine = own == y_slot(slot)
        first = jnp.where(mine, ahead(part, -y_slot(slot)), first)
        last = jnp.where(mine, ahead(part, Y_BITS - y_slot(slot)), last)
    return first, last


def to_planes(source, index, target):
    for half in range(CZ // LANES):
        lanes = slice(half * LANES, (half + 1) * LANES)
        target[index, lanes, :] = source[index, :, lanes].T


def prepare_field(field, planes, first, last):
    for comp in range(6):
        to_planes(field, comp, planes)

    def chunk(i, carry):
        rows = pl.ds(pl.multiple_of(i * CHUNK, CHUNK), CHUNK)
        low, high = x_faces([planes[comp, rows, :] for comp in range(6)])
        first[rows, :] = low
        last[rows, :] = high
        return carry

    lax.fori_loop(0, CZ // CHUNK, chunk, 0)


def prepare_drive(drive, conduct, diagonal, drive_planes, conduct_planes, diagonal_turned):
    for comp in range(6):
        to_planes(drive, comp, drive_planes)
    to_planes(conduct, 0, conduct_planes)
    diagonal_turned[...] = diagonal[...].T


def kept(flag, value):
    return jnp.where(flag > 0, value, jnp.zeros_like(value))


def tiled(plane):
    return swap_tiles(plane.reshape(4, 8, LANES)).reshape(32, LANES)


def pack_y(round_id, flags, info, field, x_plus, x_minus, *rest):
    up, down = rest[-2:]

    def chunk(i, carry):
        parts = []
        for base in (0, HALF):
            rows = pl.ds(pl.multiple_of(base + i * CHUNK, CHUNK), CHUNK)
            parts += [field[comp, rows, :] for comp in range(6)]
            parts += [kept(flags[1], x_plus[rows, :]), kept(flags[0], x_minus[rows, :])]
        low, high = y_faces(parts)
        rows = pl.ds(pl.multiple_of(i * CHUNK, CHUNK), CHUNK)
        down[rows, :] = low
        up[rows, :] = high
        return carry

    lax.fori_loop(0, HALF // CHUNK, chunk, 0)
    if round_id == 1:
        for depth in range(RING):
            top = jnp.maximum(info[0] - 1 - depth, 0)
            for which in range(2):
                at = HALF + 64 * depth + 32 * which
                up[at : at + 32, :] = tiled(rest[which][top])
                down[at : at + 32, :] = tiled(rest[which][depth])
        count = jnp.full((8, LANES), info[0], jnp.int32).astype(F32)
        up[-8:, :] = count
        down[-8:, :] = count
    else:
        below, above = rest[:2]
        size = 64 * (RING - 1)
        up[HALF : HALF + size, :] = kept(info[1], below[HALF : HALF + size, :])
        down[HALF : HALF + size, :] = kept(info[2], above[HALF : HALF + size, :])
        up[-8:, :] = below[-8:, :]
        down[-8:, :] = above[-8:, :]


def planes_of(message, start, count, flag):
    return [
        kept(flag, message[start + 64 * d : start + 64 * (d + 1), :]).reshape(8, 8, LANES)
        for d in range(count)
    ]


def choose_far(info, below1, above1, below2, above2, up, down):
    for one, two, out, flag in ((below1, below2, up, info[1]), (above1, above2, down, info[2])):
        first = planes_of(one, HALF, 2, flag)
        second = planes_of(two, HALF, 1, flag)
        out[0:64, :] = first[0].reshape(64, LANES)
        out[64:128, :] = jnp.where(one[-8:, :] > 1.5, first[1], second[0]).reshape(64, LANES)


def beyond(one, two, three, near, far):
    a, b, c = planes_of(one, HALF, 4, near), planes_of(two, HALF, 3, near), planes_of(three, 0, 2, far)
    first, second = one[-8:, :], two[-8:, :]
    two_left = jnp.where(second > 1.5, b[1], c[0])
    three_left = jnp.where(second > 2.5, b[2], jnp.where(second > 1.5, c[0], c[1]))
    return (
        a[0],
        jnp.where(first > 1.5, a[1], b[0]),
        jnp.where(first > 2.5, a[2], jnp.where(first > 1.5, b[0], two_left)),
        jnp.where(
            first > 3.5,
            a[3],
            jnp.where(first > 2.5, b[0], jnp.where(first > 1.5, two_left, three_left)),
        ),
    )


def y_rows(message, row, count, upper):
    value = message[row : row + count, :]
    return ahead(value, 8) if upper else value


def pack_z(flags, *refs):
    lows, highs, (first, last) = refs[:5], refs[5:10], refs[10:]
    for (field, xp, xm, yp, ym), row, out in ((lows, 0, first), (highs, 7, last)):
        for comp in range(6):
            out[comp : comp + 1, :] = field[comp, row : row + 1, :]
        out[6:7, :] = kept(flags[1], xp[row : row + 1, :])
        out[7:8, :] = kept(flags[0], xm[row : row + 1, :])
        out[8:9, :] = kept(flags[3], y_rows(yp, row, 1, row > 0))
        out[9:10, :] = kept(flags[2], y_rows(ym, row, 1, row > 0))
        out[10:16, :] = jnp.zeros((6, LANES), F32)


def curl_chunk(wide, part):
    ex, ey, ez = wide[3 * part], wide[3 * part + 1], wide[3 * part + 2]
    xp, xm, yp, ym = wide[6], wide[7], wide[8], wide[9]
    sx, sy, sz = 3 * part, 3 * part + 1, 3 * part + 2

    def here(v):
        return v[8 : 8 + CHUNK]

    def up(v):
        return v[9 : 9 + CHUNK]

    def down(v):
        return v[7 : 7 + CHUNK]

    upper = [v[8:] for v in (ex, ey, xm, ym)]
    ex_xm = x_before(upper[0], upper[2], sx)
    ey_ym = y_before(upper[1], upper[3], sy)
    ex_xm_up, ex_xm = ex_xm[1 : 1 + CHUNK], ex_xm[:CHUNK]
    ey_ym_up, ey_ym = ey_ym[1 : 1 + CHUNK], ey_ym[:CHUNK]
    lower = [v[: 8 + CHUNK] for v in (ez, xp, yp)]
    ez_xp = x_next(lower[0], lower[1], sz)
    ez_yp = y_next(lower[0], lower[2], sz)
    ez_xp_down, ez_xp = down(ez_xp), ez_xp[8:]
    ez_yp_down, ez_yp = down(ez_yp), ez_yp[8:]
    xp0, xm0, yp0, ym0 = here(xp), here(xm), here(yp), here(ym)
    ex0, ey0, ez0 = here(ex), here(ey), here(ez)
    ex_yp = y_next(ex0, yp0, sx)
    ex_ym = y_before(ex0, ym0, sx)
    ex_xm_yp = x_before(ex_yp, y_next(xm0, yp0, XP_MINUS), sx)
    ey_xp = x_next(ey0, xp0, sy)
    ey_xm = x_before(ey0, xm0, sy)
    ey_xp_ym = x_next(ey_ym, y_before(xp0, ym0, XP_PLUS), sy)
    ez_xm = x_before(ez0, xm0, sz)
    ez_ym = y_before(ez0, ym0, sz)
    kx = 4.0 * ex0 - ex_yp - ex_ym - up(ex) - down(ex)
    kx = kx + (ey_xp - ey0 - ey_xp_ym + ey_ym) + (ez_xp - ez0 - ez_xp_down + down(ez))
    ky = 4.0 * ey0 - ey_xp - ey_xm - up(ey) - down(ey)
    ky = ky + (ex_yp - ex0 - ex_xm_yp + ex_xm) + (ez_yp - ez0 - ez_yp_down + down(ez))
    kz = 4.0 * ez0 - ez_xp - ez_xm - ez_yp - ez_ym
    kz = kz + (up(ex) - ex0 - ex_xm_up + ex_xm) + (up(ey) - ey0 - ey_ym_up + ey_ym)
    return (kx, ky, kz), (ex0, ey0, ez0)


def sweep(last_sweep, flags, seg_len, field, drive, conduct, xp, xm, yp, ym, zp, zm, diagonal, solver, *rest):
    if last_sweep:
        field_out, heat_out, ext, columns, solved = rest
    else:
        field_out, first, last, ext, columns, solved = rest
    segs = solver.shape[0]

    for base in range(0, CZ, CHUNK):
        rows = slice(base, base + CHUNK)
        to = slice(base + HALO, base + HALO + CHUNK)
        for comp in range(6):
            ext[comp, to, :] = field[comp, rows, :]
        ext[6, to, :] = kept(flags[1], xp[rows, :])
        ext[7, to, :] = kept(flags[0], xm[rows, :])
        ext[8, to, :] = kept(flags[3], y_rows(yp, base % HALF, CHUNK, base >= HALF))
        ext[9, to, :] = kept(flags[2], y_rows(ym, base % HALF, CHUNK, base >= HALF))
    for comp in range(10):
        ext[comp, HALO - 1 : HALO, :] = kept(flags[4], zm[comp : comp + 1, :])
        ext[comp, HALO + CZ : HALO + CZ + 1, :] = kept(flags[5], zp[comp : comp + 1, :])

    columns[0:PLANE, :] = jnp.zeros((PLANE, LANES), F32)
    tail = columns.shape[0] - (CZ + 1) * PLANE
    columns[(CZ + 1) * PLANE :, :] = jnp.zeros((tail, LANES), F32)

    def residual(i, carry):
        base = pl.multiple_of(i * CHUNK, CHUNK)
        rows = pl.ds(base, CHUNK)
        wide = [ext[comp, pl.ds(base, CHUNK + 2 * HALO), :] for comp in range(10)]
        curl_real, real = curl_chunk(wide, 0)
        curl_imag, imag = curl_chunk(wide, 1)
        sigma = conduct[0, rows, :]
        for axis in range(3):
            both = (
                curl_real[axis] + mass_shift * real[axis] - sigma * imag[axis],
                curl_imag[axis] + mass_shift * imag[axis] + sigma * real[axis],
            )
            for part in range(2):
                comp = 3 * part + axis
                rest_of = drive[comp, rows, :] - both[part]
                for q in range(4):
                    at = (base + 1) * PLANE + comp * 4 + q
                    columns[pl.ds(at, CHUNK, stride=PLANE), :] = ahead(rest_of, CORNER[q])
        return carry

    lax.fori_loop(0, CZ // CHUNK, residual, 0)

    row_of = lax.broadcasted_iota(jnp.int32, (512, LANES), 0)
    start = jnp.int32(0)
    for s in range(segs):
        length = seg_len[s]
        window = columns[pl.ds(pl.multiple_of(start * PLANE, 8), 512), :]
        window = jnp.where(row_of < (length + 2) * PLANE, window, 0.0).astype(jnp.bfloat16)
        product = jnp.dot(solver[s], window, preferred_element_type=F32)
        scaled = solver_scale * diagonal[:, s : s + 1] * window.astype(F32)
        result = coupling_scale * product + scaled
        to = pl.ds(pl.multiple_of(start * PLANE, 8), MAXSEG * PLANE)
        solved[to, :] = result[PLANE : (MAXSEG + 1) * PLANE, :]
        start = start + length

    def update(i, carry):
        base = pl.multiple_of(i * CHUNK, CHUNK)
        rows = pl.ds(base, CHUNK)
        lane = lax.broadcasted_iota(jnp.int32, (CHUNK, LANES), 1)
        parts = []
        for comp in range(6):
            add = jnp.zeros((CHUNK, LANES), F32)
            for q in range(4):
                piece = solved[pl.ds(base * PLANE + comp * 4 + q, CHUNK, stride=PLANE), :]
                add = jnp.where(lane & 17 == CORNER[q], ahead(piece, -CORNER[q]), add)
            part = field[comp, rows, :] + add
            field_out[comp, rows, :] = part
            parts.append(part)
        if last_sweep:
            total = parts[0] * parts[0]
            for part in parts[1:]:
                total = total + part * part
            heat_out[rows, :] = 0.5 * conduct[0, rows, :] * total
        else:
            low, high = x_faces(parts)
            first[rows, :] = low
            last[rows, :] = high
        return carry

    lax.fori_loop(0, CZ // CHUNK, update, 0)


def finish_field(planes, out):
    for comp in range(6):
        for half in range(CZ // LANES):
            lanes = slice(half * LANES, (half + 1) * LANES)
            out[comp, :, lanes] = planes[comp, lanes, :].T


def pack_heat(flags, starts, heat, below, above, out, ext):
    ext[0:8, :] = kept(flags[4], below[...])
    ext[8 : 8 + CZ, :] = heat[...]
    ext[8 + CZ : 16 + CZ, :] = kept(flags[5], above[...])
    ext[16 + CZ :, :] = jnp.zeros((ext.shape[0] - 16 - CZ, LANES), F32)
    for owner in range(out.shape[0]):
        out[owner] = ext[pl.ds(starts[owner] + 8 - (RING - 1), out.shape[1]), :]


def swap_tiles(value):
    row = lax.broadcasted_iota(jnp.int32, value.shape, value.ndim - 2)
    lane = lane_of(value)
    axis = value.ndim - 2
    for k in range(3):
        step = 1 << k
        row_bit = (row >> k) & 1
        lane_bit = (lane >> (4 + k)) & 1
        up = ahead(pltpu.roll(value, 8 - step, axis), -16 * step)
        down = up if step == 4 else ahead(pltpu.roll(value, step, axis), 16 * step)
        value = jnp.where(row_bit == lane_bit, value, jnp.where(row_bit == 0, up, down))
    return value


def prepare_slab(warm, rates, out):
    for plane in range(out.shape[0]):
        for which, source in enumerate((warm, rates)):
            out[plane, which] = swap_tiles(source[plane].reshape(4, 8, LANES))


def heat_step(info, slab, below1, above1, below2, above2, below3, above3, arrived, factor_out, warm_out, temp, rates, joule):
    count = info[0]
    planes = temp.shape[1]
    owners = arrived.shape[0]
    for plane in range(planes - 2 * RING):
        temp[0, plane + RING] = slab[plane, 0]
        rates[plane + RING] = slab[plane, 1]
    lower = beyond(below1, below2, below3, info[1], info[3])
    upper = beyond(above1, above2, above3, info[2], info[4])
    for depth in range(RING):
        for at, plane in ((RING - 1 - depth, lower[depth]), (RING + count + depth, upper[depth])):
            temp[0, at] = plane[:4]
            rates[at] = plane[4:]
    for owner in range(owners):
        joule[pl.ds(owners + owner, arrived.shape[1], stride=owners), :] = arrived[owner]

    group = 6
    section = time_step / (SECTIONS * SECTIONS)

    def one(step, now, before, base):
        value = temp[now, pl.ds(base - 1, group + 2)]
        mid = value[1:-1]
        lane = lane_of(mid)
        row = lax.broadcasted_iota(jnp.int32, mid.shape, 2)
        none = jnp.zeros_like(mid[:, :1])
        gx_up = jnp.concatenate([mid[:, 1:], none], axis=1)
        gx_down = jnp.concatenate([none, mid[:, :-1]], axis=1)
        gy_up = jnp.where(row == 7, 0.0, pltpu.roll(mid, 7, 2))
        gy_down = jnp.where(row == 0, 0.0, pltpu.roll(mid, 1, 2))
        total = ahead(jnp.where(lane < 16, gx_up, mid), 16)
        total = total + ahead(jnp.where(lane >= 112, gx_down, mid), -16)
        total = total + jnp.where(lane & 15 == 15, ahead(gy_up, -15), ahead(mid, 1))
        total = total + jnp.where(lane & 15 == 0, ahead(gy_down, 15), ahead(mid, -1))
        total = total + value[:-2] + value[2:]
        heat = joule[pl.ds(base * owners, group * owners), :].reshape(group, 4, 8, LANES)
        rate = rates[pl.ds(base, group)] * (total - 6.0 * mid) + heat
        if step == 1:
            temp[before, pl.ds(base, group)] = mid + section * rate
        else:
            old = temp[before, pl.ds(base, group)]
            temp[before, pl.ds(base, group)] = 2.0 * mid - old + 2.0 * section * rate

    for step in range(1, SECTIONS + 1):
        now, before = (step - 1) % 2, step % 2

        def loop(g, carry):
            one(step, now, before, 1 + g * group)
            return carry

        lax.fori_loop(0, (planes - 2) // group, loop, 0)
    final = SECTIONS % 2
    for plane in range(warm_out.shape[0]):
        result = temp[final, plane + RING]
        warm_out[plane] = result
        joule[plane * owners : (plane + 1) * owners, :] = jnp.exp(-heat_drop * result).reshape(owners, LANES)
    for owner in range(owners):
        factor_out[owner] = joule[pl.ds(owner, factor_out.shape[1], stride=owners), :]


def finish_slab(slab_info, warm, out):
    count = slab_info[0]
    for plane in range(out.shape[0]):
        out[plane] = kept(count - plane, swap_tiles(warm[plane])).reshape(32, LANES)


def finish_conduct(starts, returned, conduct, out, rows):
    for owner in range(returned.shape[0]):
        rows[pl.ds(starts[owner], returned.shape[1]), :] = returned[owner]
    for half in range(CZ // LANES):
        lanes = slice(half * LANES, (half + 1) * LANES)
        out[:, lanes] = conduct[:, lanes] * rows[half * LANES : (half + 1) * LANES, :].T


def shape(*dims):
    return jax.ShapeDtypeStruct(dims, F32)


def body(
    earlier_edge_voltage,
    coil_drive_current,
    sigma_omega_cellwise,
    subdomain_inverse_full,
    subdomain_inverse_main,
    subdomain_layer_counts,
    heat_layer_lookup,
    warming_amount,
    heat_spreading_coef,
):
    count_x, count_y, count_z = (lax.axis_size(axis) for axis in ("gx", "gy", "gz"))
    at_x, at_y, at_z = (lax.axis_index(axis) for axis in ("gx", "gy", "gz"))
    owners = count_x * count_y
    segs = subdomain_layer_counts.shape[3]
    slab_cap = warming_amount.shape[3]

    def turn(value, axis, step):
        count = lax.axis_size(axis)
        return lax.ppermute(value, axis, [(i, (i + step) % count) for i in range(count)])

    def device(slab):
        return (slab % owners) * count_z + slab // owners

    def ring(value, step):
        total = owners * count_z
        pairs = [(device(i), device((i + step) % total)) for i in range(total)]
        return lax.ppermute(value, ("gx", "gy", "gz"), pairs)

    flags = jnp.stack(
        [at_x > 0, at_x < count_x - 1, at_y > 0, at_y < count_y - 1, at_z > 0, at_z < count_z - 1]
    ).astype(jnp.int32)
    seg_len = subdomain_layer_counts[0, 0, 0]
    slab_lengths = heat_layer_lookup[0]
    slab_ids = jnp.arange(owners, dtype=jnp.int32)
    starts = jnp.sum(
        jnp.where(slab_ids[None, :] < slab_ids[:, None], slab_lengths[None, :], 0), axis=1
    ).astype(jnp.int32)
    my_owner = at_x * count_y + at_y
    my_length = jnp.sum(jnp.where(slab_ids == my_owner, slab_lengths, 0)).astype(jnp.int32)
    my_slab = at_z * owners + my_owner
    slabs = owners * count_z
    slab_info = jnp.stack(
        [my_length, my_slab > 0, my_slab < slabs - 1, my_slab > 1, my_slab < slabs - 2]
    ).astype(jnp.int32)

    field_bytes = 6 * CZ * LANES * 4
    plane_array = shape(CZ, LANES)
    field, face_low, face_high = pl.pallas_call(
        prepare_field,
        out_shape=(shape(6, CZ, LANES), plane_array, plane_array),
        in_specs=[VMEM],
        out_specs=[VMEM] * 3,
        compiler_params=params(),
        cost_estimate=cost(1 << 20, 2 * field_bytes),
        name="prepare_field",
    )(earlier_edge_voltage.reshape(6, LANES, CZ))
    drive, conduct, diagonal = pl.pallas_call(
        prepare_drive,
        out_shape=(shape(6, CZ, LANES), shape(1, CZ, LANES), shape(512, segs)),
        in_specs=[VMEM] * 3,
        out_specs=[VMEM] * 3,
        compiler_params=params(),
        cost_estimate=cost(1 << 20, 2 * field_bytes),
        name="prepare_drive",
    )(
        coil_drive_current.reshape(6, LANES, CZ),
        sigma_omega_cellwise.reshape(1, LANES, CZ),
        subdomain_inverse_main[0, 0, 0],
    )
    slab = pl.pallas_call(
        prepare_slab,
        out_shape=shape(slab_cap, 2, 4, 8, LANES),
        in_specs=[VMEM] * 2,
        out_specs=VMEM,
        compiler_params=params(),
        cost_estimate=cost(1 << 20, 2 * field_bytes),
        name="prepare_slab",
    )(warming_amount[0, 0, 0], heat_spreading_coef[0, 0, 0])

    def halo(round_id, field, face_low, face_high, extra):
        x_plus, x_minus = turn(face_low, "gx", -1), turn(face_high, "gx", 1)
        message = shape(HALF + 64 * (RING + 1 - round_id) + 8, LANES)
        up, down = pl.pallas_call(
            functools.partial(pack_y, round_id),
            out_shape=(message, message),
            in_specs=[SMEM] * 2 + [VMEM] * 5,
            out_specs=[VMEM] * 2,
            compiler_params=params(),
            cost_estimate=cost(1 << 20, field_bytes),
            name="pack_y",
        )(flags, slab_info, field, x_plus, x_minus, *extra)
        y_plus, y_minus = ring(down, -1), ring(up, 1)
        sides = (x_plus, x_minus, y_plus, y_minus)
        specs = []
        for block, half_block in ((0, 0), (CZ // 8 - 1, HALF // 8 - 1)):
            specs.append(pl.BlockSpec((6, 8, LANES), lambda i, block=block: (0, block, 0)))
            specs += [pl.BlockSpec((8, LANES), lambda i, block=block: (block, 0))] * 2
            specs += [pl.BlockSpec((8, LANES), lambda i, block=half_block: (block, 0))] * 2
        z_low, z_high = pl.pallas_call(
            pack_z,
            grid=(1,),
            out_shape=(shape(16, LANES), shape(16, LANES)),
            in_specs=[SMEM] + specs,
            out_specs=[pl.BlockSpec((16, LANES), lambda i: (0, 0))] * 2,
            compiler_params=params(),
            name="pack_z",
        )(flags, field, *sides, field, *sides)
        z_plus, z_minus = turn(z_low, "gz", -1), turn(z_high, "gz", 1)
        return sides + (z_plus, z_minus)

    solver = subdomain_inverse_full[0, 0, 0]
    extra = (warming_amount[0, 0, 0], heat_spreading_coef[0, 0, 0])
    received = []
    for sweep_index in range(SWEEPS):
        final = sweep_index == SWEEPS - 1
        ghosts = halo(sweep_index + 1, field, face_low, face_high, extra)
        extra = (ghosts[3], ghosts[2])
        received += extra
        scratch = [
            pltpu.VMEM((10, CZ + 2 * HALO, LANES), F32),
            pltpu.VMEM(((CZ + 1 + WINDOW) * PLANE + 8, LANES), F32),
            pltpu.VMEM(((CZ + MAXSEG) * PLANE, LANES), F32),
        ]
        inputs = [flags, seg_len, field, drive, conduct, *ghosts, diagonal, solver]
        specs = [SMEM] * 2 + [VMEM] * 11
        if final:
            outs = (shape(6, CZ, LANES), plane_array)
        else:
            outs = (shape(6, CZ, LANES), plane_array, plane_array)
        result = pl.pallas_call(
            functools.partial(sweep, final),
            out_shape=outs,
            in_specs=specs,
            out_specs=[VMEM] * len(outs),
            scratch_shapes=scratch,
            compiler_params=params(),
            cost_estimate=cost(1 << 28, 4 * field_bytes),
            name="sweep",
        )(*inputs)
        if final:
            field, heat = result
        else:
            field, face_low, face_high = result

    field_new = pl.pallas_call(
        finish_field,
        out_shape=shape(6, LANES, CZ),
        in_specs=[VMEM],
        out_specs=VMEM,
        compiler_params=params(),
        cost_estimate=cost(1 << 20, 2 * field_bytes),
        name="finish_field",
    )(field)
    far = shape(128, LANES)
    far_up, far_down = pl.pallas_call(
        choose_far,
        out_shape=(far, far),
        in_specs=[SMEM] + [VMEM] * 4,
        out_specs=[VMEM] * 2,
        compiler_params=params(),
        name="choose_far",
    )(slab_info, *received)
    received += [ring(far_up, 2), ring(far_down, -2)]
    heat_above, heat_below = turn(heat[:8], "gz", -1), turn(heat[CZ - 8 :], "gz", 1)
    rows = slab_cap + 8
    outgoing = pl.pallas_call(
        pack_heat,
        out_shape=shape(owners, rows, LANES),
        in_specs=[SMEM] * 2 + [VMEM] * 3,
        out_specs=VMEM,
        scratch_shapes=[pltpu.VMEM((CZ + 16 + rows, LANES), F32)],
        compiler_params=params(),
        name="pack_heat",
    )(flags, starts, heat, heat_below, heat_above)
    arrived = lax.all_to_all(outgoing, ("gx", "gy"), split_axis=0, concat_axis=0, tiled=True)
    planes = slab_cap + 2 * RING
    factor, warm = pl.pallas_call(
        heat_step,
        out_shape=(shape(owners, slab_cap, LANES), shape(slab_cap, 4, 8, LANES)),
        in_specs=[SMEM] + [VMEM] * 8,
        out_specs=[VMEM] * 2,
        scratch_shapes=[
            pltpu.VMEM((2, planes, 4, 8, LANES), F32),
            pltpu.VMEM((planes, 4, 8, LANES), F32),
            pltpu.VMEM(((1 + rows) * owners, LANES), F32),
        ],
        compiler_params=params(),
        name="heat_step",
    )(slab_info, slab, *received, arrived)
    returned = lax.all_to_all(factor, ("gx", "gy"), split_axis=0, concat_axis=0, tiled=True)
    renewed_heat_rise = pl.pallas_call(
        finish_slab,
        out_shape=shape(slab_cap, 32, LANES),
        in_specs=[SMEM, VMEM],
        out_specs=VMEM,
        compiler_params=params(),
        name="finish_slab",
    )(slab_info, warm)
    renewed_sigma_omega = pl.pallas_call(
        finish_conduct,
        out_shape=shape(LANES, CZ),
        in_specs=[SMEM] + [VMEM] * 2,
        out_specs=VMEM,
        scratch_shapes=[pltpu.VMEM((CZ + slab_cap, LANES), F32)],
        compiler_params=params(),
        name="finish_conduct",
    )(starts, returned, sigma_omega_cellwise.reshape(LANES, CZ))
    return (
        field_new.reshape(6, CX, CY, CZ),
        renewed_heat_rise[None, None, None],
        renewed_sigma_omega.reshape(CX, CY, CZ),
    )


def solution(mesh):
    return jax.shard_map(
        body,
        mesh=mesh,
        in_specs=(
            P(None, "gx", "gy", "gz"),
            P(None, "gx", "gy", "gz"),
            P("gx", "gy", "gz"),
            P("gx", "gy", "gz", None, None, None),
            P("gx", "gy", "gz", None, None),
            P("gx", "gy", "gz", None),
            P("gz", None),
            P("gx", "gy", "gz", None, None, None),
            P("gx", "gy", "gz", None, None, None),
        ),
        out_specs=(
            P(None, "gx", "gy", "gz"),
            P("gx", "gy", "gz", None, None, None),
            P("gx", "gy", "gz"),
        ),
        check_vma=False,
    )
```

```python
import functools

import jax
import jax.numpy as jnp
from jax import lax
from jax.experimental import pallas as pl
from jax.experimental.pallas import tpu as pltpu
from jax.sharding import PartitionSpec as P

SWEEPS = 2
SECTIONS = 4

mass_shift = 1.0
solver_scale = 0.2
coupling_scale = 0.05
time_step = 2.5
heat_drop = 0.15

CX, CY, CZ = 8, 16, 256
LANES = CX * CY
PLANE = 24
WINDOW = 21
MAXSEG = 19
F32 = jnp.float32
HALO = 8
CHUNK = 32
XP_PLUS, XP_MINUS = 6, 7
X_BITS, Y_BITS = 112, 15
RING = SECTIONS
HALF = CZ // 2
N_X, N_Y, N_Z = 4, 8, 8
OWNERS = N_X * N_Y
CORNER = (0, 1, 16, 17)
VMEM = pl.BlockSpec(memory_space=pltpu.VMEM)
SMEM = pl.BlockSpec(memory_space=pltpu.SMEM)
HBM = pl.BlockSpec(memory_space=pltpu.HBM)


def params(mib=24):
    return pltpu.CompilerParams(vmem_limit_bytes=mib << 20)


def cost(flops, moved):
    return pl.CostEstimate(flops=flops, bytes_accessed=moved, transcendentals=0)


def lane_of(value):
    return lax.broadcasted_iota(jnp.int32, value.shape, value.ndim - 1)


def ahead(value, by):
    shift = (-by) % LANES
    return value if shift == 0 else pltpu.roll(value, shift, value.ndim - 1)


def x_slot(slot):
    return 16 * slot


def y_slot(slot):
    return slot


def x_next(value, halo, slot):
    lane = lane_of(value)
    return jnp.where(lane & X_BITS == X_BITS, ahead(halo, x_slot(slot) - X_BITS), ahead(value, 16))


def x_before(value, halo, slot):
    lane = lane_of(value)
    return jnp.where(lane & X_BITS == 0, ahead(halo, x_slot(slot)), ahead(value, -16))


def y_next(value, halo, slot):
    lane = lane_of(value)
    return jnp.where(lane & Y_BITS == Y_BITS, ahead(halo, y_slot(slot) - Y_BITS), ahead(value, 1))


def y_before(value, halo, slot):
    lane = lane_of(value)
    return jnp.where(lane & Y_BITS == 0, ahead(halo, y_slot(slot)), ahead(value, -1))


def x_faces(parts):
    lane = lane_of(parts[0])
    own = lane & X_BITS
    first = jnp.zeros_like(parts[0])
    last = first
    for slot, part in enumerate(parts):
        mine = own == x_slot(slot)
        first = jnp.where(mine, ahead(part, -x_slot(slot)), first)
        last = jnp.where(mine, ahead(part, X_BITS - x_slot(slot)), last)
    return first, last


def y_faces(parts):
    lane = lane_of(parts[0])
    own = lane & Y_BITS
    first = jnp.zeros_like(parts[0])
    last = first
    for slot, part in enumerate(parts):
        mine = own == y_slot(slot)
        first = jnp.where(mine, ahead(part, -y_slot(slot)), first)
        last = jnp.where(mine, ahead(part, Y_BITS - y_slot(slot)), last)
    return first, last


def sides(place):
    x, y, z = place[0], place[1], place[2]
    return x > 0, x < N_X - 1, y > 0, y < N_Y - 1, z > 0, z < N_Z - 1


def own_slab(place):
    owner = place[0] * N_Y + place[1]
    slab = place[2] * OWNERS + owner
    last = OWNERS * N_Z - 1
    return owner, (slab > 0, slab < last, slab > 1, slab < last - 1)


def kept(flag, value):
    return jnp.where(flag, value, jnp.zeros_like(value))


def to_planes(source, index, target):
    for half in range(CZ // LANES):
        lanes = slice(half * LANES, (half + 1) * LANES)
        target[index, lanes, :] = source[index, :, lanes].T


def prepare_field(field, planes, first, last, loaded, sems):
    copies = [pltpu.make_async_copy(field.at[c], loaded.at[c], sems.at[c]) for c in range(6)]
    for copy in copies:
        copy.start()
    for comp in range(6):
        copies[comp].wait()
        to_planes(loaded, comp, planes)

    def chunk(i, carry):
        rows = pl.ds(pl.multiple_of(i * CHUNK, CHUNK), CHUNK)
        low, high = x_faces([planes[comp, rows, :] for comp in range(6)])
        first[rows, :] = low
        last[rows, :] = high
        return carry

    lax.fori_loop(0, CZ // CHUNK, chunk, 0)


def prepare_rest(
    drive, conduct, diagonal, warm, rates, solver,
    drive_planes, conduct_planes, diagonal_turned, slab, solver_here,
    drive_in, conduct_in, diagonal_in, slab_in, sems,
):
    copies = [pltpu.make_async_copy(warm, slab_in.at[0], sems.at[0])]
    copies.append(pltpu.make_async_copy(rates, slab_in.at[1], sems.at[1]))
    copies.append(pltpu.make_async_copy(drive, drive_in, sems.at[2]))
    copies.append(pltpu.make_async_copy(conduct, conduct_in, sems.at[3]))
    copies.append(pltpu.make_async_copy(diagonal, diagonal_in, sems.at[4]))
    parts = 4
    size = solver.shape[0] // parts
    for part in range(parts):
        at = pl.ds(part * size, size)
        copies.append(pltpu.make_async_copy(solver.at[at], solver_here.at[at], sems.at[5 + part]))
    for copy in copies:
        copy.start()
    batch = 4
    for which in range(2):
        copies[which].wait()
        for base in range(0, slab.shape[0], batch):
            value = slab_in[which, base : base + batch].reshape(4 * batch, 8, LANES)
            slab[base : base + batch, which] = swap_tiles(value).reshape(batch, 4, 8, LANES)
    for copy in copies[2:5]:
        copy.wait()
    for comp in range(6):
        to_planes(drive_in, comp, drive_planes)
    to_planes(conduct_in, 0, conduct_planes)
    diagonal_turned[...] = diagonal_in[...].T
    for copy in copies[5:]:
        copy.wait()


def pack_y(round_id, place, lookup, field, x_plus, x_minus, *rest):
    up, down = rest[-2:]
    flags = sides(place)
    owner, near = own_slab(place)

    def chunk(i, carry):
        parts = []
        for base in (0, HALF):
            rows = pl.ds(pl.multiple_of(base + i * CHUNK, CHUNK), CHUNK)
            parts += [field[comp, rows, :] for comp in range(6)]
            parts += [kept(flags[1], x_plus[rows, :]), kept(flags[0], x_minus[rows, :])]
        low, high = y_faces(parts)
        rows = pl.ds(pl.multiple_of(i * CHUNK, CHUNK), CHUNK)
        down[rows, :] = low
        up[rows, :] = high
        return carry

    lax.fori_loop(0, HALF // CHUNK, chunk, 0)
    if round_id == 1:
        slab = rest[0]
        for depth in range(RING):
            top = jnp.maximum(lookup[owner] - 1 - depth, 0)
            at = slice(HALF + 64 * depth, HALF + 64 * (depth + 1))
            up[at, :] = slab[top].reshape(64, LANES)
            down[at, :] = slab[depth].reshape(64, LANES)
        count = jnp.full((8, LANES), lookup[owner], jnp.int32).astype(F32)
        up[-8:, :] = count
        down[-8:, :] = count
    else:
        below, above = rest[:2]
        size = 64 * (RING - 1)
        up[HALF : HALF + size, :] = kept(near[0], below[HALF : HALF + size, :])
        down[HALF : HALF + size, :] = kept(near[1], above[HALF : HALF + size, :])
        up[-8:, :] = below[-8:, :]
        down[-8:, :] = above[-8:, :]


def planes_of(message, start, count, flag):
    return [
        kept(flag, message[start + 64 * d : start + 64 * (d + 1), :]).reshape(8, 8, LANES)
        for d in range(count)
    ]


def choose_far(place, below1, above1, below2, above2, up, down):
    near = own_slab(place)[1]
    for one, two, out, flag in ((below1, below2, up, near[0]), (above1, above2, down, near[1])):
        first = planes_of(one, HALF, 2, flag)
        second = planes_of(two, HALF, 1, flag)
        out[0:64, :] = first[0].reshape(64, LANES)
        out[64:128, :] = jnp.where(one[-8:, :] > 1.5, first[1], second[0]).reshape(64, LANES)


def beyond(one, two, three, near, far):
    a, b, c = planes_of(one, HALF, 4, near), planes_of(two, HALF, 3, near), planes_of(three, 0, 2, far)
    first, second = one[-8:, :], two[-8:, :]
    two_left = jnp.where(second > 1.5, b[1], c[0])
    three_left = jnp.where(second > 2.5, b[2], jnp.where(second > 1.5, c[0], c[1]))
    return (
        a[0],
        jnp.where(first > 1.5, a[1], b[0]),
        jnp.where(first > 2.5, a[2], jnp.where(first > 1.5, b[0], two_left)),
        jnp.where(
            first > 3.5,
            a[3],
            jnp.where(first > 2.5, b[0], jnp.where(first > 1.5, two_left, three_left)),
        ),
    )


def y_rows(message, row, count, upper):
    value = message[row : row + count, :]
    return ahead(value, 8) if upper else value


def pack_z(place, *refs):
    flags = sides(place)
    lows, highs, (first, last) = refs[:5], refs[5:10], refs[10:]
    for (field, xp, xm, yp, ym), row, out in ((lows, 0, first), (highs, 7, last)):
        for comp in range(6):
            out[comp : comp + 1, :] = field[comp, row : row + 1, :]
        out[6:7, :] = kept(flags[1], xp[row : row + 1, :])
        out[7:8, :] = kept(flags[0], xm[row : row + 1, :])
        out[8:9, :] = kept(flags[3], y_rows(yp, row, 1, row > 0))
        out[9:10, :] = kept(flags[2], y_rows(ym, row, 1, row > 0))
        out[10:16, :] = jnp.zeros((6, LANES), F32)


def curl_chunk(wide, part):
    ex, ey, ez = wide[3 * part], wide[3 * part + 1], wide[3 * part + 2]
    xp, xm, yp, ym = wide[6], wide[7], wide[8], wide[9]
    sx, sy, sz = 3 * part, 3 * part + 1, 3 * part + 2

    def here(v):
        return v[8 : 8 + CHUNK]

    def up(v):
        return v[9 : 9 + CHUNK]

    def down(v):
        return v[7 : 7 + CHUNK]

    upper = [v[8:] for v in (ex, ey, xm, ym)]
    ex_xm = x_before(upper[0], upper[2], sx)
    ey_ym = y_before(upper[1], upper[3], sy)
    ex_xm_up, ex_xm = ex_xm[1 : 1 + CHUNK], ex_xm[:CHUNK]
    ey_ym_up, ey_ym = ey_ym[1 : 1 + CHUNK], ey_ym[:CHUNK]
    lower = [v[: 8 + CHUNK] for v in (ez, xp, yp)]
    ez_xp = x_next(lower[0], lower[1], sz)
    ez_yp = y_next(lower[0], lower[2], sz)
    ez_xp_down, ez_xp = down(ez_xp), ez_xp[8:]
    ez_yp_down, ez_yp = down(ez_yp), ez_yp[8:]
    xp0, xm0, yp0, ym0 = here(xp), here(xm), here(yp), here(ym)
    ex0, ey0, ez0 = here(ex), here(ey), here(ez)
    ex_yp = y_next(ex0, yp0, sx)
    ex_ym = y_before(ex0, ym0, sx)
    ex_xm_yp = x_before(ex_yp, y_next(xm0, yp0, XP_MINUS), sx)
    ey_xp = x_next(ey0, xp0, sy)
    ey_xm = x_before(ey0, xm0, sy)
    ey_xp_ym = x_next(ey_ym, y_before(xp0, ym0, XP_PLUS), sy)
    ez_xm = x_before(ez0, xm0, sz)
    ez_ym = y_before(ez0, ym0, sz)
    kx = 4.0 * ex0 - ex_yp - ex_ym - up(ex) - down(ex)
    kx = kx + (ey_xp - ey0 - ey_xp_ym + ey_ym) + (ez_xp - ez0 - ez_xp_down + down(ez))
    ky = 4.0 * ey0 - ey_xp - ey_xm - up(ey) - down(ey)
    ky = ky + (ex_yp - ex0 - ex_xm_yp + ex_xm) + (ez_yp - ez0 - ez_yp_down + down(ez))
    kz = 4.0 * ez0 - ez_xp - ez_xm - ez_yp - ez_ym
    kz = kz + (up(ex) - ex0 - ex_xm_up + ex_xm) + (up(ey) - ey0 - ey_ym_up + ey_ym)
    return (kx, ky, kz), (ex0, ey0, ez0)


def sweep(last_sweep, place, seg_len, field, drive, conduct, xp, xm, yp, ym, zp, zm, diagonal, solver, *rest):
    if last_sweep:
        field_out, heat_out, ext, columns, solved = rest
    else:
        field_out, first, last, ext, columns, solved = rest
    segs = solver.shape[0]
    flags = sides(place)

    for base in range(0, CZ, CHUNK):
        rows = slice(base, base + CHUNK)
        to = slice(base + HALO, base + HALO + CHUNK)
        for comp in range(6):
            ext[comp, to, :] = field[comp, rows, :]
        ext[6, to, :] = kept(flags[1], xp[rows, :])
        ext[7, to, :] = kept(flags[0], xm[rows, :])
        ext[8, to, :] = kept(flags[3], y_rows(yp, base % HALF, CHUNK, base >= HALF))
        ext[9, to, :] = kept(flags[2], y_rows(ym, base % HALF, CHUNK, base >= HALF))
    for comp in range(10):
        ext[comp, HALO - 1 : HALO, :] = kept(flags[4], zm[comp : comp + 1, :])
        ext[comp, HALO + CZ : HALO + CZ + 1, :] = kept(flags[5], zp[comp : comp + 1, :])

    columns[0:PLANE, :] = jnp.zeros((PLANE, LANES), F32)
    tail = columns.shape[0] - (CZ + 1) * PLANE
    columns[(CZ + 1) * PLANE :, :] = jnp.zeros((tail, LANES), F32)

    def residual(i, carry):
        base = pl.multiple_of(i * CHUNK, CHUNK)
        rows = pl.ds(base, CHUNK)
        wide = [ext[comp, pl.ds(base, CHUNK + 2 * HALO), :] for comp in range(10)]
        curl_real, real = curl_chunk(wide, 0)
        curl_imag, imag = curl_chunk(wide, 1)
        sigma = conduct[0, rows, :]
        for axis in range(3):
            both = (
                curl_real[axis] + mass_shift * real[axis] - sigma * imag[axis],
                curl_imag[axis] + mass_shift * imag[axis] + sigma * real[axis],
            )
            for part in range(2):
                comp = 3 * part + axis
                rest_of = drive[comp, rows, :] - both[part]
                for q in range(4):
                    at = (base + 1) * PLANE + comp * 4 + q
                    columns[pl.ds(at, CHUNK, stride=PLANE), :] = ahead(rest_of, CORNER[q])
        return carry

    lax.fori_loop(0, CZ // CHUNK, residual, 0)

    row_of = lax.broadcasted_iota(jnp.int32, (512, LANES), 0)
    start = jnp.int32(0)
    for s in range(segs):
        length = seg_len[s]
        window = columns[pl.ds(pl.multiple_of(start * PLANE, 8), 512), :]
        window = jnp.where(row_of < (length + 2) * PLANE, window, 0.0).astype(jnp.bfloat16)
        product = jnp.dot(solver[s], window, preferred_element_type=F32)
        scaled = solver_scale * diagonal[:, s : s + 1] * window.astype(F32)
        result = coupling_scale * product + scaled
        to = pl.ds(pl.multiple_of(start * PLANE, 8), MAXSEG * PLANE)
        solved[to, :] = result[PLANE : (MAXSEG + 1) * PLANE, :]
        start = start + length

    def update(i, carry):
        base = pl.multiple_of(i * CHUNK, CHUNK)
        rows = pl.ds(base, CHUNK)
        lane = lax.broadcasted_iota(jnp.int32, (CHUNK, LANES), 1)
        parts = []
        for comp in range(6):
            add = jnp.zeros((CHUNK, LANES), F32)
            for q in range(4):
                piece = solved[pl.ds(base * PLANE + comp * 4 + q, CHUNK, stride=PLANE), :]
                add = jnp.where(lane & 17 == CORNER[q], ahead(piece, -CORNER[q]), add)
            part = field[comp, rows, :] + add
            field_out[comp, rows, :] = part
            parts.append(part)
        if last_sweep:
            total = parts[0] * parts[0]
            for part in parts[1:]:
                total = total + part * part
            heat_out[rows, :] = 0.5 * conduct[0, rows, :] * total
        else:
            low, high = x_faces(parts)
            first[rows, :] = low
            last[rows, :] = high
        return carry

    lax.fori_loop(0, CZ // CHUNK, update, 0)


def finish_field(planes, out):
    for comp in range(6):
        for half in range(CZ // LANES):
            lanes = slice(half * LANES, (half + 1) * LANES)
            out[comp, :, lanes] = planes[comp, lanes, :].T


def pack_heat(place, lookup, heat, below, above, out, ext):
    flags = sides(place)
    ext[0:8, :] = kept(flags[4], below[...])
    ext[8 : 8 + CZ, :] = heat[...]
    ext[8 + CZ : 16 + CZ, :] = kept(flags[5], above[...])
    ext[16 + CZ :, :] = jnp.zeros((ext.shape[0] - 16 - CZ, LANES), F32)
    start = 8 - (RING - 1)
    for owner in range(out.shape[0]):
        out[owner] = ext[pl.ds(start, out.shape[1]), :]
        start = start + lookup[owner]


def swap_tiles(value):
    row = lax.broadcasted_iota(jnp.int32, value.shape, value.ndim - 2)
    lane = lane_of(value)
    axis = value.ndim - 2
    for k in range(3):
        step = 1 << k
        row_bit = (row >> k) & 1
        lane_bit = (lane >> (4 + k)) & 1
        up = ahead(pltpu.roll(value, 8 - step, axis), -16 * step)
        down = up if step == 4 else ahead(pltpu.roll(value, step, axis), 16 * step)
        value = jnp.where(row_bit == lane_bit, value, jnp.where(row_bit == 0, up, down))
    return value


def heat_step(place, lookup, slab, below1, above1, below2, above2, below3, above3, arrived, factor_out, warm_out, temp, rates, joule):
    owner, near = own_slab(place)
    count = lookup[owner]
    planes = temp.shape[1]
    owners = arrived.shape[0]
    for plane in range(planes - 2 * RING):
        temp[0, plane + RING] = slab[plane, 0]
        rates[plane + RING] = slab[plane, 1]
    lower = beyond(below1, below2, below3, near[0], near[2])
    upper = beyond(above1, above2, above3, near[1], near[3])
    for depth in range(RING):
        for at, plane in ((RING - 1 - depth, lower[depth]), (RING + count + depth, upper[depth])):
            temp[0, at] = plane[:4]
            rates[at] = plane[4:]
    for owner in range(owners):
        joule[pl.ds(owners + owner, arrived.shape[1], stride=owners), :] = arrived[owner]

    group = 2
    section = time_step / (SECTIONS * SECTIONS)

    def one(step, now, before, base):
        value = temp[now, pl.ds(base - 1, group + 2)]
        mid = value[1:-1]
        lane = lane_of(mid)
        row = lax.broadcasted_iota(jnp.int32, mid.shape, 2)
        none = jnp.zeros_like(mid[:, :1])
        gx_up = jnp.concatenate([mid[:, 1:], none], axis=1)
        gx_down = jnp.concatenate([none, mid[:, :-1]], axis=1)
        gy_up = jnp.where(row == 7, 0.0, pltpu.roll(mid, 7, 2))
        gy_down = jnp.where(row == 0, 0.0, pltpu.roll(mid, 1, 2))
        total = ahead(jnp.where(lane < 16, gx_up, mid), 16)
        total = total + ahead(jnp.where(lane >= 112, gx_down, mid), -16)
        total = total + jnp.where(lane & 15 == 15, ahead(gy_up, -15), ahead(mid, 1))
        total = total + jnp.where(lane & 15 == 0, ahead(gy_down, 15), ahead(mid, -1))
        total = total + value[:-2] + value[2:]
        heat = joule[pl.ds(base * owners, group * owners), :].reshape(group, 4, 8, LANES)
        rate = rates[pl.ds(base, group)] * (total - 6.0 * mid) + heat
        if step == 1:
            temp[before, pl.ds(base, group)] = mid + section * rate
        else:
            old = temp[before, pl.ds(base, group)]
            temp[before, pl.ds(base, group)] = 2.0 * mid - old + 2.0 * section * rate

    for step in range(1, SECTIONS + 1):
        now, before = (step - 1) % 2, step % 2

        def loop(g, carry):
            one(step, now, before, step + g * group)
            return carry

        trips = (planes - 2 * step) // group
        lax.fori_loop(0, trips, loop, 0, unroll={15: 5, 14: 7, 13: 13, 12: 6}[trips])
    final = SECTIONS % 2
    for plane in range(warm_out.shape[0]):
        result = temp[final, plane + RING]
        warm_out[plane] = result
        joule[plane * owners : (plane + 1) * owners, :] = jnp.exp(-heat_drop * result).reshape(owners, LANES)
    for owner in range(owners):
        factor_out[owner] = joule[pl.ds(owner, factor_out.shape[1], stride=owners), :]


def finish_slab(place, lookup, warm, out):
    count = lookup[own_slab(place)[0]]
    batch = 4
    for base in range(0, out.shape[0], batch):
        value = swap_tiles(warm[base : base + batch].reshape(4 * batch, 8, LANES))
        value = value.reshape(batch, 32, LANES)
        for plane in range(batch):
            out[base + plane] = kept(count > base + plane, value[plane])


def finish_conduct(lookup, returned, conduct, out, rows):
    start = 0
    for owner in range(returned.shape[0]):
        rows[pl.ds(start, returned.shape[1]), :] = returned[owner]
        start = start + lookup[owner]
    for half in range(CZ // LANES):
        lanes = slice(half * LANES, (half + 1) * LANES)
        out[:, lanes] = conduct[:, lanes] * rows[half * LANES : (half + 1) * LANES, :].T


def shape(*dims):
    return jax.ShapeDtypeStruct(dims, F32)


def body(
    earlier_edge_voltage,
    coil_drive_current,
    sigma_omega_cellwise,
    subdomain_inverse_full,
    subdomain_inverse_main,
    subdomain_layer_counts,
    heat_layer_lookup,
    warming_amount,
    heat_spreading_coef,
):
    count_x, count_y, count_z = (lax.axis_size(axis) for axis in ("gx", "gy", "gz"))
    owners = count_x * count_y
    segs = subdomain_layer_counts.shape[3]
    slab_cap = warming_amount.shape[3]

    def turn(value, axis, step):
        count = lax.axis_size(axis)
        return lax.ppermute(value, axis, [(i, (i + step) % count) for i in range(count)])

    def device(slab):
        return (slab % owners) * count_z + slab // owners

    def ring(value, step):
        total = owners * count_z
        pairs = [(device(i), device((i + step) % total)) for i in range(total)]
        return lax.ppermute(value, ("gx", "gy", "gz"), pairs)

    place = jnp.stack([lax.axis_index(axis) for axis in ("gx", "gy", "gz")]).astype(jnp.int32)
    seg_len = subdomain_layer_counts[0, 0, 0]
    lookup = heat_layer_lookup[0]

    field_bytes = 6 * CZ * LANES * 4
    plane_array = shape(CZ, LANES)
    field, face_low, face_high = pl.pallas_call(
        prepare_field,
        out_shape=(shape(6, CZ, LANES), plane_array, plane_array),
        in_specs=[HBM],
        out_specs=[VMEM] * 3,
        scratch_shapes=[pltpu.VMEM((6, LANES, CZ), F32), pltpu.SemaphoreType.DMA((6,))],
        compiler_params=params(),
        cost_estimate=cost(1 << 20, 2 * field_bytes),
        name="prepare_field",
    )(earlier_edge_voltage.reshape(6, LANES, CZ))
    x_ghosts = turn(face_low, "gx", -1), turn(face_high, "gx", 1)
    solver = subdomain_inverse_full[0, 0, 0]
    drive, conduct, diagonal, slab, solver = pl.pallas_call(
        prepare_rest,
        out_shape=(
            shape(6, CZ, LANES),
            shape(1, CZ, LANES),
            shape(512, segs),
            shape(slab_cap, 2, 4, 8, LANES),
            jax.ShapeDtypeStruct(solver.shape, solver.dtype),
        ),
        in_specs=[HBM] * 6,
        out_specs=[VMEM] * 5,
        scratch_shapes=[
            pltpu.VMEM((6, LANES, CZ), F32),
            pltpu.VMEM((1, LANES, CZ), F32),
            pltpu.VMEM((segs, 512), F32),
            pltpu.VMEM((2, slab_cap, 32, LANES), F32),
            pltpu.SemaphoreType.DMA((9,)),
        ],
        compiler_params=params(),
        cost_estimate=cost(1 << 20, 16 * field_bytes),
        name="prepare_rest",
    )(
        coil_drive_current.reshape(6, LANES, CZ),
        sigma_omega_cellwise.reshape(1, LANES, CZ),
        subdomain_inverse_main[0, 0, 0],
        warming_amount[0, 0, 0],
        heat_spreading_coef[0, 0, 0],
        solver,
    )
    x_ghosts, drive, conduct, diagonal, slab, solver = lax.optimization_barrier(
        (x_ghosts, drive, conduct, diagonal, slab, solver)
    )

    def halo(round_id, field, x_plus, x_minus, extra):
        message = shape(HALF + 64 * (RING + 1 - round_id) + 8, LANES)
        up, down = pl.pallas_call(
            functools.partial(pack_y, round_id),
            out_shape=(message, message),
            in_specs=[SMEM] * 2 + [VMEM] * (3 + len(extra)),
            out_specs=[VMEM] * 2,
            compiler_params=params(),
            cost_estimate=cost(1 << 20, field_bytes),
            name="pack_y",
        )(place, lookup, field, x_plus, x_minus, *extra)
        y_plus, y_minus = ring(down, -1), ring(up, 1)
        ghosts = (x_plus, x_minus, y_plus, y_minus)
        specs = []
        for block, half_block in ((0, 0), (CZ // 8 - 1, HALF // 8 - 1)):
            specs.append(pl.BlockSpec((6, 8, LANES), lambda i, block=block: (0, block, 0)))
            specs += [pl.BlockSpec((8, LANES), lambda i, block=block: (block, 0))] * 2
            specs += [pl.BlockSpec((8, LANES), lambda i, block=half_block: (block, 0))] * 2
        z_low, z_high = pl.pallas_call(
            pack_z,
            grid=(1,),
            out_shape=(shape(16, LANES), shape(16, LANES)),
            in_specs=[SMEM] + specs,
            out_specs=[pl.BlockSpec((16, LANES), lambda i: (0, 0))] * 2,
            compiler_params=params(),
            name="pack_z",
        )(place, field, *ghosts, field, *ghosts)
        z_plus, z_minus = turn(z_low, "gz", -1), turn(z_high, "gz", 1)
        return ghosts + (z_plus, z_minus)

    extra = (slab,)
    received = []
    for sweep_index in range(SWEEPS):
        final = sweep_index == SWEEPS - 1
        ghosts = halo(sweep_index + 1, field, *x_ghosts, extra)
        extra = (ghosts[3], ghosts[2])
        received += extra
        scratch = [
            pltpu.VMEM((10, CZ + 2 * HALO, LANES), F32),
            pltpu.VMEM(((CZ + 1 + WINDOW) * PLANE + 8, LANES), F32),
            pltpu.VMEM(((CZ + MAXSEG) * PLANE, LANES), F32),
        ]
        inputs = [place, seg_len, field, drive, conduct, *ghosts, diagonal, solver]
        specs = [SMEM] * 2 + [VMEM] * 11
        if final:
            outs = (shape(6, CZ, LANES), plane_array)
        else:
            outs = (shape(6, CZ, LANES), plane_array, plane_array)
        result = pl.pallas_call(
            functools.partial(sweep, final),
            out_shape=outs,
            in_specs=specs,
            out_specs=[VMEM] * len(outs),
            scratch_shapes=scratch,
            compiler_params=params(),
            cost_estimate=cost(1 << 28, 4 * field_bytes),
            name="sweep",
        )(*inputs)
        if final:
            field, heat = result
        else:
            field, face_low, face_high = result
            x_ghosts = turn(face_low, "gx", -1), turn(face_high, "gx", 1)

    field_new = pl.pallas_call(
        finish_field,
        out_shape=shape(6, LANES, CZ),
        in_specs=[VMEM],
        out_specs=VMEM,
        compiler_params=params(),
        cost_estimate=cost(1 << 20, 2 * field_bytes),
        name="finish_field",
    )(field)
    far = shape(128, LANES)
    far_up, far_down = pl.pallas_call(
        choose_far,
        out_shape=(far, far),
        in_specs=[SMEM] + [VMEM] * 4,
        out_specs=[VMEM] * 2,
        compiler_params=params(),
        name="choose_far",
    )(place, *received)
    received += [ring(far_up, 2), ring(far_down, -2)]
    heat_above, heat_below = turn(heat[:8], "gz", -1), turn(heat[CZ - 8 :], "gz", 1)
    heat_above, heat_below, field_new, *far_planes = lax.optimization_barrier(
        (heat_above, heat_below, field_new, *received[-2:])
    )
    received[-2:] = far_planes
    rows = slab_cap + 8
    outgoing = pl.pallas_call(
        pack_heat,
        out_shape=shape(owners, rows, LANES),
        in_specs=[SMEM] * 2 + [VMEM] * 3,
        out_specs=VMEM,
        scratch_shapes=[pltpu.VMEM((CZ + 16 + rows, LANES), F32)],
        compiler_params=params(),
        name="pack_heat",
    )(place, lookup, heat, heat_below, heat_above)
    arrived = lax.all_to_all(outgoing, ("gx", "gy"), split_axis=0, concat_axis=0, tiled=True)
    planes = slab_cap + 2 * RING
    factor, warm = pl.pallas_call(
        heat_step,
        out_shape=(shape(owners, slab_cap, LANES), shape(slab_cap, 4, 8, LANES)),
        in_specs=[SMEM] * 2 + [VMEM] * 8,
        out_specs=[VMEM] * 2,
        scratch_shapes=[
            pltpu.VMEM((2, planes, 4, 8, LANES), F32),
            pltpu.VMEM((planes, 4, 8, LANES), F32),
            pltpu.VMEM(((1 + rows) * owners, LANES), F32),
        ],
        compiler_params=params(),
        name="heat_step",
    )(place, lookup, slab, *received, arrived)
    returned = lax.all_to_all(factor, ("gx", "gy"), split_axis=0, concat_axis=0, tiled=True)
    renewed_heat_rise = pl.pallas_call(
        finish_slab,
        out_shape=shape(slab_cap, 32, LANES),
        in_specs=[SMEM, SMEM, VMEM],
        out_specs=VMEM,
        compiler_params=params(),
        name="finish_slab",
    )(place, lookup, warm)
    renewed_sigma_omega = pl.pallas_call(
        finish_conduct,
        out_shape=shape(LANES, CZ),
        in_specs=[SMEM] + [VMEM] * 2,
        out_specs=VMEM,
        scratch_shapes=[pltpu.VMEM((CZ + slab_cap, LANES), F32)],
        compiler_params=params(),
        name="finish_conduct",
    )(lookup, returned, sigma_omega_cellwise.reshape(LANES, CZ))
    return (
        field_new.reshape(6, CX, CY, CZ),
        renewed_heat_rise[None, None, None],
        renewed_sigma_omega.reshape(CX, CY, CZ),
    )


def solution(mesh):
    return jax.shard_map(
        body,
        mesh=mesh,
        in_specs=(
            P(None, "gx", "gy", "gz"),
            P(None, "gx", "gy", "gz"),
            P("gx", "gy", "gz"),
            P("gx", "gy", "gz", None, None, None),
            P("gx", "gy", "gz", None, None),
            P("gx", "gy", "gz", None),
            P("gz", None),
            P("gx", "gy", "gz", None, None, None),
            P("gx", "gy", "gz", None, None, None),
        ),
        out_specs=(
            P(None, "gx", "gy", "gz"),
            P("gx", "gy", "gz", None, None, None),
            P("gx", "gy", "gz"),
        ),
        check_vma=False,
    )
```

```python
import functools

import jax
import jax.numpy as jnp
from jax import lax
from jax.experimental import pallas as pl
from jax.experimental.pallas import tpu as pltpu
from jax.sharding import PartitionSpec as P

SWEEPS = 2
SECTIONS = 4

mass_shift = 1.0
solver_scale = 0.2
coupling_scale = 0.05
time_step = 2.5
heat_drop = 0.15

CX, CY, CZ = 8, 16, 256
LANES = CX * CY
PLANE = 24
WINDOW = 21
MAXSEG = 19
F32 = jnp.float32
HALO = 8
CHUNK = 32
XP_PLUS, XP_MINUS = 6, 7
X_BITS, Y_BITS = 112, 15
RING = SECTIONS
HALF = CZ // 2
N_X, N_Y, N_Z = 4, 8, 8
OWNERS = N_X * N_Y
CORNER = (0, 1, 16, 17)
VMEM = pl.BlockSpec(memory_space=pltpu.VMEM)
SMEM = pl.BlockSpec(memory_space=pltpu.SMEM)
HBM = pl.BlockSpec(memory_space=pltpu.HBM)


def params(mib=24):
    return pltpu.CompilerParams(vmem_limit_bytes=mib << 20)


def cost(flops, moved):
    return pl.CostEstimate(flops=flops, bytes_accessed=moved, transcendentals=0)


def lane_of(value):
    return lax.broadcasted_iota(jnp.int32, value.shape, value.ndim - 1)


def ahead(value, by):
    shift = (-by) % LANES
    return value if shift == 0 else pltpu.roll(value, shift, value.ndim - 1)


def x_slot(slot):
    return 16 * slot


def y_slot(slot):
    return slot


def x_next(value, halo, slot):
    lane = lane_of(value)
    return jnp.where(lane & X_BITS == X_BITS, ahead(halo, x_slot(slot) - X_BITS), ahead(value, 16))


def x_before(value, halo, slot):
    lane = lane_of(value)
    return jnp.where(lane & X_BITS == 0, ahead(halo, x_slot(slot)), ahead(value, -16))


def y_next(value, halo, slot):
    lane = lane_of(value)
    return jnp.where(lane & Y_BITS == Y_BITS, ahead(halo, y_slot(slot) - Y_BITS), ahead(value, 1))


def y_before(value, halo, slot):
    lane = lane_of(value)
    return jnp.where(lane & Y_BITS == 0, ahead(halo, y_slot(slot)), ahead(value, -1))


def x_faces(parts):
    lane = lane_of(parts[0])
    own = lane & X_BITS
    first = jnp.zeros_like(parts[0])
    last = first
    for slot, part in enumerate(parts):
        mine = own == x_slot(slot)
        first = jnp.where(mine, ahead(part, -x_slot(slot)), first)
        last = jnp.where(mine, ahead(part, X_BITS - x_slot(slot)), last)
    return first, last


def y_faces(parts):
    lane = lane_of(parts[0])
    own = lane & Y_BITS
    first = jnp.zeros_like(parts[0])
    last = first
    for slot, part in enumerate(parts):
        mine = own == y_slot(slot)
        first = jnp.where(mine, ahead(part, -y_slot(slot)), first)
        last = jnp.where(mine, ahead(part, Y_BITS - y_slot(slot)), last)
    return first, last


def sides(place):
    x, y, z = place[0], place[1], place[2]
    return x > 0, x < N_X - 1, y > 0, y < N_Y - 1, z > 0, z < N_Z - 1


def own_slab(place):
    owner = place[0] * N_Y + place[1]
    slab = place[2] * OWNERS + owner
    last = OWNERS * N_Z - 1
    return owner, (slab > 0, slab < last, slab > 1, slab < last - 1)


def kept(flag, value):
    return jnp.where(flag, value, jnp.zeros_like(value))


def to_planes(source, index, target):
    for half in range(CZ // LANES):
        lanes = slice(half * LANES, (half + 1) * LANES)
        target[index, lanes, :] = source[index, :, lanes].T


def prepare_field(field, planes, first, last, loaded, sems):
    copies = [pltpu.make_async_copy(field.at[c], loaded.at[c], sems.at[c]) for c in range(6)]
    for copy in copies:
        copy.start()
    for comp in range(6):
        copies[comp].wait()
        to_planes(loaded, comp, planes)

    def chunk(i, carry):
        rows = pl.ds(pl.multiple_of(i * CHUNK, CHUNK), CHUNK)
        low, high = x_faces([planes[comp, rows, :] for comp in range(6)])
        first[rows, :] = low
        last[rows, :] = high
        return carry

    lax.fori_loop(0, CZ // CHUNK, chunk, 0)


def prepare_rest(
    drive, conduct, diagonal, warm, rates, solver,
    drive_planes, conduct_planes, diagonal_turned, slab, solver_here,
    drive_in, conduct_in, diagonal_in, slab_in, sems,
):
    copies = [pltpu.make_async_copy(warm, slab_in.at[0], sems.at[0])]
    copies.append(pltpu.make_async_copy(rates, slab_in.at[1], sems.at[1]))
    copies.append(pltpu.make_async_copy(drive, drive_in, sems.at[2]))
    copies.append(pltpu.make_async_copy(conduct, conduct_in, sems.at[3]))
    copies.append(pltpu.make_async_copy(diagonal, diagonal_in, sems.at[4]))
    parts = 4
    size = solver.shape[0] // parts
    for part in range(parts):
        at = pl.ds(part * size, size)
        copies.append(pltpu.make_async_copy(solver.at[at], solver_here.at[at], sems.at[5 + part]))
    for copy in copies:
        copy.start()
    batch = 4
    for which in range(2):
        copies[which].wait()
        for base in range(0, slab.shape[0], batch):
            value = slab_in[which, base : base + batch].reshape(4 * batch, 8, LANES)
            slab[base : base + batch, which] = swap_tiles(value).reshape(batch, 4, 8, LANES)
    for copy in copies[2:5]:
        copy.wait()
    for comp in range(6):
        to_planes(drive_in, comp, drive_planes)
    to_planes(conduct_in, 0, conduct_planes)
    diagonal_turned[...] = diagonal_in[...].T
    for copy in copies[5:]:
        copy.wait()


def pack_y(place, field, x_plus, x_minus, down, up):
    flags = sides(place)

    def chunk(i, carry):
        parts = []
        for base in (0, HALF):
            rows = pl.ds(pl.multiple_of(base + i * CHUNK, CHUNK), CHUNK)
            parts += [field[comp, rows, :] for comp in range(6)]
            parts += [kept(flags[1], x_plus[rows, :]), kept(flags[0], x_minus[rows, :])]
        low, high = y_faces(parts)
        rows = pl.ds(pl.multiple_of(i * CHUNK, CHUNK), CHUNK)
        down[rows, :] = low
        up[rows, :] = high
        return carry

    lax.fori_loop(0, HALF // CHUNK, chunk, 0)


def choose_near(place, lookup, slab, up, down):
    count = lookup[own_slab(place)[0]]
    for depth in range(RING):
        at = slice(64 * depth, 64 * (depth + 1))
        up[at, :] = slab[jnp.maximum(count - 1 - depth, 0)].reshape(64, LANES)
        down[at, :] = slab[depth].reshape(64, LANES)
    count = jnp.full((8, LANES), count, jnp.int32).astype(F32)
    up[-8:, :] = count
    down[-8:, :] = count


def choose_next(place, below, above, up, down):
    near = own_slab(place)[1]
    size = 64 * (RING - 1)
    up[:size, :] = kept(near[0], below[:size, :])
    down[:size, :] = kept(near[1], above[:size, :])
    up[-8:, :] = below[-8:, :]
    down[-8:, :] = above[-8:, :]


def planes_of(message, count, flag):
    return [
        kept(flag, message[64 * d : 64 * (d + 1), :]).reshape(8, 8, LANES)
        for d in range(count)
    ]


def choose_far(place, below1, above1, below2, above2, up, down):
    near = own_slab(place)[1]
    for one, two, out, flag in ((below1, below2, up, near[0]), (above1, above2, down, near[1])):
        first = planes_of(one, 2, flag)
        second = planes_of(two, 1, flag)
        out[0:64, :] = first[0].reshape(64, LANES)
        out[64:128, :] = jnp.where(one[-8:, :] > 1.5, first[1], second[0]).reshape(64, LANES)


def beyond(one, two, three, near, far):
    a, b, c = planes_of(one, 4, near), planes_of(two, 3, near), planes_of(three, 2, far)
    first, second = one[-8:, :], two[-8:, :]
    two_left = jnp.where(second > 1.5, b[1], c[0])
    three_left = jnp.where(second > 2.5, b[2], jnp.where(second > 1.5, c[0], c[1]))
    return (
        a[0],
        jnp.where(first > 1.5, a[1], b[0]),
        jnp.where(first > 2.5, a[2], jnp.where(first > 1.5, b[0], two_left)),
        jnp.where(
            first > 3.5,
            a[3],
            jnp.where(first > 2.5, b[0], jnp.where(first > 1.5, two_left, three_left)),
        ),
    )


def y_rows(message, row, count, upper):
    value = message[row : row + count, :]
    return ahead(value, 8) if upper else value


def pack_z(place, *refs):
    flags = sides(place)
    lows, highs, (first, last) = refs[:5], refs[5:10], refs[10:]
    for (field, xp, xm, yp, ym), row, out in ((lows, 0, first), (highs, 7, last)):
        for comp in range(6):
            out[comp : comp + 1, :] = field[comp, row : row + 1, :]
        out[6:7, :] = kept(flags[1], xp[row : row + 1, :])
        out[7:8, :] = kept(flags[0], xm[row : row + 1, :])
        out[8:9, :] = kept(flags[3], y_rows(yp, row, 1, row > 0))
        out[9:10, :] = kept(flags[2], y_rows(ym, row, 1, row > 0))
        out[10:16, :] = jnp.zeros((6, LANES), F32)


def curl_chunk(wide, part):
    ex, ey, ez = wide[3 * part], wide[3 * part + 1], wide[3 * part + 2]
    xp, xm, yp, ym = wide[6], wide[7], wide[8], wide[9]
    sx, sy, sz = 3 * part, 3 * part + 1, 3 * part + 2

    def here(v):
        return v[8 : 8 + CHUNK]

    def up(v):
        return v[9 : 9 + CHUNK]

    def down(v):
        return v[7 : 7 + CHUNK]

    upper = [v[8:] for v in (ex, ey, xm, ym)]
    ex_xm = x_before(upper[0], upper[2], sx)
    ey_ym = y_before(upper[1], upper[3], sy)
    ex_xm_up, ex_xm = ex_xm[1 : 1 + CHUNK], ex_xm[:CHUNK]
    ey_ym_up, ey_ym = ey_ym[1 : 1 + CHUNK], ey_ym[:CHUNK]
    lower = [v[: 8 + CHUNK] for v in (ez, xp, yp)]
    ez_xp = x_next(lower[0], lower[1], sz)
    ez_yp = y_next(lower[0], lower[2], sz)
    ez_xp_down, ez_xp = down(ez_xp), ez_xp[8:]
    ez_yp_down, ez_yp = down(ez_yp), ez_yp[8:]
    xp0, xm0, yp0, ym0 = here(xp), here(xm), here(yp), here(ym)
    ex0, ey0, ez0 = here(ex), here(ey), here(ez)
    ex_yp = y_next(ex0, yp0, sx)
    ex_ym = y_before(ex0, ym0, sx)
    ex_xm_yp = x_before(ex_yp, y_next(xm0, yp0, XP_MINUS), sx)
    ey_xp = x_next(ey0, xp0, sy)
    ey_xm = x_before(ey0, xm0, sy)
    ey_xp_ym = x_next(ey_ym, y_before(xp0, ym0, XP_PLUS), sy)
    ez_xm = x_before(ez0, xm0, sz)
    ez_ym = y_before(ez0, ym0, sz)
    kx = 4.0 * ex0 - ex_yp - ex_ym - up(ex) - down(ex)
    kx = kx + (ey_xp - ey0 - ey_xp_ym + ey_ym) + (ez_xp - ez0 - ez_xp_down + down(ez))
    ky = 4.0 * ey0 - ey_xp - ey_xm - up(ey) - down(ey)
    ky = ky + (ex_yp - ex0 - ex_xm_yp + ex_xm) + (ez_yp - ez0 - ez_yp_down + down(ez))
    kz = 4.0 * ez0 - ez_xp - ez_xm - ez_yp - ez_ym
    kz = kz + (up(ex) - ex0 - ex_xm_up + ex_xm) + (up(ey) - ey0 - ey_ym_up + ey_ym)
    return (kx, ky, kz), (ex0, ey0, ez0)


def sweep(last_sweep, place, seg_len, field, drive, conduct, xp, xm, yp, ym, zp, zm, diagonal, solver, *rest):
    if last_sweep:
        field_out, heat_out, ext, columns, solved = rest
    else:
        field_out, first, last, ext, columns, solved = rest
    segs = solver.shape[0]
    flags = sides(place)

    for base in range(0, CZ, CHUNK):
        rows = slice(base, base + CHUNK)
        to = slice(base + HALO, base + HALO + CHUNK)
        for comp in range(6):
            ext[comp, to, :] = field[comp, rows, :]
        ext[6, to, :] = kept(flags[1], xp[rows, :])
        ext[7, to, :] = kept(flags[0], xm[rows, :])
        ext[8, to, :] = kept(flags[3], y_rows(yp, base % HALF, CHUNK, base >= HALF))
        ext[9, to, :] = kept(flags[2], y_rows(ym, base % HALF, CHUNK, base >= HALF))
    for comp in range(10):
        ext[comp, HALO - 1 : HALO, :] = kept(flags[4], zm[comp : comp + 1, :])
        ext[comp, HALO + CZ : HALO + CZ + 1, :] = kept(flags[5], zp[comp : comp + 1, :])

    columns[0:PLANE, :] = jnp.zeros((PLANE, LANES), F32)
    tail = columns.shape[0] - (CZ + 1) * PLANE
    columns[(CZ + 1) * PLANE :, :] = jnp.zeros((tail, LANES), F32)

    def residual(i, carry):
        base = pl.multiple_of(i * CHUNK, CHUNK)
        rows = pl.ds(base, CHUNK)
        wide = [ext[comp, pl.ds(base, CHUNK + 2 * HALO), :] for comp in range(10)]
        curl_real, real = curl_chunk(wide, 0)
        curl_imag, imag = curl_chunk(wide, 1)
        sigma = conduct[0, rows, :]
        for axis in range(3):
            both = (
                curl_real[axis] + mass_shift * real[axis] - sigma * imag[axis],
                curl_imag[axis] + mass_shift * imag[axis] + sigma * real[axis],
            )
            for part in range(2):
                comp = 3 * part + axis
                rest_of = drive[comp, rows, :] - both[part]
                for q in range(4):
                    at = (base + 1) * PLANE + comp * 4 + q
                    columns[pl.ds(at, CHUNK, stride=PLANE), :] = ahead(rest_of, CORNER[q])
        return carry

    lax.fori_loop(0, CZ // CHUNK, residual, 0)

    row_of = lax.broadcasted_iota(jnp.int32, (512, LANES), 0)
    start = jnp.int32(0)
    for s in range(segs):
        length = seg_len[s]
        window = columns[pl.ds(pl.multiple_of(start * PLANE, 8), 512), :]
        window = jnp.where(row_of < (length + 2) * PLANE, window, 0.0).astype(jnp.bfloat16)
        product = jnp.dot(solver[s], window, preferred_element_type=F32)
        scaled = solver_scale * diagonal[:, s : s + 1] * window.astype(F32)
        result = coupling_scale * product + scaled
        to = pl.ds(pl.multiple_of(start * PLANE, 8), MAXSEG * PLANE)
        solved[to, :] = result[PLANE : (MAXSEG + 1) * PLANE, :]
        start = start + length

    def update(i, carry):
        base = pl.multiple_of(i * CHUNK, CHUNK)
        rows = pl.ds(base, CHUNK)
        lane = lax.broadcasted_iota(jnp.int32, (CHUNK, LANES), 1)
        parts = []
        for comp in range(6):
            add = jnp.zeros((CHUNK, LANES), F32)
            for q in range(4):
                piece = solved[pl.ds(base * PLANE + comp * 4 + q, CHUNK, stride=PLANE), :]
                add = jnp.where(lane & 17 == CORNER[q], ahead(piece, -CORNER[q]), add)
            part = field[comp, rows, :] + add
            field_out[comp, rows, :] = part
            parts.append(part)
        if last_sweep:
            total = parts[0] * parts[0]
            for part in parts[1:]:
                total = total + part * part
            heat_out[rows, :] = 0.5 * conduct[0, rows, :] * total
        else:
            low, high = x_faces(parts)
            first[rows, :] = low
            last[rows, :] = high
        return carry

    lax.fori_loop(0, CZ // CHUNK, update, 0)


def finish_field(planes, out):
    for comp in range(6):
        for half in range(CZ // LANES):
            lanes = slice(half * LANES, (half + 1) * LANES)
            out[comp, :, lanes] = planes[comp, lanes, :].T


def pack_heat(place, lookup, heat, below, above, out, ext):
    flags = sides(place)
    ext[0:8, :] = kept(flags[4], below[...])
    ext[8 : 8 + CZ, :] = heat[...]
    ext[8 + CZ : 16 + CZ, :] = kept(flags[5], above[...])
    ext[16 + CZ :, :] = jnp.zeros((ext.shape[0] - 16 - CZ, LANES), F32)
    start = 8 - (RING - 1)
    for owner in range(out.shape[0]):
        out[owner] = ext[pl.ds(start, out.shape[1]), :]
        start = start + lookup[owner]


def swap_tiles(value):
    row = lax.broadcasted_iota(jnp.int32, value.shape, value.ndim - 2)
    lane = lane_of(value)
    axis = value.ndim - 2
    for k in range(3):
        step = 1 << k
        row_bit = (row >> k) & 1
        lane_bit = (lane >> (4 + k)) & 1
        up = ahead(pltpu.roll(value, 8 - step, axis), -16 * step)
        down = up if step == 4 else ahead(pltpu.roll(value, step, axis), 16 * step)
        value = jnp.where(row_bit == lane_bit, value, jnp.where(row_bit == 0, up, down))
    return value


def heat_step(place, lookup, slab, below1, above1, below2, above2, below3, above3, arrived, factor_out, warm_out, temp, rates, joule):
    owner, near = own_slab(place)
    count = lookup[owner]
    planes = temp.shape[1]
    owners = arrived.shape[0]
    for plane in range(planes - 2 * RING):
        temp[0, plane + RING] = slab[plane, 0]
        rates[plane + RING] = slab[plane, 1]
    lower = beyond(below1, below2, below3, near[0], near[2])
    upper = beyond(above1, above2, above3, near[1], near[3])
    for depth in range(RING):
        for at, plane in ((RING - 1 - depth, lower[depth]), (RING + count + depth, upper[depth])):
            temp[0, at] = plane[:4]
            rates[at] = plane[4:]
    for owner in range(owners):
        joule[pl.ds(owners + owner, arrived.shape[1], stride=owners), :] = arrived[owner]

    group = 2
    section = time_step / (SECTIONS * SECTIONS)

    def one(step, now, before, base):
        value = temp[now, pl.ds(base - 1, group + 2)]
        mid = value[1:-1]
        lane = lane_of(mid)
        row = lax.broadcasted_iota(jnp.int32, mid.shape, 2)
        none = jnp.zeros_like(mid[:, :1])
        gx_up = jnp.concatenate([mid[:, 1:], none], axis=1)
        gx_down = jnp.concatenate([none, mid[:, :-1]], axis=1)
        gy_up = jnp.where(row == 7, 0.0, pltpu.roll(mid, 7, 2))
        gy_down = jnp.where(row == 0, 0.0, pltpu.roll(mid, 1, 2))
        total = ahead(jnp.where(lane < 16, gx_up, mid), 16)
        total = total + ahead(jnp.where(lane >= 112, gx_down, mid), -16)
        total = total + jnp.where(lane & 15 == 15, ahead(gy_up, -15), ahead(mid, 1))
        total = total + jnp.where(lane & 15 == 0, ahead(gy_down, 15), ahead(mid, -1))
        total = total + value[:-2] + value[2:]
        heat = joule[pl.ds(base * owners, group * owners), :].reshape(group, 4, 8, LANES)
        rate = rates[pl.ds(base, group)] * (total - 6.0 * mid) + heat
        if step == 1:
            temp[before, pl.ds(base, group)] = mid + section * rate
        else:
            old = temp[before, pl.ds(base, group)]
            temp[before, pl.ds(base, group)] = 2.0 * mid - old + 2.0 * section * rate

    for step in range(1, SECTIONS + 1):
        now, before = (step - 1) % 2, step % 2

        def loop(g, carry):
            one(step, now, before, step + g * group)
            return carry

        trips = (planes - 2 * step) // group
        lax.fori_loop(0, trips, loop, 0, unroll={15: 5, 14: 7, 13: 13, 12: 6}[trips])
    final = SECTIONS % 2
    for plane in range(warm_out.shape[0]):
        result = temp[final, plane + RING]
        warm_out[plane] = result
        joule[plane * owners : (plane + 1) * owners, :] = jnp.exp(-heat_drop * result).reshape(owners, LANES)
    for owner in range(owners):
        factor_out[owner] = joule[pl.ds(owner, factor_out.shape[1], stride=owners), :]


def finish_slab(place, lookup, warm, out):
    count = lookup[own_slab(place)[0]]
    batch = 4
    for base in range(0, out.shape[0], batch):
        value = swap_tiles(warm[base : base + batch].reshape(4 * batch, 8, LANES))
        value = value.reshape(batch, 32, LANES)
        for plane in range(batch):
            out[base + plane] = kept(count > base + plane, value[plane])


def finish_conduct(lookup, returned, conduct, out, rows):
    start = 0
    for owner in range(returned.shape[0]):
        rows[pl.ds(start, returned.shape[1]), :] = returned[owner]
        start = start + lookup[owner]
    for half in range(CZ // LANES):
        lanes = slice(half * LANES, (half + 1) * LANES)
        out[:, lanes] = conduct[:, lanes] * rows[half * LANES : (half + 1) * LANES, :].T


def in_hbm(value):
    return pltpu.with_memory_space_constraint(value, pltpu.HBM)


def shape(*dims):
    return jax.ShapeDtypeStruct(dims, F32)


def body(
    earlier_edge_voltage,
    coil_drive_current,
    sigma_omega_cellwise,
    subdomain_inverse_full,
    subdomain_inverse_main,
    subdomain_layer_counts,
    heat_layer_lookup,
    warming_amount,
    heat_spreading_coef,
):
    count_x, count_y, count_z = (lax.axis_size(axis) for axis in ("gx", "gy", "gz"))
    owners = count_x * count_y
    segs = subdomain_layer_counts.shape[3]
    slab_cap = warming_amount.shape[3]

    def turn(value, axis, step):
        count = lax.axis_size(axis)
        return lax.ppermute(value, axis, [(i, (i + step) % count) for i in range(count)])

    def device(slab):
        return (slab % owners) * count_z + slab // owners

    def ring(value, step):
        total = owners * count_z
        pairs = [(device(i), device((i + step) % total)) for i in range(total)]
        return lax.ppermute(value, ("gx", "gy", "gz"), pairs)

    place = jnp.stack([lax.axis_index(axis) for axis in ("gx", "gy", "gz")]).astype(jnp.int32)
    seg_len = subdomain_layer_counts[0, 0, 0]
    lookup = heat_layer_lookup[0]

    field_bytes = 6 * CZ * LANES * 4
    plane_array = shape(CZ, LANES)
    field, face_low, face_high = pl.pallas_call(
        prepare_field,
        out_shape=(shape(6, CZ, LANES), plane_array, plane_array),
        in_specs=[HBM],
        out_specs=[VMEM] * 3,
        scratch_shapes=[pltpu.VMEM((6, LANES, CZ), F32), pltpu.SemaphoreType.DMA((6,))],
        compiler_params=params(),
        cost_estimate=cost(1 << 20, 2 * field_bytes),
        name="prepare_field",
    )(in_hbm(earlier_edge_voltage.reshape(6, LANES, CZ)))
    x_ghosts = turn(face_low, "gx", -1), turn(face_high, "gx", 1)
    solver = subdomain_inverse_full[0, 0, 0]
    drive, conduct, diagonal, slab, solver = pl.pallas_call(
        prepare_rest,
        out_shape=(
            shape(6, CZ, LANES),
            shape(1, CZ, LANES),
            shape(512, segs),
            shape(slab_cap, 2, 4, 8, LANES),
            jax.ShapeDtypeStruct(solver.shape, solver.dtype),
        ),
        in_specs=[HBM] * 6,
        out_specs=[VMEM] * 5,
        scratch_shapes=[
            pltpu.VMEM((6, LANES, CZ), F32),
            pltpu.VMEM((1, LANES, CZ), F32),
            pltpu.VMEM((segs, 512), F32),
            pltpu.VMEM((2, slab_cap, 32, LANES), F32),
            pltpu.SemaphoreType.DMA((9,)),
        ],
        compiler_params=params(),
        cost_estimate=cost(1 << 20, 16 * field_bytes),
        name="prepare_rest",
    )(
        in_hbm(coil_drive_current.reshape(6, LANES, CZ)),
        in_hbm(sigma_omega_cellwise.reshape(1, LANES, CZ)),
        in_hbm(subdomain_inverse_main[0, 0, 0]),
        in_hbm(warming_amount[0, 0, 0]),
        in_hbm(heat_spreading_coef[0, 0, 0]),
        in_hbm(solver),
    )
    x_ghosts, drive, conduct, diagonal, slab, solver = lax.optimization_barrier(
        (x_ghosts, drive, conduct, diagonal, slab, solver)
    )

    def chosen(kernel, rows, *inputs):
        message = shape(rows, LANES)
        small = inputs[1].ndim == 1
        up, down = pl.pallas_call(
            kernel,
            out_shape=(message, message),
            in_specs=[SMEM] * (1 + small) + [VMEM] * (len(inputs) - 1 - small),
            out_specs=[VMEM] * 2,
            compiler_params=params(),
            name=kernel.__name__,
        )(*inputs)
        step = 2 if kernel is choose_far else 1
        return ring(up, step), ring(down, -step)

    def halo(field, x_plus, x_minus):
        message = shape(HALF, LANES)
        down, up = pl.pallas_call(
            pack_y,
            out_shape=(message, message),
            in_specs=[SMEM] + [VMEM] * 3,
            out_specs=[VMEM] * 2,
            compiler_params=params(),
            cost_estimate=cost(1 << 20, field_bytes),
            name="pack_y",
        )(place, field, x_plus, x_minus)
        y_plus, y_minus = turn(down, "gy", -1), turn(up, "gy", 1)
        ghosts = (x_plus, x_minus, y_plus, y_minus)
        specs = []
        for block, half_block in ((0, 0), (CZ // 8 - 1, HALF // 8 - 1)):
            specs.append(pl.BlockSpec((6, 8, LANES), lambda i, block=block: (0, block, 0)))
            specs += [pl.BlockSpec((8, LANES), lambda i, block=block: (block, 0))] * 2
            specs += [pl.BlockSpec((8, LANES), lambda i, block=half_block: (block, 0))] * 2
        z_low, z_high = pl.pallas_call(
            pack_z,
            grid=(1,),
            out_shape=(shape(16, LANES), shape(16, LANES)),
            in_specs=[SMEM] + specs,
            out_specs=[pl.BlockSpec((16, LANES), lambda i: (0, 0))] * 2,
            compiler_params=params(),
            name="pack_z",
        )(place, field, *ghosts, field, *ghosts)
        z_plus, z_minus = turn(z_low, "gz", -1), turn(z_high, "gz", 1)
        return ghosts + (z_plus, z_minus)

    near_planes = chosen(choose_near, 64 * RING + 8, place, lookup, slab)
    for sweep_index in range(SWEEPS):
        final = sweep_index == SWEEPS - 1
        if final:
            next_planes = chosen(choose_next, 64 * (RING - 1) + 8, place, *near_planes)
        ghosts = halo(field, *x_ghosts)
        scratch = [
            pltpu.VMEM((10, CZ + 2 * HALO, LANES), F32),
            pltpu.VMEM(((CZ + 1 + WINDOW) * PLANE + 8, LANES), F32),
            pltpu.VMEM(((CZ + MAXSEG) * PLANE, LANES), F32),
        ]
        inputs = [place, seg_len, field, drive, conduct, *ghosts, diagonal, solver]
        specs = [SMEM] * 2 + [VMEM] * 11
        if final:
            outs = (shape(6, CZ, LANES), plane_array)
        else:
            outs = (shape(6, CZ, LANES), plane_array, plane_array)
        result = pl.pallas_call(
            functools.partial(sweep, final),
            out_shape=outs,
            in_specs=specs,
            out_specs=[VMEM] * len(outs),
            scratch_shapes=scratch,
            compiler_params=params(),
            cost_estimate=cost(1 << 28, 4 * field_bytes),
            name="sweep",
        )(*inputs)
        if final:
            field, heat = result
        else:
            field, face_low, face_high = result
            x_ghosts = turn(face_low, "gx", -1), turn(face_high, "gx", 1)

    field_new = pl.pallas_call(
        finish_field,
        out_shape=shape(6, LANES, CZ),
        in_specs=[VMEM],
        out_specs=VMEM,
        compiler_params=params(),
        cost_estimate=cost(1 << 20, 2 * field_bytes),
        name="finish_field",
    )(field)
    received = [*near_planes, *next_planes]
    received += chosen(choose_far, 128, place, *received)
    heat_above, heat_below = turn(heat[:8], "gz", -1), turn(heat[CZ - 8 :], "gz", 1)
    heat_above, heat_below, field_new, *far_planes = lax.optimization_barrier(
        (heat_above, heat_below, field_new, *received[-2:])
    )
    received[-2:] = far_planes
    rows = slab_cap + 8
    outgoing = pl.pallas_call(
        pack_heat,
        out_shape=shape(owners, rows, LANES),
        in_specs=[SMEM] * 2 + [VMEM] * 3,
        out_specs=VMEM,
        scratch_shapes=[pltpu.VMEM((CZ + 16 + rows, LANES), F32)],
        compiler_params=params(),
        name="pack_heat",
    )(place, lookup, heat, heat_below, heat_above)
    arrived = lax.all_to_all(outgoing, ("gx", "gy"), split_axis=0, concat_axis=0, tiled=True)
    planes = slab_cap + 2 * RING
    factor, warm = pl.pallas_call(
        heat_step,
        out_shape=(shape(owners, slab_cap, LANES), shape(slab_cap, 4, 8, LANES)),
        in_specs=[SMEM] * 2 + [VMEM] * 8,
        out_specs=[VMEM] * 2,
        scratch_shapes=[
            pltpu.VMEM((2, planes, 4, 8, LANES), F32),
            pltpu.VMEM((planes, 4, 8, LANES), F32),
            pltpu.VMEM(((1 + rows) * owners, LANES), F32),
        ],
        compiler_params=params(),
        name="heat_step",
    )(place, lookup, slab, *received, arrived)
    returned = lax.all_to_all(factor, ("gx", "gy"), split_axis=0, concat_axis=0, tiled=True)
    renewed_heat_rise = pl.pallas_call(
        finish_slab,
        out_shape=shape(slab_cap, 32, LANES),
        in_specs=[SMEM, SMEM, VMEM],
        out_specs=VMEM,
        compiler_params=params(),
        name="finish_slab",
    )(place, lookup, warm)
    renewed_sigma_omega = pl.pallas_call(
        finish_conduct,
        out_shape=shape(LANES, CZ),
        in_specs=[SMEM] + [VMEM] * 2,
        out_specs=VMEM,
        scratch_shapes=[pltpu.VMEM((CZ + slab_cap, LANES), F32)],
        compiler_params=params(),
        name="finish_conduct",
    )(lookup, returned, sigma_omega_cellwise.reshape(LANES, CZ))
    return (
        field_new.reshape(6, CX, CY, CZ),
        renewed_heat_rise[None, None, None],
        renewed_sigma_omega.reshape(CX, CY, CZ),
    )


def solution(mesh):
    return jax.shard_map(
        body,
        mesh=mesh,
        in_specs=(
            P(None, "gx", "gy", "gz"),
            P(None, "gx", "gy", "gz"),
            P("gx", "gy", "gz"),
            P("gx", "gy", "gz", None, None, None),
            P("gx", "gy", "gz", None, None),
            P("gx", "gy", "gz", None),
            P("gz", None),
            P("gx", "gy", "gz", None, None, None),
            P("gx", "gy", "gz", None, None, None),
        ),
        out_specs=(
            P(None, "gx", "gy", "gz"),
            P("gx", "gy", "gz", None, None, None),
            P("gx", "gy", "gz"),
        ),
        check_vma=False,
    )
```

```python
import functools

import jax
import jax.numpy as jnp
from jax import lax
from jax.experimental import pallas as pl
from jax.experimental.pallas import tpu as pltpu
from jax.sharding import PartitionSpec as P

SWEEPS = 2
SECTIONS = 4

mass_shift = 1.0
solver_scale = 0.2
coupling_scale = 0.05
time_step = 2.5
heat_drop = 0.15

CX, CY, CZ = 8, 16, 256
LANES = CX * CY
PLANE = 24
WINDOW = 21
MAXSEG = 19
F32 = jnp.float32
HALO = 8
CHUNK = 32
XP_PLUS, XP_MINUS = 6, 7
X_BITS, Y_BITS = 112, 15
RING = SECTIONS
HALF = CZ // 2
N_X, N_Y, N_Z = 4, 8, 8
OWNERS = N_X * N_Y
CORNER = (0, 1, 16, 17)
VMEM = pl.BlockSpec(memory_space=pltpu.VMEM)
SMEM = pl.BlockSpec(memory_space=pltpu.SMEM)
HBM = pl.BlockSpec(memory_space=pltpu.HBM)


def params(mib=24):
    return pltpu.CompilerParams(vmem_limit_bytes=mib << 20)


def cost(flops, moved):
    return pl.CostEstimate(flops=flops, bytes_accessed=moved, transcendentals=0)


def lane_of(value):
    return lax.broadcasted_iota(jnp.int32, value.shape, value.ndim - 1)


def ahead(value, by):
    shift = (-by) % LANES
    return value if shift == 0 else pltpu.roll(value, shift, value.ndim - 1)


def x_slot(slot):
    return 16 * slot


def y_slot(slot):
    return slot


def x_next(value, halo, slot):
    lane = lane_of(value)
    return jnp.where(lane & X_BITS == X_BITS, ahead(halo, x_slot(slot) - X_BITS), ahead(value, 16))


def x_before(value, halo, slot):
    lane = lane_of(value)
    return jnp.where(lane & X_BITS == 0, ahead(halo, x_slot(slot)), ahead(value, -16))


def y_next(value, halo, slot):
    lane = lane_of(value)
    return jnp.where(lane & Y_BITS == Y_BITS, ahead(halo, y_slot(slot) - Y_BITS), ahead(value, 1))


def y_before(value, halo, slot):
    lane = lane_of(value)
    return jnp.where(lane & Y_BITS == 0, ahead(halo, y_slot(slot)), ahead(value, -1))


def x_faces(parts):
    lane = lane_of(parts[0])
    own = lane & X_BITS
    first = jnp.zeros_like(parts[0])
    last = first
    for slot, part in enumerate(parts):
        mine = own == x_slot(slot)
        first = jnp.where(mine, ahead(part, -x_slot(slot)), first)
        last = jnp.where(mine, ahead(part, X_BITS - x_slot(slot)), last)
    return first, last


def y_faces(parts):
    lane = lane_of(parts[0])
    own = lane & Y_BITS
    first = jnp.zeros_like(parts[0])
    last = first
    for slot, part in enumerate(parts):
        mine = own == y_slot(slot)
        first = jnp.where(mine, ahead(part, -y_slot(slot)), first)
        last = jnp.where(mine, ahead(part, Y_BITS - y_slot(slot)), last)
    return first, last


def sides(place):
    x, y, z = place[0], place[1], place[2]
    return x > 0, x < N_X - 1, y > 0, y < N_Y - 1, z > 0, z < N_Z - 1


def own_slab(place):
    owner = place[0] * N_Y + place[1]
    slab = place[2] * OWNERS + owner
    last = OWNERS * N_Z - 1
    return owner, (slab > 0, slab < last, slab > 1, slab < last - 1)


def kept(flag, value):
    return jnp.where(flag, value, jnp.zeros_like(value))


def to_planes(source, index, target):
    for half in range(CZ // LANES):
        lanes = slice(half * LANES, (half + 1) * LANES)
        target[index, lanes, :] = source[index, :, lanes].T


def prepare_field(field, planes, first, last, loaded, sems):
    copies = [pltpu.make_async_copy(field.at[c], loaded.at[c], sems.at[c]) for c in range(6)]
    for copy in copies:
        copy.start()
    for comp in range(6):
        copies[comp].wait()
        to_planes(loaded, comp, planes)

    def chunk(i, carry):
        rows = pl.ds(pl.multiple_of(i * CHUNK, CHUNK), CHUNK)
        low, high = x_faces([planes[comp, rows, :] for comp in range(6)])
        first[rows, :] = low
        last[rows, :] = high
        return carry

    lax.fori_loop(0, CZ // CHUNK, chunk, 0)


def prepare_rest(
    drive, conduct, diagonal, warm, rates, solver,
    drive_planes, conduct_planes, diagonal_turned, slab, solver_here,
    drive_in, conduct_in, diagonal_in, slab_in, sems,
):
    copies = [pltpu.make_async_copy(warm, slab_in.at[0], sems.at[0])]
    copies.append(pltpu.make_async_copy(rates, slab_in.at[1], sems.at[1]))
    copies.append(pltpu.make_async_copy(drive, drive_in, sems.at[2]))
    copies.append(pltpu.make_async_copy(conduct, conduct_in, sems.at[3]))
    copies.append(pltpu.make_async_copy(diagonal, diagonal_in, sems.at[4]))
    parts = 4
    size = solver.shape[0] // parts
    for part in range(parts):
        at = pl.ds(part * size, size)
        copies.append(pltpu.make_async_copy(solver.at[at], solver_here.at[at], sems.at[5 + part]))
    for copy in copies:
        copy.start()
    batch = 4
    for which in range(2):
        copies[which].wait()
        for base in range(0, slab.shape[0], batch):
            value = slab_in[which, base : base + batch].reshape(4 * batch, 8, LANES)
            slab[base : base + batch, which] = swap_tiles(value).reshape(batch, 4, 8, LANES)
    for copy in copies[2:5]:
        copy.wait()
    for comp in range(6):
        to_planes(drive_in, comp, drive_planes)
    to_planes(conduct_in, 0, conduct_planes)
    diagonal_turned[...] = diagonal_in[...].T
    for copy in copies[5:]:
        copy.wait()


def pack_y(place, field, x_plus, x_minus, down, up):
    flags = sides(place)

    def chunk(i, carry):
        parts = []
        for base in (0, HALF):
            rows = pl.ds(pl.multiple_of(base + i * CHUNK, CHUNK), CHUNK)
            parts += [field[comp, rows, :] for comp in range(6)]
            parts += [kept(flags[1], x_plus[rows, :]), kept(flags[0], x_minus[rows, :])]
        low, high = y_faces(parts)
        rows = pl.ds(pl.multiple_of(i * CHUNK, CHUNK), CHUNK)
        down[rows, :] = low
        up[rows, :] = high
        return carry

    lax.fori_loop(0, HALF // CHUNK, chunk, 0)


def choose_near(place, lookup, slab, up, down):
    count = lookup[own_slab(place)[0]]
    for depth in range(RING):
        at = slice(64 * depth, 64 * (depth + 1))
        up[at, :] = slab[jnp.maximum(count - 1 - depth, 0)].reshape(64, LANES)
        down[at, :] = slab[depth].reshape(64, LANES)
    count = jnp.full((8, LANES), count, jnp.int32).astype(F32)
    up[-8:, :] = count
    down[-8:, :] = count


def planes_of(message, count, flag):
    return [
        kept(flag, message[64 * d : 64 * (d + 1), :]).reshape(8, 8, LANES)
        for d in range(count)
    ]


def choose_far(place, below1, above1, below2, above2, up, down):
    flags = own_slab(place)[1]
    for one, two, out, side in ((below1, below2, up, 0), (above1, above2, down, 1)):
        first = planes_of(one, 2, flags[side])
        second = planes_of(two, 1, flags[side + 2])
        out[0:64, :] = first[0].reshape(64, LANES)
        out[64:128, :] = jnp.where(one[-8:, :] > 1.5, first[1], second[0]).reshape(64, LANES)


def beyond(one, two, three, near, far):
    a, b, c = planes_of(one, 4, near), planes_of(two, 3, far), planes_of(three, 2, far)
    first, second = one[-8:, :], two[-8:, :]
    two_left = jnp.where(second > 1.5, b[1], c[0])
    three_left = jnp.where(second > 2.5, b[2], jnp.where(second > 1.5, c[0], c[1]))
    return (
        a[0],
        jnp.where(first > 1.5, a[1], b[0]),
        jnp.where(first > 2.5, a[2], jnp.where(first > 1.5, b[0], two_left)),
        jnp.where(
            first > 3.5,
            a[3],
            jnp.where(first > 2.5, b[0], jnp.where(first > 1.5, two_left, three_left)),
        ),
    )


def y_rows(message, row, count, upper):
    value = message[row : row + count, :]
    return ahead(value, 8) if upper else value


def pack_z(place, *refs):
    flags = sides(place)
    lows, highs, (first, last) = refs[:5], refs[5:10], refs[10:]
    for (field, xp, xm, yp, ym), row, out in ((lows, 0, first), (highs, 7, last)):
        for comp in range(6):
            out[comp : comp + 1, :] = field[comp, row : row + 1, :]
        out[6:7, :] = kept(flags[1], xp[row : row + 1, :])
        out[7:8, :] = kept(flags[0], xm[row : row + 1, :])
        out[8:9, :] = kept(flags[3], y_rows(yp, row, 1, row > 0))
        out[9:10, :] = kept(flags[2], y_rows(ym, row, 1, row > 0))
        out[10:16, :] = jnp.zeros((6, LANES), F32)


def curl_chunk(wide, part):
    ex, ey, ez = wide[3 * part], wide[3 * part + 1], wide[3 * part + 2]
    xp, xm, yp, ym = wide[6], wide[7], wide[8], wide[9]
    sx, sy, sz = 3 * part, 3 * part + 1, 3 * part + 2

    def here(v):
        return v[8 : 8 + CHUNK]

    def up(v):
        return v[9 : 9 + CHUNK]

    def down(v):
        return v[7 : 7 + CHUNK]

    upper = [v[8:] for v in (ex, ey, xm, ym)]
    ex_xm = x_before(upper[0], upper[2], sx)
    ey_ym = y_before(upper[1], upper[3], sy)
    ex_xm_up, ex_xm = ex_xm[1 : 1 + CHUNK], ex_xm[:CHUNK]
    ey_ym_up, ey_ym = ey_ym[1 : 1 + CHUNK], ey_ym[:CHUNK]
    lower = [v[: 8 + CHUNK] for v in (ez, xp, yp)]
    ez_xp = x_next(lower[0], lower[1], sz)
    ez_yp = y_next(lower[0], lower[2], sz)
    ez_xp_down, ez_xp = down(ez_xp), ez_xp[8:]
    ez_yp_down, ez_yp = down(ez_yp), ez_yp[8:]
    xp0, xm0, yp0, ym0 = here(xp), here(xm), here(yp), here(ym)
    ex0, ey0, ez0 = here(ex), here(ey), here(ez)
    ex_yp = y_next(ex0, yp0, sx)
    ex_ym = y_before(ex0, ym0, sx)
    ex_xm_yp = x_before(ex_yp, y_next(xm0, yp0, XP_MINUS), sx)
    ey_xp = x_next(ey0, xp0, sy)
    ey_xm = x_before(ey0, xm0, sy)
    ey_xp_ym = x_next(ey_ym, y_before(xp0, ym0, XP_PLUS), sy)
    ez_xm = x_before(ez0, xm0, sz)
    ez_ym = y_before(ez0, ym0, sz)
    kx = 4.0 * ex0 - ex_yp - ex_ym - up(ex) - down(ex)
    kx = kx + (ey_xp - ey0 - ey_xp_ym + ey_ym) + (ez_xp - ez0 - ez_xp_down + down(ez))
    ky = 4.0 * ey0 - ey_xp - ey_xm - up(ey) - down(ey)
    ky = ky + (ex_yp - ex0 - ex_xm_yp + ex_xm) + (ez_yp - ez0 - ez_yp_down + down(ez))
    kz = 4.0 * ez0 - ez_xp - ez_xm - ez_yp - ez_ym
    kz = kz + (up(ex) - ex0 - ex_xm_up + ex_xm) + (up(ey) - ey0 - ey_ym_up + ey_ym)
    return (kx, ky, kz), (ex0, ey0, ez0)


def sweep(last_sweep, place, seg_len, field, drive, conduct, xp, xm, yp, ym, zp, zm, diagonal, solver, *rest):
    if last_sweep:
        field_out, heat_out, ext, columns, solved = rest
    else:
        field_out, first, last, ext, columns, solved = rest
    segs = solver.shape[0]
    flags = sides(place)

    for base in range(0, CZ, CHUNK):
        rows = slice(base, base + CHUNK)
        to = slice(base + HALO, base + HALO + CHUNK)
        for comp in range(6):
            ext[comp, to, :] = field[comp, rows, :]
        ext[6, to, :] = kept(flags[1], xp[rows, :])
        ext[7, to, :] = kept(flags[0], xm[rows, :])
        ext[8, to, :] = kept(flags[3], y_rows(yp, base % HALF, CHUNK, base >= HALF))
        ext[9, to, :] = kept(flags[2], y_rows(ym, base % HALF, CHUNK, base >= HALF))
    for comp in range(10):
        ext[comp, HALO - 1 : HALO, :] = kept(flags[4], zm[comp : comp + 1, :])
        ext[comp, HALO + CZ : HALO + CZ + 1, :] = kept(flags[5], zp[comp : comp + 1, :])

    columns[0:PLANE, :] = jnp.zeros((PLANE, LANES), F32)
    tail = columns.shape[0] - (CZ + 1) * PLANE
    columns[(CZ + 1) * PLANE :, :] = jnp.zeros((tail, LANES), F32)

    def residual(i, carry):
        base = pl.multiple_of(i * CHUNK, CHUNK)
        rows = pl.ds(base, CHUNK)
        wide = [ext[comp, pl.ds(base, CHUNK + 2 * HALO), :] for comp in range(10)]
        curl_real, real = curl_chunk(wide, 0)
        curl_imag, imag = curl_chunk(wide, 1)
        sigma = conduct[0, rows, :]
        for axis in range(3):
            both = (
                curl_real[axis] + mass_shift * real[axis] - sigma * imag[axis],
                curl_imag[axis] + mass_shift * imag[axis] + sigma * real[axis],
            )
            for part in range(2):
                comp = 3 * part + axis
                rest_of = drive[comp, rows, :] - both[part]
                for q in range(4):
                    at = (base + 1) * PLANE + comp * 4 + q
                    columns[pl.ds(at, CHUNK, stride=PLANE), :] = ahead(rest_of, CORNER[q])
        return carry

    lax.fori_loop(0, CZ // CHUNK, residual, 0)

    row_of = lax.broadcasted_iota(jnp.int32, (512, LANES), 0)
    start = jnp.int32(0)
    for s in range(segs):
        length = seg_len[s]
        window = columns[pl.ds(pl.multiple_of(start * PLANE, 8), 512), :]
        window = jnp.where(row_of < (length + 2) * PLANE, window, 0.0).astype(jnp.bfloat16)
        product = jnp.dot(solver[s], window, preferred_element_type=F32)
        scaled = solver_scale * diagonal[:, s : s + 1] * window.astype(F32)
        result = coupling_scale * product + scaled
        to = pl.ds(pl.multiple_of(start * PLANE, 8), MAXSEG * PLANE)
        solved[to, :] = result[PLANE : (MAXSEG + 1) * PLANE, :]
        start = start + length

    def update(i, carry):
        base = pl.multiple_of(i * CHUNK, CHUNK)
        rows = pl.ds(base, CHUNK)
        lane = lax.broadcasted_iota(jnp.int32, (CHUNK, LANES), 1)
        parts = []
        for comp in range(6):
            add = jnp.zeros((CHUNK, LANES), F32)
            for q in range(4):
                piece = solved[pl.ds(base * PLANE + comp * 4 + q, CHUNK, stride=PLANE), :]
                add = jnp.where(lane & 17 == CORNER[q], ahead(piece, -CORNER[q]), add)
            part = field[comp, rows, :] + add
            field_out[comp, rows, :] = part
            parts.append(part)
        if last_sweep:
            total = parts[0] * parts[0]
            for part in parts[1:]:
                total = total + part * part
            heat_out[rows, :] = 0.5 * conduct[0, rows, :] * total
        else:
            low, high = x_faces(parts)
            first[rows, :] = low
            last[rows, :] = high
        return carry

    lax.fori_loop(0, CZ // CHUNK, update, 0)


def finish_field(planes, out):
    for comp in range(6):
        for half in range(CZ // LANES):
            lanes = slice(half * LANES, (half + 1) * LANES)
            out[comp, :, lanes] = planes[comp, lanes, :].T


def pack_heat(place, lookup, heat, below, above, out, ext):
    flags = sides(place)
    ext[0:8, :] = kept(flags[4], below[...])
    ext[8 : 8 + CZ, :] = heat[...]
    ext[8 + CZ : 16 + CZ, :] = kept(flags[5], above[...])
    ext[16 + CZ :, :] = jnp.zeros((ext.shape[0] - 16 - CZ, LANES), F32)
    start = 8 - (RING - 1)
    for owner in range(out.shape[0]):
        out[owner] = ext[pl.ds(start, out.shape[1]), :]
        start = start + lookup[owner]


def swap_tiles(value):
    row = lax.broadcasted_iota(jnp.int32, value.shape, value.ndim - 2)
    lane = lane_of(value)
    axis = value.ndim - 2
    for k in range(3):
        step = 1 << k
        row_bit = (row >> k) & 1
        lane_bit = (lane >> (4 + k)) & 1
        up = ahead(pltpu.roll(value, 8 - step, axis), -16 * step)
        down = up if step == 4 else ahead(pltpu.roll(value, step, axis), 16 * step)
        value = jnp.where(row_bit == lane_bit, value, jnp.where(row_bit == 0, up, down))
    return value


def heat_step(place, lookup, slab, below1, above1, below2, above2, below3, above3, arrived, factor_out, warm_out, temp, rates, joule):
    owner, near = own_slab(place)
    count = lookup[owner]
    planes = temp.shape[1]
    owners = arrived.shape[0]
    for plane in range(planes - 2 * RING):
        temp[0, plane + RING] = slab[plane, 0]
        rates[plane + RING] = slab[plane, 1]
    lower = beyond(below1, below2, below3, near[0], near[2])
    upper = beyond(above1, above2, above3, near[1], near[3])
    for depth in range(RING):
        for at, plane in ((RING - 1 - depth, lower[depth]), (RING + count + depth, upper[depth])):
            temp[0, at] = plane[:4]
            rates[at] = plane[4:]
    for owner in range(owners):
        joule[pl.ds(owners + owner, arrived.shape[1], stride=owners), :] = arrived[owner]

    group = 2
    section = time_step / (SECTIONS * SECTIONS)

    def one(step, now, before, base):
        value = temp[now, pl.ds(base - 1, group + 2)]
        mid = value[1:-1]
        lane = lane_of(mid)
        row = lax.broadcasted_iota(jnp.int32, mid.shape, 2)
        none = jnp.zeros_like(mid[:, :1])
        gx_up = jnp.concatenate([mid[:, 1:], none], axis=1)
        gx_down = jnp.concatenate([none, mid[:, :-1]], axis=1)
        gy_up = jnp.where(row == 7, 0.0, pltpu.roll(mid, 7, 2))
        gy_down = jnp.where(row == 0, 0.0, pltpu.roll(mid, 1, 2))
        total = ahead(jnp.where(lane < 16, gx_up, mid), 16)
        total = total + ahead(jnp.where(lane >= 112, gx_down, mid), -16)
        total = total + jnp.where(lane & 15 == 15, ahead(gy_up, -15), ahead(mid, 1))
        total = total + jnp.where(lane & 15 == 0, ahead(gy_down, 15), ahead(mid, -1))
        total = total + value[:-2] + value[2:]
        heat = joule[pl.ds(base * owners, group * owners), :].reshape(group, 4, 8, LANES)
        rate = rates[pl.ds(base, group)] * (total - 6.0 * mid) + heat
        if step == 1:
            temp[before, pl.ds(base, group)] = mid + section * rate
        else:
            old = temp[before, pl.ds(base, group)]
            temp[before, pl.ds(base, group)] = 2.0 * mid - old + 2.0 * section * rate

    for step in range(1, SECTIONS + 1):
        now, before = (step - 1) % 2, step % 2

        def loop(g, carry):
            one(step, now, before, step + g * group)
            return carry

        trips = (planes - 2 * step) // group
        lax.fori_loop(0, trips, loop, 0, unroll={15: 5, 14: 7, 13: 13, 12: 6}[trips])
    final = SECTIONS % 2
    for plane in range(warm_out.shape[0]):
        result = temp[final, plane + RING]
        warm_out[plane] = result
        joule[plane * owners : (plane + 1) * owners, :] = jnp.exp(-heat_drop * result).reshape(owners, LANES)
    for owner in range(owners):
        factor_out[owner] = joule[pl.ds(owner, factor_out.shape[1], stride=owners), :]


def finish_slab(place, lookup, warm, out):
    count = lookup[own_slab(place)[0]]
    batch = 4
    for base in range(0, out.shape[0], batch):
        value = swap_tiles(warm[base : base + batch].reshape(4 * batch, 8, LANES))
        value = value.reshape(batch, 32, LANES)
        for plane in range(batch):
            out[base + plane] = kept(count > base + plane, value[plane])


def finish_conduct(lookup, returned, conduct, out, rows):
    start = 0
    for owner in range(returned.shape[0]):
        rows[pl.ds(start, returned.shape[1]), :] = returned[owner]
        start = start + lookup[owner]
    for half in range(CZ // LANES):
        lanes = slice(half * LANES, (half + 1) * LANES)
        out[:, lanes] = conduct[:, lanes] * rows[half * LANES : (half + 1) * LANES, :].T


def in_hbm(value):
    return pltpu.with_memory_space_constraint(value, pltpu.HBM)


def shape(*dims):
    return jax.ShapeDtypeStruct(dims, F32)


def body(
    earlier_edge_voltage,
    coil_drive_current,
    sigma_omega_cellwise,
    subdomain_inverse_full,
    subdomain_inverse_main,
    subdomain_layer_counts,
    heat_layer_lookup,
    warming_amount,
    heat_spreading_coef,
):
    count_x, count_y, count_z = (lax.axis_size(axis) for axis in ("gx", "gy", "gz"))
    owners = count_x * count_y
    segs = subdomain_layer_counts.shape[3]
    slab_cap = warming_amount.shape[3]

    def turn(value, axis, step):
        count = lax.axis_size(axis)
        return lax.ppermute(value, axis, [(i, (i + step) % count) for i in range(count)])

    def device(slab):
        return (slab % owners) * count_z + slab // owners

    def ring(value, step):
        total = owners * count_z
        pairs = [(device(i), device((i + step) % total)) for i in range(total)]
        return lax.ppermute(value, ("gx", "gy", "gz"), pairs)

    place = jnp.stack([lax.axis_index(axis) for axis in ("gx", "gy", "gz")]).astype(jnp.int32)
    seg_len = subdomain_layer_counts[0, 0, 0]
    lookup = heat_layer_lookup[0]

    field_bytes = 6 * CZ * LANES * 4
    plane_array = shape(CZ, LANES)
    field, face_low, face_high = pl.pallas_call(
        prepare_field,
        out_shape=(shape(6, CZ, LANES), plane_array, plane_array),
        in_specs=[HBM],
        out_specs=[VMEM] * 3,
        scratch_shapes=[pltpu.VMEM((6, LANES, CZ), F32), pltpu.SemaphoreType.DMA((6,))],
        compiler_params=params(),
        cost_estimate=cost(1 << 20, 2 * field_bytes),
        name="prepare_field",
    )(in_hbm(earlier_edge_voltage.reshape(6, LANES, CZ)))
    x_ghosts = turn(face_low, "gx", -1), turn(face_high, "gx", 1)
    solver = subdomain_inverse_full[0, 0, 0]
    drive, conduct, diagonal, slab, solver = pl.pallas_call(
        prepare_rest,
        out_shape=(
            shape(6, CZ, LANES),
            shape(1, CZ, LANES),
            shape(512, segs),
            shape(slab_cap, 2, 4, 8, LANES),
            jax.ShapeDtypeStruct(solver.shape, solver.dtype),
        ),
        in_specs=[HBM] * 6,
        out_specs=[VMEM] * 5,
        scratch_shapes=[
            pltpu.VMEM((6, LANES, CZ), F32),
            pltpu.VMEM((1, LANES, CZ), F32),
            pltpu.VMEM((segs, 512), F32),
            pltpu.VMEM((2, slab_cap, 32, LANES), F32),
            pltpu.SemaphoreType.DMA((9,)),
        ],
        compiler_params=params(),
        cost_estimate=cost(1 << 20, 16 * field_bytes),
        name="prepare_rest",
    )(
        in_hbm(coil_drive_current.reshape(6, LANES, CZ)),
        in_hbm(sigma_omega_cellwise.reshape(1, LANES, CZ)),
        in_hbm(subdomain_inverse_main[0, 0, 0]),
        in_hbm(warming_amount[0, 0, 0]),
        in_hbm(heat_spreading_coef[0, 0, 0]),
        in_hbm(solver),
    )
    x_ghosts, drive, conduct, diagonal, slab, solver = lax.optimization_barrier(
        (x_ghosts, drive, conduct, diagonal, slab, solver)
    )

    def chosen(kernel, rows, *inputs):
        small = inputs[1].ndim == 1
        return pl.pallas_call(
            kernel,
            out_shape=(shape(rows, LANES),) * 2,
            in_specs=[SMEM] * (1 + small) + [VMEM] * (len(inputs) - 1 - small),
            out_specs=[VMEM] * 2,
            compiler_params=params(),
            name=kernel.__name__,
        )(*inputs)

    def halo(field, x_plus, x_minus, early, late):
        message = shape(HALF, LANES)
        down, up = pl.pallas_call(
            pack_y,
            out_shape=(message, message),
            in_specs=[SMEM] + [VMEM] * 3,
            out_specs=[VMEM] * 2,
            compiler_params=params(),
            cost_estimate=cost(1 << 20, field_bytes),
            name="pack_y",
        )(place, field, x_plus, x_minus)
        y_plus, y_minus = turn(down, "gy", -1), turn(up, "gy", 1)
        (y_plus, y_minus), early, late = lax.optimization_barrier(((y_plus, y_minus), early, late))
        late = [ring(value, step) for value, step in zip(late, (2, -2))]
        ghosts = (x_plus, x_minus, y_plus, y_minus)
        specs = []
        for block, half_block in ((0, 0), (CZ // 8 - 1, HALF // 8 - 1)):
            specs.append(pl.BlockSpec((6, 8, LANES), lambda i, block=block: (0, block, 0)))
            specs += [pl.BlockSpec((8, LANES), lambda i, block=block: (block, 0))] * 2
            specs += [pl.BlockSpec((8, LANES), lambda i, block=half_block: (block, 0))] * 2
        z_low, z_high = pl.pallas_call(
            pack_z,
            grid=(1,),
            out_shape=(shape(16, LANES), shape(16, LANES)),
            in_specs=[SMEM] + specs,
            out_specs=[pl.BlockSpec((16, LANES), lambda i: (0, 0))] * 2,
            compiler_params=params(),
            name="pack_z",
        )(place, field, *ghosts, field, *ghosts)
        z_plus, z_minus = turn(z_low, "gz", -1), turn(z_high, "gz", 1)
        (z_plus, z_minus), late = lax.optimization_barrier(((z_plus, z_minus), late))
        return ghosts + (z_plus, z_minus), early + late

    received = []
    for sweep_index in range(SWEEPS):
        final = sweep_index == SWEEPS - 1
        if final:
            up, down = chosen(choose_far, 128, place, *received)
            early, late = [ring(up, 2), ring(down, -2)], []
        else:
            up, down = chosen(choose_near, 64 * RING + 8, place, lookup, slab)
            early, late = [ring(up, 1), ring(down, -1)], [up, down]
        x_ghosts, _, _ = lax.optimization_barrier((x_ghosts, up, down))
        ghosts, arrivals = halo(field, *x_ghosts, early, late)
        received += arrivals
        scratch = [
            pltpu.VMEM((10, CZ + 2 * HALO, LANES), F32),
            pltpu.VMEM(((CZ + 1 + WINDOW) * PLANE + 8, LANES), F32),
            pltpu.VMEM(((CZ + MAXSEG) * PLANE, LANES), F32),
        ]
        inputs = [place, seg_len, field, drive, conduct, *ghosts, diagonal, solver]
        specs = [SMEM] * 2 + [VMEM] * 11
        if final:
            outs = (shape(6, CZ, LANES), plane_array)
        else:
            outs = (shape(6, CZ, LANES), plane_array, plane_array)
        result = pl.pallas_call(
            functools.partial(sweep, final),
            out_shape=outs,
            in_specs=specs,
            out_specs=[VMEM] * len(outs),
            scratch_shapes=scratch,
            compiler_params=params(),
            cost_estimate=cost(1 << 28, 4 * field_bytes),
            name="sweep",
        )(*inputs)
        if final:
            field, heat = result
        else:
            field, face_low, face_high = result
            x_ghosts = turn(face_low, "gx", -1), turn(face_high, "gx", 1)

    field_new = pl.pallas_call(
        finish_field,
        out_shape=shape(6, LANES, CZ),
        in_specs=[VMEM],
        out_specs=VMEM,
        compiler_params=params(),
        cost_estimate=cost(1 << 20, 2 * field_bytes),
        name="finish_field",
    )(field)
    heat_above, heat_below = turn(heat[:8], "gz", -1), turn(heat[CZ - 8 :], "gz", 1)
    heat_above, heat_below, field_new = lax.optimization_barrier(
        (heat_above, heat_below, field_new)
    )
    rows = slab_cap + 8
    outgoing = pl.pallas_call(
        pack_heat,
        out_shape=shape(owners, rows, LANES),
        in_specs=[SMEM] * 2 + [VMEM] * 3,
        out_specs=VMEM,
        scratch_shapes=[pltpu.VMEM((CZ + 16 + rows, LANES), F32)],
        compiler_params=params(),
        name="pack_heat",
    )(place, lookup, heat, heat_below, heat_above)
    arrived = lax.all_to_all(outgoing, ("gx", "gy"), split_axis=0, concat_axis=0, tiled=True)
    planes = slab_cap + 2 * RING
    factor, warm = pl.pallas_call(
        heat_step,
        out_shape=(shape(owners, slab_cap, LANES), shape(slab_cap, 4, 8, LANES)),
        in_specs=[SMEM] * 2 + [VMEM] * 8,
        out_specs=[VMEM] * 2,
        scratch_shapes=[
            pltpu.VMEM((2, planes, 4, 8, LANES), F32),
            pltpu.VMEM((planes, 4, 8, LANES), F32),
            pltpu.VMEM(((1 + rows) * owners, LANES), F32),
        ],
        compiler_params=params(),
        name="heat_step",
    )(place, lookup, slab, *received, arrived)
    returned = lax.all_to_all(factor, ("gx", "gy"), split_axis=0, concat_axis=0, tiled=True)
    renewed_heat_rise = pl.pallas_call(
        finish_slab,
        out_shape=shape(slab_cap, 32, LANES),
        in_specs=[SMEM, SMEM, VMEM],
        out_specs=VMEM,
        compiler_params=params(),
        name="finish_slab",
    )(place, lookup, warm)
    renewed_sigma_omega = pl.pallas_call(
        finish_conduct,
        out_shape=shape(LANES, CZ),
        in_specs=[SMEM] + [VMEM] * 2,
        out_specs=VMEM,
        scratch_shapes=[pltpu.VMEM((CZ + slab_cap, LANES), F32)],
        compiler_params=params(),
        name="finish_conduct",
    )(lookup, returned, sigma_omega_cellwise.reshape(LANES, CZ))
    return (
        field_new.reshape(6, CX, CY, CZ),
        renewed_heat_rise[None, None, None],
        renewed_sigma_omega.reshape(CX, CY, CZ),
    )


def solution(mesh):
    return jax.shard_map(
        body,
        mesh=mesh,
        in_specs=(
            P(None, "gx", "gy", "gz"),
            P(None, "gx", "gy", "gz"),
            P("gx", "gy", "gz"),
            P("gx", "gy", "gz", None, None, None),
            P("gx", "gy", "gz", None, None),
            P("gx", "gy", "gz", None),
            P("gz", None),
            P("gx", "gy", "gz", None, None, None),
            P("gx", "gy", "gz", None, None, None),
        ),
        out_specs=(
            P(None, "gx", "gy", "gz"),
            P("gx", "gy", "gz", None, None, None),
            P("gx", "gy", "gz"),
        ),
        check_vma=False,
    )
```

```python
import functools

import jax
import jax.numpy as jnp
from jax import lax
from jax.experimental import pallas as pl
from jax.experimental.pallas import tpu as pltpu
from jax.sharding import PartitionSpec as P

SWEEPS = 2
SECTIONS = 4

mass_shift = 1.0
solver_scale = 0.2
coupling_scale = 0.05
time_step = 2.5
heat_drop = 0.15

CX, CY, CZ = 8, 16, 256
LANES = CX * CY
PLANE = 24
WINDOW = 21
MAXSEG = 19
F32 = jnp.float32
HALO = 8
CHUNK = 32
XP_PLUS, XP_MINUS = 6, 7
X_BITS, Y_BITS = 112, 15
RING = SECTIONS
HALF = CZ // 2
N_X, N_Y, N_Z = 4, 8, 8
OWNERS = N_X * N_Y
CORNER = (0, 1, 16, 17)
VMEM = pl.BlockSpec(memory_space=pltpu.VMEM)
SMEM = pl.BlockSpec(memory_space=pltpu.SMEM)
HBM = pl.BlockSpec(memory_space=pltpu.HBM)


def params(mib=24):
    return pltpu.CompilerParams(vmem_limit_bytes=mib << 20)


def cost(flops, moved):
    return pl.CostEstimate(flops=flops, bytes_accessed=moved, transcendentals=0)


def lane_of(value):
    return lax.broadcasted_iota(jnp.int32, value.shape, value.ndim - 1)


def ahead(value, by):
    shift = (-by) % LANES
    return value if shift == 0 else pltpu.roll(value, shift, value.ndim - 1)


def x_slot(slot):
    return 16 * slot


def y_slot(slot):
    return slot


def x_next(value, halo, slot):
    lane = lane_of(value)
    return jnp.where(lane & X_BITS == X_BITS, ahead(halo, x_slot(slot) - X_BITS), ahead(value, 16))


def x_before(value, halo, slot):
    lane = lane_of(value)
    return jnp.where(lane & X_BITS == 0, ahead(halo, x_slot(slot)), ahead(value, -16))


def y_next(value, halo, slot):
    lane = lane_of(value)
    return jnp.where(lane & Y_BITS == Y_BITS, ahead(halo, y_slot(slot) - Y_BITS), ahead(value, 1))


def y_before(value, halo, slot):
    lane = lane_of(value)
    return jnp.where(lane & Y_BITS == 0, ahead(halo, y_slot(slot)), ahead(value, -1))


def x_faces(parts):
    lane = lane_of(parts[0])
    own = lane & X_BITS
    first = jnp.zeros_like(parts[0])
    last = first
    for slot, part in enumerate(parts):
        mine = own == x_slot(slot)
        first = jnp.where(mine, ahead(part, -x_slot(slot)), first)
        last = jnp.where(mine, ahead(part, X_BITS - x_slot(slot)), last)
    return first, last


def y_faces(parts):
    lane = lane_of(parts[0])
    own = lane & Y_BITS
    first = jnp.zeros_like(parts[0])
    last = first
    for slot, part in enumerate(parts):
        mine = own == y_slot(slot)
        first = jnp.where(mine, ahead(part, -y_slot(slot)), first)
        last = jnp.where(mine, ahead(part, Y_BITS - y_slot(slot)), last)
    return first, last


def sides(place):
    x, y, z = place[0], place[1], place[2]
    return x > 0, x < N_X - 1, y > 0, y < N_Y - 1, z > 0, z < N_Z - 1


def own_slab(place):
    owner = place[0] * N_Y + place[1]
    slab = place[2] * OWNERS + owner
    last = OWNERS * N_Z - 1
    return owner, (slab > 0, slab < last, slab > 1, slab < last - 1)


def kept(flag, value):
    return jnp.where(flag, value, jnp.zeros_like(value))


def to_planes(source, index, target):
    for half in range(CZ // LANES):
        lanes = slice(half * LANES, (half + 1) * LANES)
        target[index, lanes, :] = source[index, :, lanes].T


def prepare_field(field, planes, first, last, loaded, sems):
    copies = [pltpu.make_async_copy(field.at[c], loaded.at[c], sems.at[c]) for c in range(6)]
    for copy in copies:
        copy.start()
    for comp in range(6):
        copies[comp].wait()
        to_planes(loaded, comp, planes)

    def chunk(i, carry):
        rows = pl.ds(pl.multiple_of(i * CHUNK, CHUNK), CHUNK)
        low, high = x_faces([planes[comp, rows, :] for comp in range(6)])
        first[rows, :] = low
        last[rows, :] = high
        return carry

    lax.fori_loop(0, CZ // CHUNK, chunk, 0)


def prepare_rest(
    drive, conduct, diagonal, warm, rates, solver,
    drive_planes, conduct_planes, diagonal_turned, slab, solver_here,
    drive_in, conduct_in, diagonal_in, slab_in, sems,
):
    copies = [pltpu.make_async_copy(warm, slab_in.at[0], sems.at[0])]
    copies.append(pltpu.make_async_copy(rates, slab_in.at[1], sems.at[1]))
    copies.append(pltpu.make_async_copy(drive, drive_in, sems.at[2]))
    copies.append(pltpu.make_async_copy(conduct, conduct_in, sems.at[3]))
    copies.append(pltpu.make_async_copy(diagonal, diagonal_in, sems.at[4]))
    parts = 4
    size = solver.shape[0] // parts
    for part in range(parts):
        at = pl.ds(part * size, size)
        copies.append(pltpu.make_async_copy(solver.at[at], solver_here.at[at], sems.at[5 + part]))
    for copy in copies:
        copy.start()
    batch = 4
    for which in range(2):
        copies[which].wait()
        for base in range(0, slab.shape[0], batch):
            value = slab_in[which, base : base + batch].reshape(4 * batch, 8, LANES)
            slab[base : base + batch, which] = swap_tiles(value).reshape(batch, 4, 8, LANES)
    for copy in copies[2:5]:
        copy.wait()
    for comp in range(6):
        to_planes(drive_in, comp, drive_planes)
    to_planes(conduct_in, 0, conduct_planes)
    diagonal_turned[...] = diagonal_in[...].T
    for copy in copies[5:]:
        copy.wait()


def pack_y(place, field, x_plus, x_minus, down, up):
    flags = sides(place)

    def chunk(i, carry):
        parts = []
        for base in (0, HALF):
            rows = pl.ds(pl.multiple_of(base + i * CHUNK, CHUNK), CHUNK)
            parts += [field[comp, rows, :] for comp in range(6)]
            parts += [kept(flags[1], x_plus[rows, :]), kept(flags[0], x_minus[rows, :])]
        low, high = y_faces(parts)
        rows = pl.ds(pl.multiple_of(i * CHUNK, CHUNK), CHUNK)
        down[rows, :] = low
        up[rows, :] = high
        return carry

    lax.fori_loop(0, HALF // CHUNK, chunk, 0)


def choose_near(place, lookup, slab, up, down):
    count = lookup[own_slab(place)[0]]
    for depth in range(RING):
        at = slice(64 * depth, 64 * (depth + 1))
        up[at, :] = slab[jnp.maximum(count - 1 - depth, 0)].reshape(64, LANES)
        down[at, :] = slab[depth].reshape(64, LANES)
    count = jnp.full((8, LANES), count, jnp.int32).astype(F32)
    up[-8:, :] = count
    down[-8:, :] = count


def choose_next(place, below, above, up, down):
    near = own_slab(place)[1]
    size = 64 * (RING - 1)
    up[:size, :] = kept(near[0], below[:size, :])
    down[:size, :] = kept(near[1], above[:size, :])
    up[-8:, :] = below[-8:, :]
    down[-8:, :] = above[-8:, :]


def planes_of(message, count, flag):
    return [
        kept(flag, message[64 * d : 64 * (d + 1), :]).reshape(8, 8, LANES)
        for d in range(count)
    ]


def choose_far(place, below1, above1, below2, above2, up, down):
    near = own_slab(place)[1]
    for one, two, out, flag in ((below1, below2, up, near[0]), (above1, above2, down, near[1])):
        first = planes_of(one, 2, flag)
        second = planes_of(two, 1, flag)
        out[0:64, :] = first[0].reshape(64, LANES)
        out[64:128, :] = jnp.where(one[-8:, :] > 1.5, first[1], second[0]).reshape(64, LANES)


def beyond(one, two, three, near, far):
    a, b, c = planes_of(one, 4, near), planes_of(two, 3, near), planes_of(three, 2, far)
    first, second = one[-8:, :], two[-8:, :]
    two_left = jnp.where(second > 1.5, b[1], c[0])
    three_left = jnp.where(second > 2.5, b[2], jnp.where(second > 1.5, c[0], c[1]))
    return (
        a[0],
        jnp.where(first > 1.5, a[1], b[0]),
        jnp.where(first > 2.5, a[2], jnp.where(first > 1.5, b[0], two_left)),
        jnp.where(
            first > 3.5,
            a[3],
            jnp.where(first > 2.5, b[0], jnp.where(first > 1.5, two_left, three_left)),
        ),
    )


def y_rows(message, row, count, upper):
    value = message[row : row + count, :]
    return ahead(value, 8) if upper else value


def pack_z(place, *refs):
    flags = sides(place)
    lows, highs, (first, last) = refs[:5], refs[5:10], refs[10:]
    for (field, xp, xm, yp, ym), row, out in ((lows, 0, first), (highs, 7, last)):
        for comp in range(6):
            out[comp : comp + 1, :] = field[comp, row : row + 1, :]
        out[6:7, :] = kept(flags[1], xp[row : row + 1, :])
        out[7:8, :] = kept(flags[0], xm[row : row + 1, :])
        out[8:9, :] = kept(flags[3], y_rows(yp, row, 1, row > 0))
        out[9:10, :] = kept(flags[2], y_rows(ym, row, 1, row > 0))
        out[10:16, :] = jnp.zeros((6, LANES), F32)


def curl_chunk(wide, part):
    ex, ey, ez = wide[3 * part], wide[3 * part + 1], wide[3 * part + 2]
    xp, xm, yp, ym = wide[6], wide[7], wide[8], wide[9]
    sx, sy, sz = 3 * part, 3 * part + 1, 3 * part + 2

    def here(v):
        return v[8 : 8 + CHUNK]

    def up(v):
        return v[9 : 9 + CHUNK]

    def down(v):
        return v[7 : 7 + CHUNK]

    upper = [v[8:] for v in (ex, ey, xm, ym)]
    ex_xm = x_before(upper[0], upper[2], sx)
    ey_ym = y_before(upper[1], upper[3], sy)
    ex_xm_up, ex_xm = ex_xm[1 : 1 + CHUNK], ex_xm[:CHUNK]
    ey_ym_up, ey_ym = ey_ym[1 : 1 + CHUNK], ey_ym[:CHUNK]
    lower = [v[: 8 + CHUNK] for v in (ez, xp, yp)]
    ez_xp = x_next(lower[0], lower[1], sz)
    ez_yp = y_next(lower[0], lower[2], sz)
    ez_xp_down, ez_xp = down(ez_xp), ez_xp[8:]
    ez_yp_down, ez_yp = down(ez_yp), ez_yp[8:]
    xp0, xm0, yp0, ym0 = here(xp), here(xm), here(yp), here(ym)
    ex0, ey0, ez0 = here(ex), here(ey), here(ez)
    ex_yp = y_next(ex0, yp0, sx)
    ex_ym = y_before(ex0, ym0, sx)
    ex_xm_yp = x_before(ex_yp, y_next(xm0, yp0, XP_MINUS), sx)
    ey_xp = x_next(ey0, xp0, sy)
    ey_xm = x_before(ey0, xm0, sy)
    ey_xp_ym = x_next(ey_ym, y_before(xp0, ym0, XP_PLUS), sy)
    ez_xm = x_before(ez0, xm0, sz)
    ez_ym = y_before(ez0, ym0, sz)
    kx = 4.0 * ex0 - ex_yp - ex_ym - up(ex) - down(ex)
    kx = kx + (ey_xp - ey0 - ey_xp_ym + ey_ym) + (ez_xp - ez0 - ez_xp_down + down(ez))
    ky = 4.0 * ey0 - ey_xp - ey_xm - up(ey) - down(ey)
    ky = ky + (ex_yp - ex0 - ex_xm_yp + ex_xm) + (ez_yp - ez0 - ez_yp_down + down(ez))
    kz = 4.0 * ez0 - ez_xp - ez_xm - ez_yp - ez_ym
    kz = kz + (up(ex) - ex0 - ex_xm_up + ex_xm) + (up(ey) - ey0 - ey_ym_up + ey_ym)
    return (kx, ky, kz), (ex0, ey0, ez0)


def sweep(last_sweep, place, seg_len, field, drive, conduct, xp, xm, yp, ym, zp, zm, diagonal, solver, *rest):
    if last_sweep:
        field_out, heat_out, ext, columns, solved = rest
    else:
        field_out, first, last, ext, columns, solved = rest
    segs = solver.shape[0]
    flags = sides(place)

    for base in range(0, CZ, CHUNK):
        rows = slice(base, base + CHUNK)
        to = slice(base + HALO, base + HALO + CHUNK)
        for comp in range(6):
            ext[comp, to, :] = field[comp, rows, :]
        ext[6, to, :] = kept(flags[1], xp[rows, :])
        ext[7, to, :] = kept(flags[0], xm[rows, :])
        ext[8, to, :] = kept(flags[3], y_rows(yp, base % HALF, CHUNK, base >= HALF))
        ext[9, to, :] = kept(flags[2], y_rows(ym, base % HALF, CHUNK, base >= HALF))
    for comp in range(10):
        ext[comp, HALO - 1 : HALO, :] = kept(flags[4], zm[comp : comp + 1, :])
        ext[comp, HALO + CZ : HALO + CZ + 1, :] = kept(flags[5], zp[comp : comp + 1, :])

    columns[0:PLANE, :] = jnp.zeros((PLANE, LANES), F32)
    tail = columns.shape[0] - (CZ + 1) * PLANE
    columns[(CZ + 1) * PLANE :, :] = jnp.zeros((tail, LANES), F32)

    def residual(i, carry):
        base = pl.multiple_of(i * CHUNK, CHUNK)
        rows = pl.ds(base, CHUNK)
        wide = [ext[comp, pl.ds(base, CHUNK + 2 * HALO), :] for comp in range(10)]
        curl_real, real = curl_chunk(wide, 0)
        curl_imag, imag = curl_chunk(wide, 1)
        sigma = conduct[0, rows, :]
        for axis in range(3):
            both = (
                curl_real[axis] + mass_shift * real[axis] - sigma * imag[axis],
                curl_imag[axis] + mass_shift * imag[axis] + sigma * real[axis],
            )
            for part in range(2):
                comp = 3 * part + axis
                rest_of = drive[comp, rows, :] - both[part]
                for q in range(4):
                    at = (base + 1) * PLANE + comp * 4 + q
                    columns[pl.ds(at, CHUNK, stride=PLANE), :] = ahead(rest_of, CORNER[q])
        return carry

    lax.fori_loop(0, CZ // CHUNK, residual, 0)

    row_of = lax.broadcasted_iota(jnp.int32, (512, LANES), 0)
    start = jnp.int32(0)
    for s in range(segs):
        length = seg_len[s]
        window = columns[pl.ds(pl.multiple_of(start * PLANE, 8), 512), :]
        window = jnp.where(row_of < (length + 2) * PLANE, window, 0.0).astype(jnp.bfloat16)
        product = jnp.dot(solver[s], window, preferred_element_type=F32)
        scaled = solver_scale * diagonal[:, s : s + 1] * window.astype(F32)
        result = coupling_scale * product + scaled
        to = pl.ds(pl.multiple_of(start * PLANE, 8), MAXSEG * PLANE)
        solved[to, :] = result[PLANE : (MAXSEG + 1) * PLANE, :]
        start = start + length

    def update(i, carry):
        base = pl.multiple_of(i * CHUNK, CHUNK)
        rows = pl.ds(base, CHUNK)
        lane = lax.broadcasted_iota(jnp.int32, (CHUNK, LANES), 1)
        parts = []
        for comp in range(6):
            add = jnp.zeros((CHUNK, LANES), F32)
            for q in range(4):
                piece = solved[pl.ds(base * PLANE + comp * 4 + q, CHUNK, stride=PLANE), :]
                add = jnp.where(lane & 17 == CORNER[q], ahead(piece, -CORNER[q]), add)
            part = field[comp, rows, :] + add
            field_out[comp, rows, :] = part
            parts.append(part)
        if last_sweep:
            total = parts[0] * parts[0]
            for part in parts[1:]:
                total = total + part * part
            heat_out[rows, :] = 0.5 * conduct[0, rows, :] * total
        else:
            low, high = x_faces(parts)
            first[rows, :] = low
            last[rows, :] = high
        return carry

    lax.fori_loop(0, CZ // CHUNK, update, 0)


def finish_field(planes, out):
    for comp in range(6):
        for half in range(CZ // LANES):
            lanes = slice(half * LANES, (half + 1) * LANES)
            out[comp, :, lanes] = planes[comp, lanes, :].T


def pack_heat(place, lookup, heat, below, above, out, ext):
    flags = sides(place)
    ext[0:8, :] = kept(flags[4], below[...])
    ext[8 : 8 + CZ, :] = heat[...]
    ext[8 + CZ : 16 + CZ, :] = kept(flags[5], above[...])
    ext[16 + CZ :, :] = jnp.zeros((ext.shape[0] - 16 - CZ, LANES), F32)
    start = 8 - (RING - 1)
    for owner in range(out.shape[0]):
        out[owner] = ext[pl.ds(start, out.shape[1]), :]
        start = start + lookup[owner]


def swap_tiles(value):
    row = lax.broadcasted_iota(jnp.int32, value.shape, value.ndim - 2)
    lane = lane_of(value)
    axis = value.ndim - 2
    for k in range(3):
        step = 1 << k
        row_bit = (row >> k) & 1
        lane_bit = (lane >> (4 + k)) & 1
        up = ahead(pltpu.roll(value, 8 - step, axis), -16 * step)
        down = up if step == 4 else ahead(pltpu.roll(value, step, axis), 16 * step)
        value = jnp.where(row_bit == lane_bit, value, jnp.where(row_bit == 0, up, down))
    return value


def heat_step(place, lookup, slab, below1, above1, below2, above2, below3, above3, arrived, factor_out, warm_out, temp, rates, joule):
    owner, near = own_slab(place)
    count = lookup[owner]
    planes = temp.shape[1]
    owners = arrived.shape[0]
    for plane in range(planes - 2 * RING):
        temp[0, plane + RING] = slab[plane, 0]
        rates[plane + RING] = slab[plane, 1]
    lower = beyond(below1, below2, below3, near[0], near[2])
    upper = beyond(above1, above2, above3, near[1], near[3])
    for depth in range(RING):
        for at, plane in ((RING - 1 - depth, lower[depth]), (RING + count + depth, upper[depth])):
            temp[0, at] = plane[:4]
            rates[at] = plane[4:]
    for owner in range(owners):
        joule[pl.ds(owners + owner, arrived.shape[1], stride=owners), :] = arrived[owner]

    group = 2
    section = time_step / (SECTIONS * SECTIONS)

    def one(step, now, before, base):
        value = temp[now, pl.ds(base - 1, group + 2)]
        mid = value[1:-1]
        lane = lane_of(mid)
        row = lax.broadcasted_iota(jnp.int32, mid.shape, 2)
        none = jnp.zeros_like(mid[:, :1])
        gx_up = jnp.concatenate([mid[:, 1:], none], axis=1)
        gx_down = jnp.concatenate([none, mid[:, :-1]], axis=1)
        gy_up = jnp.where(row == 7, 0.0, pltpu.roll(mid, 7, 2))
        gy_down = jnp.where(row == 0, 0.0, pltpu.roll(mid, 1, 2))
        total = ahead(jnp.where(lane < 16, gx_up, mid), 16)
        total = total + ahead(jnp.where(lane >= 112, gx_down, mid), -16)
        total = total + jnp.where(lane & 15 == 15, ahead(gy_up, -15), ahead(mid, 1))
        total = total + jnp.where(lane & 15 == 0, ahead(gy_down, 15), ahead(mid, -1))
        total = total + value[:-2] + value[2:]
        heat = joule[pl.ds(base * owners, group * owners), :].reshape(group, 4, 8, LANES)
        rate = rates[pl.ds(base, group)] * (total - 6.0 * mid) + heat
        if step == 1:
            temp[before, pl.ds(base, group)] = mid + section * rate
        else:
            old = temp[before, pl.ds(base, group)]
            temp[before, pl.ds(base, group)] = 2.0 * mid - old + 2.0 * section * rate

    for step in range(1, SECTIONS + 1):
        now, before = (step - 1) % 2, step % 2

        def loop(g, carry):
            one(step, now, before, step + g * group)
            return carry

        trips = (planes - 2 * step) // group
        lax.fori_loop(0, trips, loop, 0, unroll={15: 5, 14: 7, 13: 13, 12: 6}[trips])
    final = SECTIONS % 2
    for plane in range(warm_out.shape[0]):
        result = temp[final, plane + RING]
        warm_out[plane] = result
        joule[plane * owners : (plane + 1) * owners, :] = jnp.exp(-heat_drop * result).reshape(owners, LANES)
    for owner in range(owners):
        factor_out[owner] = joule[pl.ds(owner, factor_out.shape[1], stride=owners), :]


def finish_slab(place, lookup, warm, out):
    count = lookup[own_slab(place)[0]]
    batch = 4
    for base in range(0, out.shape[0], batch):
        value = swap_tiles(warm[base : base + batch].reshape(4 * batch, 8, LANES))
        value = value.reshape(batch, 32, LANES)
        for plane in range(batch):
            out[base + plane] = kept(count > base + plane, value[plane])


def finish_conduct(lookup, returned, conduct, out, rows):
    start = 0
    for owner in range(returned.shape[0]):
        rows[pl.ds(start, returned.shape[1]), :] = returned[owner]
        start = start + lookup[owner]
    for half in range(CZ // LANES):
        lanes = slice(half * LANES, (half + 1) * LANES)
        out[:, lanes] = conduct[:, lanes] * rows[half * LANES : (half + 1) * LANES, :].T


def in_hbm(value):
    return pltpu.with_memory_space_constraint(value, pltpu.HBM)


def shape(*dims):
    return jax.ShapeDtypeStruct(dims, F32)


def body(
    earlier_edge_voltage,
    coil_drive_current,
    sigma_omega_cellwise,
    subdomain_inverse_full,
    subdomain_inverse_main,
    subdomain_layer_counts,
    heat_layer_lookup,
    warming_amount,
    heat_spreading_coef,
):
    count_x, count_y, count_z = (lax.axis_size(axis) for axis in ("gx", "gy", "gz"))
    owners = count_x * count_y
    segs = subdomain_layer_counts.shape[3]
    slab_cap = warming_amount.shape[3]

    def turn(value, axis, step):
        count = lax.axis_size(axis)
        return lax.ppermute(value, axis, [(i, (i + step) % count) for i in range(count)])

    def device(slab):
        return (slab % owners) * count_z + slab // owners

    def ring(value, step):
        total = owners * count_z
        pairs = [(device(i), device((i + step) % total)) for i in range(total)]
        return lax.ppermute(value, ("gx", "gy", "gz"), pairs)

    place = jnp.stack([lax.axis_index(axis) for axis in ("gx", "gy", "gz")]).astype(jnp.int32)
    seg_len = subdomain_layer_counts[0, 0, 0]
    lookup = heat_layer_lookup[0]

    field_bytes = 6 * CZ * LANES * 4
    plane_array = shape(CZ, LANES)
    field, face_low, face_high = pl.pallas_call(
        prepare_field,
        out_shape=(shape(6, CZ, LANES), plane_array, plane_array),
        in_specs=[HBM],
        out_specs=[VMEM] * 3,
        scratch_shapes=[pltpu.VMEM((6, LANES, CZ), F32), pltpu.SemaphoreType.DMA((6,))],
        compiler_params=params(),
        cost_estimate=cost(1 << 20, 2 * field_bytes),
        name="prepare_field",
    )(in_hbm(earlier_edge_voltage.reshape(6, LANES, CZ)))
    x_ghosts = turn(face_low, "gx", -1), turn(face_high, "gx", 1)
    solver = subdomain_inverse_full[0, 0, 0]
    drive, conduct, diagonal, slab, solver = pl.pallas_call(
        prepare_rest,
        out_shape=(
            shape(6, CZ, LANES),
            shape(1, CZ, LANES),
            shape(512, segs),
            shape(slab_cap, 2, 4, 8, LANES),
            jax.ShapeDtypeStruct(solver.shape, solver.dtype),
        ),
        in_specs=[HBM] * 6,
        out_specs=[VMEM] * 5,
        scratch_shapes=[
            pltpu.VMEM((6, LANES, CZ), F32),
            pltpu.VMEM((1, LANES, CZ), F32),
            pltpu.VMEM((segs, 512), F32),
            pltpu.VMEM((2, slab_cap, 32, LANES), F32),
            pltpu.SemaphoreType.DMA((9,)),
        ],
        compiler_params=params(),
        cost_estimate=cost(1 << 20, 16 * field_bytes),
        name="prepare_rest",
    )(
        in_hbm(coil_drive_current.reshape(6, LANES, CZ)),
        in_hbm(sigma_omega_cellwise.reshape(1, LANES, CZ)),
        in_hbm(subdomain_inverse_main[0, 0, 0]),
        in_hbm(warming_amount[0, 0, 0]),
        in_hbm(heat_spreading_coef[0, 0, 0]),
        in_hbm(solver),
    )
    x_ghosts, drive, conduct, diagonal, slab, solver = lax.optimization_barrier(
        (x_ghosts, drive, conduct, diagonal, slab, solver)
    )

    def chosen(kernel, rows, *inputs):
        small = inputs[1].ndim == 1
        return pl.pallas_call(
            kernel,
            out_shape=(shape(rows, LANES),) * 2,
            in_specs=[SMEM] * (1 + small) + [VMEM] * (len(inputs) - 1 - small),
            out_specs=[VMEM] * 2,
            compiler_params=params(),
            name=kernel.__name__,
        )(*inputs)

    def halo(field, x_plus, x_minus, source):
        message = shape(HALF, LANES)
        down, up = pl.pallas_call(
            pack_y,
            out_shape=(message, message),
            in_specs=[SMEM] + [VMEM] * 3,
            out_specs=[VMEM] * 2,
            compiler_params=params(),
            cost_estimate=cost(1 << 20, field_bytes),
            name="pack_y",
        )(place, field, x_plus, x_minus)
        y_plus, y_minus = turn(down, "gy", -1), turn(up, "gy", 1)
        planes = []
        if source:
            _, source = lax.optimization_barrier(((down, up), source))
            slab_up, slab_down = chosen(choose_far, 128, place, *source)
            planes = [ring(slab_up, 2), ring(slab_down, -2)]
        ghosts = (x_plus, x_minus, y_plus, y_minus)
        specs = []
        for block, half_block in ((0, 0), (CZ // 8 - 1, HALF // 8 - 1)):
            specs.append(pl.BlockSpec((6, 8, LANES), lambda i, block=block: (0, block, 0)))
            specs += [pl.BlockSpec((8, LANES), lambda i, block=block: (block, 0))] * 2
            specs += [pl.BlockSpec((8, LANES), lambda i, block=half_block: (block, 0))] * 2
        z_low, z_high = pl.pallas_call(
            pack_z,
            grid=(1,),
            out_shape=(shape(16, LANES), shape(16, LANES)),
            in_specs=[SMEM] + specs,
            out_specs=[pl.BlockSpec((16, LANES), lambda i: (0, 0))] * 2,
            compiler_params=params(),
            name="pack_z",
        )(place, field, *ghosts, field, *ghosts)
        z_plus, z_minus = turn(z_low, "gz", -1), turn(z_high, "gz", 1)
        if source:
            (z_plus, z_minus), planes = lax.optimization_barrier(((z_plus, z_minus), planes))
        return ghosts + (z_plus, z_minus), planes

    up, down = chosen(choose_near, 64 * RING + 8, place, lookup, slab)
    received = [ring(up, 1), ring(down, -1)]
    for sweep_index in range(SWEEPS):
        final = sweep_index == SWEEPS - 1
        if final:
            up, down = chosen(choose_next, 64 * (RING - 1) + 8, place, *received)
            received += [ring(up, 1), ring(down, -1)]
            x_ghosts, _, _ = lax.optimization_barrier((x_ghosts, up, down))
        ghosts, planes = halo(field, *x_ghosts, received if final else [])
        received += planes
        scratch = [
            pltpu.VMEM((10, CZ + 2 * HALO, LANES), F32),
            pltpu.VMEM(((CZ + 1 + WINDOW) * PLANE + 8, LANES), F32),
            pltpu.VMEM(((CZ + MAXSEG) * PLANE, LANES), F32),
        ]
        inputs = [place, seg_len, field, drive, conduct, *ghosts, diagonal, solver]
        specs = [SMEM] * 2 + [VMEM] * 11
        if final:
            outs = (shape(6, CZ, LANES), plane_array)
        else:
            outs = (shape(6, CZ, LANES), plane_array, plane_array)
        result = pl.pallas_call(
            functools.partial(sweep, final),
            out_shape=outs,
            in_specs=specs,
            out_specs=[VMEM] * len(outs),
            scratch_shapes=scratch,
            compiler_params=params(),
            cost_estimate=cost(1 << 28, 4 * field_bytes),
            name="sweep",
        )(*inputs)
        if final:
            field, heat = result
        else:
            field, face_low, face_high = result
            x_ghosts = turn(face_low, "gx", -1), turn(face_high, "gx", 1)

    field_new = pl.pallas_call(
        finish_field,
        out_shape=shape(6, LANES, CZ),
        in_specs=[VMEM],
        out_specs=VMEM,
        compiler_params=params(),
        cost_estimate=cost(1 << 20, 2 * field_bytes),
        name="finish_field",
    )(field)
    heat_above, heat_below = turn(heat[:8], "gz", -1), turn(heat[CZ - 8 :], "gz", 1)
    heat_above, heat_below, field_new = lax.optimization_barrier(
        (heat_above, heat_below, field_new)
    )
    rows = slab_cap + 8
    outgoing = pl.pallas_call(
        pack_heat,
        out_shape=shape(owners, rows, LANES),
        in_specs=[SMEM] * 2 + [VMEM] * 3,
        out_specs=VMEM,
        scratch_shapes=[pltpu.VMEM((CZ + 16 + rows, LANES), F32)],
        compiler_params=params(),
        name="pack_heat",
    )(place, lookup, heat, heat_below, heat_above)
    arrived = lax.all_to_all(outgoing, ("gx", "gy"), split_axis=0, concat_axis=0, tiled=True)
    planes = slab_cap + 2 * RING
    factor, warm = pl.pallas_call(
        heat_step,
        out_shape=(shape(owners, slab_cap, LANES), shape(slab_cap, 4, 8, LANES)),
        in_specs=[SMEM] * 2 + [VMEM] * 8,
        out_specs=[VMEM] * 2,
        scratch_shapes=[
            pltpu.VMEM((2, planes, 4, 8, LANES), F32),
            pltpu.VMEM((planes, 4, 8, LANES), F32),
            pltpu.VMEM(((1 + rows) * owners, LANES), F32),
        ],
        compiler_params=params(),
        name="heat_step",
    )(place, lookup, slab, *received, arrived)
    returned = lax.all_to_all(factor, ("gx", "gy"), split_axis=0, concat_axis=0, tiled=True)
    renewed_heat_rise = pl.pallas_call(
        finish_slab,
        out_shape=shape(slab_cap, 32, LANES),
        in_specs=[SMEM, SMEM, VMEM],
        out_specs=VMEM,
        compiler_params=params(),
        name="finish_slab",
    )(place, lookup, warm)
    renewed_sigma_omega = pl.pallas_call(
        finish_conduct,
        out_shape=shape(LANES, CZ),
        in_specs=[SMEM] + [VMEM] * 2,
        out_specs=VMEM,
        scratch_shapes=[pltpu.VMEM((CZ + slab_cap, LANES), F32)],
        compiler_params=params(),
        name="finish_conduct",
    )(lookup, returned, sigma_omega_cellwise.reshape(LANES, CZ))
    return (
        field_new.reshape(6, CX, CY, CZ),
        renewed_heat_rise[None, None, None],
        renewed_sigma_omega.reshape(CX, CY, CZ),
    )


def solution(mesh):
    return jax.shard_map(
        body,
        mesh=mesh,
        in_specs=(
            P(None, "gx", "gy", "gz"),
            P(None, "gx", "gy", "gz"),
            P("gx", "gy", "gz"),
            P("gx", "gy", "gz", None, None, None),
            P("gx", "gy", "gz", None, None),
            P("gx", "gy", "gz", None),
            P("gz", None),
            P("gx", "gy", "gz", None, None, None),
            P("gx", "gy", "gz", None, None, None),
        ),
        out_specs=(
            P(None, "gx", "gy", "gz"),
            P("gx", "gy", "gz", None, None, None),
            P("gx", "gy", "gz"),
        ),
        check_vma=False,
    )
```

```python
import functools

import jax
import jax.numpy as jnp
from jax import lax
from jax.experimental import pallas as pl
from jax.experimental.pallas import tpu as pltpu
from jax.sharding import PartitionSpec as P

SWEEPS = 2
SECTIONS = 4

mass_shift = 1.0
solver_scale = 0.2
coupling_scale = 0.05
time_step = 2.5
heat_drop = 0.15

CX, CY, CZ = 8, 16, 256
LANES = CX * CY
PLANE = 24
WINDOW = 21
MAXSEG = 19
F32 = jnp.float32
HALO = 8
CHUNK = 128
XP_PLUS, XP_MINUS = 6, 7
X_BITS, Y_BITS = 112, 15
RING = SECTIONS
HALF = CZ // 2
N_X, N_Y, N_Z = 4, 8, 8
OWNERS = N_X * N_Y
CORNER = (0, 1, 16, 17)
VMEM = pl.BlockSpec(memory_space=pltpu.VMEM)
SMEM = pl.BlockSpec(memory_space=pltpu.SMEM)
HBM = pl.BlockSpec(memory_space=pltpu.HBM)


def params(mib=24):
    return pltpu.CompilerParams(vmem_limit_bytes=mib << 20)


def cost(flops, moved):
    return pl.CostEstimate(flops=flops, bytes_accessed=moved, transcendentals=0)


def lane_of(value):
    return lax.broadcasted_iota(jnp.int32, value.shape, value.ndim - 1)


def ahead(value, by):
    shift = (-by) % LANES
    return value if shift == 0 else pltpu.roll(value, shift, value.ndim - 1)


def x_slot(slot):
    return 16 * slot


def y_slot(slot):
    return slot


def x_next(value, halo, slot):
    lane = lane_of(value)
    return jnp.where(lane & X_BITS == X_BITS, ahead(halo, x_slot(slot) - X_BITS), ahead(value, 16))


def x_before(value, halo, slot):
    lane = lane_of(value)
    return jnp.where(lane & X_BITS == 0, ahead(halo, x_slot(slot)), ahead(value, -16))


def y_next(value, halo, slot):
    lane = lane_of(value)
    return jnp.where(lane & Y_BITS == Y_BITS, ahead(halo, y_slot(slot) - Y_BITS), ahead(value, 1))


def y_before(value, halo, slot):
    lane = lane_of(value)
    return jnp.where(lane & Y_BITS == 0, ahead(halo, y_slot(slot)), ahead(value, -1))


def x_faces(parts):
    lane = lane_of(parts[0])
    own = lane & X_BITS
    first = jnp.zeros_like(parts[0])
    last = first
    for slot, part in enumerate(parts):
        mine = own == x_slot(slot)
        first = jnp.where(mine, ahead(part, -x_slot(slot)), first)
        last = jnp.where(mine, ahead(part, X_BITS - x_slot(slot)), last)
    return first, last


def y_faces(parts):
    lane = lane_of(parts[0])
    own = lane & Y_BITS
    first = jnp.zeros_like(parts[0])
    last = first
    for slot, part in enumerate(parts):
        mine = own == y_slot(slot)
        first = jnp.where(mine, ahead(part, -y_slot(slot)), first)
        last = jnp.where(mine, ahead(part, Y_BITS - y_slot(slot)), last)
    return first, last


def sides(place):
    x, y, z = place[0], place[1], place[2]
    return x > 0, x < N_X - 1, y > 0, y < N_Y - 1, z > 0, z < N_Z - 1


def own_slab(place):
    owner = place[0] * N_Y + place[1]
    slab = place[2] * OWNERS + owner
    last = OWNERS * N_Z - 1
    return owner, (slab > 0, slab < last, slab > 1, slab < last - 1)


def kept(flag, value):
    return jnp.where(flag, value, jnp.zeros_like(value))


def to_planes(source, index, target):
    for half in range(CZ // LANES):
        lanes = slice(half * LANES, (half + 1) * LANES)
        target[index, lanes, :] = source[index, :, lanes].T


def prepare_field(field, planes, first, last, loaded, sems):
    copies = [pltpu.make_async_copy(field.at[c], loaded.at[c], sems.at[c]) for c in range(6)]
    for copy in copies:
        copy.start()
    for comp in range(6):
        copies[comp].wait()
        to_planes(loaded, comp, planes)

    def chunk(i, carry):
        rows = pl.ds(pl.multiple_of(i * CHUNK, CHUNK), CHUNK)
        low, high = x_faces([planes[comp, rows, :] for comp in range(6)])
        first[rows, :] = low
        last[rows, :] = high
        return carry

    lax.fori_loop(0, CZ // CHUNK, chunk, 0)


def prepare_rest(
    drive, conduct, diagonal, warm, rates, solver,
    drive_planes, conduct_planes, diagonal_turned, slab, solver_here,
    drive_in, conduct_in, diagonal_in, slab_in, sems,
):
    copies = [pltpu.make_async_copy(warm, slab_in.at[0], sems.at[0])]
    copies.append(pltpu.make_async_copy(rates, slab_in.at[1], sems.at[1]))
    copies.append(pltpu.make_async_copy(drive, drive_in, sems.at[2]))
    copies.append(pltpu.make_async_copy(conduct, conduct_in, sems.at[3]))
    copies.append(pltpu.make_async_copy(diagonal, diagonal_in, sems.at[4]))
    parts = 4
    size = solver.shape[0] // parts
    for part in range(parts):
        at = pl.ds(part * size, size)
        copies.append(pltpu.make_async_copy(solver.at[at], solver_here.at[at], sems.at[5 + part]))
    for copy in copies:
        copy.start()
    batch = 4
    for which in range(2):
        copies[which].wait()
        for base in range(0, slab.shape[0], batch):
            value = slab_in[which, base : base + batch].reshape(4 * batch, 8, LANES)
            slab[base : base + batch, which] = swap_tiles(value).reshape(batch, 4, 8, LANES)
    for copy in copies[2:5]:
        copy.wait()
    for comp in range(6):
        to_planes(drive_in, comp, drive_planes)
    to_planes(conduct_in, 0, conduct_planes)
    diagonal_turned[...] = diagonal_in[...].T
    for copy in copies[5:]:
        copy.wait()


def pack_y(place, field, x_plus, x_minus, down, up):
    flags = sides(place)

    def chunk(i, carry):
        parts = []
        for base in (0, HALF):
            rows = pl.ds(pl.multiple_of(base + i * CHUNK, CHUNK), CHUNK)
            parts += [field[comp, rows, :] for comp in range(6)]
            parts += [kept(flags[1], x_plus[rows, :]), kept(flags[0], x_minus[rows, :])]
        low, high = y_faces(parts)
        rows = pl.ds(pl.multiple_of(i * CHUNK, CHUNK), CHUNK)
        down[rows, :] = low
        up[rows, :] = high
        return carry

    lax.fori_loop(0, HALF // CHUNK, chunk, 0)


def choose_near(place, lookup, slab, up, down):
    count = lookup[own_slab(place)[0]]
    for depth in range(RING):
        at = slice(64 * depth, 64 * (depth + 1))
        up[at, :] = slab[jnp.maximum(count - 1 - depth, 0)].reshape(64, LANES)
        down[at, :] = slab[depth].reshape(64, LANES)
    count = jnp.full((8, LANES), count, jnp.int32).astype(F32)
    up[-8:, :] = count
    down[-8:, :] = count


def choose_next(place, below, above, up, down):
    near = own_slab(place)[1]
    size = 64 * (RING - 1)
    up[:size, :] = kept(near[0], below[:size, :])
    down[:size, :] = kept(near[1], above[:size, :])
    up[-8:, :] = below[-8:, :]
    down[-8:, :] = above[-8:, :]


def planes_of(message, count, flag):
    return [
        kept(flag, message[64 * d : 64 * (d + 1), :]).reshape(8, 8, LANES)
        for d in range(count)
    ]


def choose_far(place, below1, above1, below2, above2, up, down):
    near = own_slab(place)[1]
    for one, two, out, flag in ((below1, below2, up, near[0]), (above1, above2, down, near[1])):
        first = planes_of(one, 2, flag)
        second = planes_of(two, 1, flag)
        out[0:64, :] = first[0].reshape(64, LANES)
        out[64:128, :] = jnp.where(one[-8:, :] > 1.5, first[1], second[0]).reshape(64, LANES)


def beyond(one, two, three, near, far):
    a, b, c = planes_of(one, 4, near), planes_of(two, 3, near), planes_of(three, 2, far)
    first, second = one[-8:, :], two[-8:, :]
    two_left = jnp.where(second > 1.5, b[1], c[0])
    three_left = jnp.where(second > 2.5, b[2], jnp.where(second > 1.5, c[0], c[1]))
    return (
        a[0],
        jnp.where(first > 1.5, a[1], b[0]),
        jnp.where(first > 2.5, a[2], jnp.where(first > 1.5, b[0], two_left)),
        jnp.where(
            first > 3.5,
            a[3],
            jnp.where(first > 2.5, b[0], jnp.where(first > 1.5, two_left, three_left)),
        ),
    )


def y_rows(message, row, count, upper):
    value = message[row : row + count, :]
    return ahead(value, 8) if upper else value


def pack_z(place, *refs):
    flags = sides(place)
    lows, highs, (first, last) = refs[:5], refs[5:10], refs[10:]
    for (field, xp, xm, yp, ym), row, out in ((lows, 0, first), (highs, 7, last)):
        for comp in range(6):
            out[comp : comp + 1, :] = field[comp, row : row + 1, :]
        out[6:7, :] = kept(flags[1], xp[row : row + 1, :])
        out[7:8, :] = kept(flags[0], xm[row : row + 1, :])
        out[8:9, :] = kept(flags[3], y_rows(yp, row, 1, row > 0))
        out[9:10, :] = kept(flags[2], y_rows(ym, row, 1, row > 0))
        out[10:16, :] = jnp.zeros((6, LANES), F32)


def curl_chunk(wide, part):
    ex, ey, ez = wide[3 * part], wide[3 * part + 1], wide[3 * part + 2]
    xp, xm, yp, ym = wide[6], wide[7], wide[8], wide[9]
    sx, sy, sz = 3 * part, 3 * part + 1, 3 * part + 2

    def here(v):
        return v[8 : 8 + CHUNK]

    def up(v):
        return v[9 : 9 + CHUNK]

    def down(v):
        return v[7 : 7 + CHUNK]

    upper = [v[8:] for v in (ex, ey, xm, ym)]
    ex_xm = x_before(upper[0], upper[2], sx)
    ey_ym = y_before(upper[1], upper[3], sy)
    ex_xm_up, ex_xm = ex_xm[1 : 1 + CHUNK], ex_xm[:CHUNK]
    ey_ym_up, ey_ym = ey_ym[1 : 1 + CHUNK], ey_ym[:CHUNK]
    lower = [v[: 8 + CHUNK] for v in (ez, xp, yp)]
    ez_xp = x_next(lower[0], lower[1], sz)
    ez_yp = y_next(lower[0], lower[2], sz)
    ez_xp_down, ez_xp = down(ez_xp), ez_xp[8:]
    ez_yp_down, ez_yp = down(ez_yp), ez_yp[8:]
    xp0, xm0, yp0, ym0 = here(xp), here(xm), here(yp), here(ym)
    ex0, ey0, ez0 = here(ex), here(ey), here(ez)
    ex_yp = y_next(ex0, yp0, sx)
    ex_ym = y_before(ex0, ym0, sx)
    ex_xm_yp = x_before(ex_yp, y_next(xm0, yp0, XP_MINUS), sx)
    ey_xp = x_next(ey0, xp0, sy)
    ey_xm = x_before(ey0, xm0, sy)
    ey_xp_ym = x_next(ey_ym, y_before(xp0, ym0, XP_PLUS), sy)
    ez_xm = x_before(ez0, xm0, sz)
    ez_ym = y_before(ez0, ym0, sz)
    kx = 4.0 * ex0 - ex_yp - ex_ym - up(ex) - down(ex)
    kx = kx + (ey_xp - ey0 - ey_xp_ym + ey_ym) + (ez_xp - ez0 - ez_xp_down + down(ez))
    ky = 4.0 * ey0 - ey_xp - ey_xm - up(ey) - down(ey)
    ky = ky + (ex_yp - ex0 - ex_xm_yp + ex_xm) + (ez_yp - ez0 - ez_yp_down + down(ez))
    kz = 4.0 * ez0 - ez_xp - ez_xm - ez_yp - ez_ym
    kz = kz + (up(ex) - ex0 - ex_xm_up + ex_xm) + (up(ey) - ey0 - ey_ym_up + ey_ym)
    return (kx, ky, kz), (ex0, ey0, ez0)


def sweep(last_sweep, place, seg_len, field, drive, conduct, xp, xm, yp, ym, zp, zm, diagonal, solver, *rest):
    if last_sweep:
        field_out, heat_out, ext, columns, solved = rest
    else:
        field_out, first, last, ext, columns, solved = rest
    segs = solver.shape[0]
    flags = sides(place)

    for base in range(0, CZ, CHUNK):
        rows = slice(base, base + CHUNK)
        to = slice(base + HALO, base + HALO + CHUNK)
        for comp in range(6):
            ext[comp, to, :] = field[comp, rows, :]
        ext[6, to, :] = kept(flags[1], xp[rows, :])
        ext[7, to, :] = kept(flags[0], xm[rows, :])
        ext[8, to, :] = kept(flags[3], y_rows(yp, base % HALF, CHUNK, base >= HALF))
        ext[9, to, :] = kept(flags[2], y_rows(ym, base % HALF, CHUNK, base >= HALF))
    for comp in range(10):
        ext[comp, HALO - 1 : HALO, :] = kept(flags[4], zm[comp : comp + 1, :])
        ext[comp, HALO + CZ : HALO + CZ + 1, :] = kept(flags[5], zp[comp : comp + 1, :])

    columns[0:PLANE, :] = jnp.zeros((PLANE, LANES), F32)
    tail = columns.shape[0] - (CZ + 1) * PLANE
    columns[(CZ + 1) * PLANE :, :] = jnp.zeros((tail, LANES), F32)

    def residual(i, carry):
        base = pl.multiple_of(i * CHUNK, CHUNK)
        rows = pl.ds(base, CHUNK)
        wide = [ext[comp, pl.ds(base, CHUNK + 2 * HALO), :] for comp in range(10)]
        curl_real, real = curl_chunk(wide, 0)
        curl_imag, imag = curl_chunk(wide, 1)
        sigma = conduct[0, rows, :]
        for axis in range(3):
            both = (
                curl_real[axis] + mass_shift * real[axis] - sigma * imag[axis],
                curl_imag[axis] + mass_shift * imag[axis] + sigma * real[axis],
            )
            for part in range(2):
                comp = 3 * part + axis
                rest_of = drive[comp, rows, :] - both[part]
                for q in range(4):
                    at = (base + 1) * PLANE + comp * 4 + q
                    columns[pl.ds(at, CHUNK, stride=PLANE), :] = ahead(rest_of, CORNER[q])
        return carry

    lax.fori_loop(0, CZ // CHUNK, residual, 0, unroll=True)

    row_of = lax.broadcasted_iota(jnp.int32, (512, LANES), 0)
    start = jnp.int32(0)
    for s in range(segs):
        length = seg_len[s]
        window = columns[pl.ds(pl.multiple_of(start * PLANE, 8), 512), :]
        window = jnp.where(row_of < (length + 2) * PLANE, window, 0.0).astype(jnp.bfloat16)
        product = jnp.dot(solver[s], window, preferred_element_type=F32)
        scaled = solver_scale * diagonal[:, s : s + 1] * window.astype(F32)
        result = coupling_scale * product + scaled
        to = pl.ds(pl.multiple_of(start * PLANE, 8), MAXSEG * PLANE)
        solved[to, :] = result[PLANE : (MAXSEG + 1) * PLANE, :]
        start = start + length

    def update(i, carry):
        base = pl.multiple_of(i * CHUNK, CHUNK)
        rows = pl.ds(base, CHUNK)
        lane = lax.broadcasted_iota(jnp.int32, (CHUNK, LANES), 1)
        parts = []
        for comp in range(6):
            add = jnp.zeros((CHUNK, LANES), F32)
            for q in range(4):
                piece = solved[pl.ds(base * PLANE + comp * 4 + q, CHUNK, stride=PLANE), :]
                add = jnp.where(lane & 17 == CORNER[q], ahead(piece, -CORNER[q]), add)
            part = field[comp, rows, :] + add
            field_out[comp, rows, :] = part
            parts.append(part)
        if last_sweep:
            total = parts[0] * parts[0]
            for part in parts[1:]:
                total = total + part * part
            heat_out[rows, :] = 0.5 * conduct[0, rows, :] * total
        else:
            low, high = x_faces(parts)
            first[rows, :] = low
            last[rows, :] = high
        return carry

    lax.fori_loop(0, CZ // CHUNK, update, 0, unroll=True)


def finish_field(planes, out):
    for comp in range(6):
        for half in range(CZ // LANES):
            lanes = slice(half * LANES, (half + 1) * LANES)
            out[comp, :, lanes] = planes[comp, lanes, :].T


def pack_heat(place, lookup, heat, below, above, out, ext):
    flags = sides(place)
    ext[0:8, :] = kept(flags[4], below[...])
    ext[8 : 8 + CZ, :] = heat[...]
    ext[8 + CZ : 16 + CZ, :] = kept(flags[5], above[...])
    ext[16 + CZ :, :] = jnp.zeros((ext.shape[0] - 16 - CZ, LANES), F32)
    start = 8 - (RING - 1)
    for owner in range(out.shape[0]):
        out[owner] = ext[pl.ds(start, out.shape[1]), :]
        start = start + lookup[owner]


def swap_tiles(value):
    row = lax.broadcasted_iota(jnp.int32, value.shape, value.ndim - 2)
    lane = lane_of(value)
    axis = value.ndim - 2
    for k in range(3):
        step = 1 << k
        row_bit = (row >> k) & 1
        lane_bit = (lane >> (4 + k)) & 1
        up = ahead(pltpu.roll(value, 8 - step, axis), -16 * step)
        down = up if step == 4 else ahead(pltpu.roll(value, step, axis), 16 * step)
        value = jnp.where(row_bit == lane_bit, value, jnp.where(row_bit == 0, up, down))
    return value


def heat_step(place, lookup, slab, below1, above1, below2, above2, below3, above3, arrived, factor_out, warm_out, temp, rates, joule):
    owner, near = own_slab(place)
    count = lookup[owner]
    planes = temp.shape[1]
    owners = arrived.shape[0]
    for plane in range(planes - 2 * RING):
        temp[0, plane + RING] = slab[plane, 0]
        rates[plane + RING] = slab[plane, 1]
    lower = beyond(below1, below2, below3, near[0], near[2])
    upper = beyond(above1, above2, above3, near[1], near[3])
    for depth in range(RING):
        for at, plane in ((RING - 1 - depth, lower[depth]), (RING + count + depth, upper[depth])):
            temp[0, at] = plane[:4]
            rates[at] = plane[4:]
    for owner in range(owners):
        joule[pl.ds(owners + owner, arrived.shape[1], stride=owners), :] = arrived[owner]

    group = 2
    section = time_step / (SECTIONS * SECTIONS)

    def one(step, now, before, base):
        value = temp[now, pl.ds(base - 1, group + 2)]
        mid = value[1:-1]
        lane = lane_of(mid)
        row = lax.broadcasted_iota(jnp.int32, mid.shape, 2)
        none = jnp.zeros_like(mid[:, :1])
        gx_up = jnp.concatenate([mid[:, 1:], none], axis=1)
        gx_down = jnp.concatenate([none, mid[:, :-1]], axis=1)
        gy_up = jnp.where(row == 7, 0.0, pltpu.roll(mid, 7, 2))
        gy_down = jnp.where(row == 0, 0.0, pltpu.roll(mid, 1, 2))
        total = ahead(jnp.where(lane < 16, gx_up, mid), 16)
        total = total + ahead(jnp.where(lane >= 112, gx_down, mid), -16)
        total = total + jnp.where(lane & 15 == 15, ahead(gy_up, -15), ahead(mid, 1))
        total = total + jnp.where(lane & 15 == 0, ahead(gy_down, 15), ahead(mid, -1))
        total = total + value[:-2] + value[2:]
        heat = joule[pl.ds(base * owners, group * owners), :].reshape(group, 4, 8, LANES)
        rate = rates[pl.ds(base, group)] * (total - 6.0 * mid) + heat
        if step == 1:
            temp[before, pl.ds(base, group)] = mid + section * rate
        else:
            old = temp[before, pl.ds(base, group)]
            temp[before, pl.ds(base, group)] = 2.0 * mid - old + 2.0 * section * rate

    for step in range(1, SECTIONS + 1):
        now, before = (step - 1) % 2, step % 2

        for base in range(step, planes - step, group):
            one(step, now, before, base)
    final = SECTIONS % 2
    for plane in range(warm_out.shape[0]):
        result = temp[final, plane + RING]
        warm_out[plane] = result
        joule[plane * owners : (plane + 1) * owners, :] = jnp.exp(-heat_drop * result).reshape(owners, LANES)
    for owner in range(owners):
        factor_out[owner] = joule[pl.ds(owner, factor_out.shape[1], stride=owners), :]


def finish_slab(place, lookup, warm, out):
    count = lookup[own_slab(place)[0]]
    batch = 4
    for base in range(0, out.shape[0], batch):
        value = swap_tiles(warm[base : base + batch].reshape(4 * batch, 8, LANES))
        value = value.reshape(batch, 32, LANES)
        for plane in range(batch):
            out[base + plane] = kept(count > base + plane, value[plane])


def finish_conduct(lookup, returned, conduct, out, rows):
    start = 0
    for owner in range(returned.shape[0]):
        rows[pl.ds(start, returned.shape[1]), :] = returned[owner]
        start = start + lookup[owner]
    for half in range(CZ // LANES):
        lanes = slice(half * LANES, (half + 1) * LANES)
        out[:, lanes] = conduct[:, lanes] * rows[half * LANES : (half + 1) * LANES, :].T


def in_hbm(value):
    return pltpu.with_memory_space_constraint(value, pltpu.HBM)


def shape(*dims):
    return jax.ShapeDtypeStruct(dims, F32)


def body(
    earlier_edge_voltage,
    coil_drive_current,
    sigma_omega_cellwise,
    subdomain_inverse_full,
    subdomain_inverse_main,
    subdomain_layer_counts,
    heat_layer_lookup,
    warming_amount,
    heat_spreading_coef,
):
    count_x, count_y, count_z = (lax.axis_size(axis) for axis in ("gx", "gy", "gz"))
    owners = count_x * count_y
    segs = subdomain_layer_counts.shape[3]
    slab_cap = warming_amount.shape[3]

    def turn(value, axis, step):
        count = lax.axis_size(axis)
        return lax.ppermute(value, axis, [(i, (i + step) % count) for i in range(count)])

    def device(slab):
        return (slab % owners) * count_z + slab // owners

    def ring(value, step):
        total = owners * count_z
        pairs = [(device(i), device((i + step) % total)) for i in range(total)]
        return lax.ppermute(value, ("gx", "gy", "gz"), pairs)

    place = jnp.stack([lax.axis_index(axis) for axis in ("gx", "gy", "gz")]).astype(jnp.int32)
    seg_len = subdomain_layer_counts[0, 0, 0]
    lookup = heat_layer_lookup[0]

    field_bytes = 6 * CZ * LANES * 4
    plane_array = shape(CZ, LANES)
    field, face_low, face_high = pl.pallas_call(
        prepare_field,
        out_shape=(shape(6, CZ, LANES), plane_array, plane_array),
        in_specs=[HBM],
        out_specs=[VMEM] * 3,
        scratch_shapes=[pltpu.VMEM((6, LANES, CZ), F32), pltpu.SemaphoreType.DMA((6,))],
        compiler_params=params(),
        cost_estimate=cost(1 << 20, 2 * field_bytes),
        name="prepare_field",
    )(in_hbm(earlier_edge_voltage.reshape(6, LANES, CZ)))
    x_ghosts = turn(face_low, "gx", -1), turn(face_high, "gx", 1)
    solver = subdomain_inverse_full[0, 0, 0]
    drive, conduct, diagonal, slab, solver = pl.pallas_call(
        prepare_rest,
        out_shape=(
            shape(6, CZ, LANES),
            shape(1, CZ, LANES),
            shape(512, segs),
            shape(slab_cap, 2, 4, 8, LANES),
            jax.ShapeDtypeStruct(solver.shape, solver.dtype),
        ),
        in_specs=[HBM] * 6,
        out_specs=[VMEM] * 5,
        scratch_shapes=[
            pltpu.VMEM((6, LANES, CZ), F32),
            pltpu.VMEM((1, LANES, CZ), F32),
            pltpu.VMEM((segs, 512), F32),
            pltpu.VMEM((2, slab_cap, 32, LANES), F32),
            pltpu.SemaphoreType.DMA((9,)),
        ],
        compiler_params=params(),
        cost_estimate=cost(1 << 20, 16 * field_bytes),
        name="prepare_rest",
    )(
        in_hbm(coil_drive_current.reshape(6, LANES, CZ)),
        in_hbm(sigma_omega_cellwise.reshape(1, LANES, CZ)),
        in_hbm(subdomain_inverse_main[0, 0, 0]),
        in_hbm(warming_amount[0, 0, 0]),
        in_hbm(heat_spreading_coef[0, 0, 0]),
        in_hbm(solver),
    )
    x_ghosts, drive, conduct, diagonal, slab, solver = lax.optimization_barrier(
        (x_ghosts, drive, conduct, diagonal, slab, solver)
    )

    def chosen(kernel, rows, *inputs):
        small = inputs[1].ndim == 1
        return pl.pallas_call(
            kernel,
            out_shape=(shape(rows, LANES),) * 2,
            in_specs=[SMEM] * (1 + small) + [VMEM] * (len(inputs) - 1 - small),
            out_specs=[VMEM] * 2,
            compiler_params=params(),
            name=kernel.__name__,
        )(*inputs)

    def halo(field, x_plus, x_minus, source):
        message = shape(HALF, LANES)
        down, up = pl.pallas_call(
            pack_y,
            out_shape=(message, message),
            in_specs=[SMEM] + [VMEM] * 3,
            out_specs=[VMEM] * 2,
            compiler_params=params(),
            cost_estimate=cost(1 << 20, field_bytes),
            name="pack_y",
        )(place, field, x_plus, x_minus)
        y_plus, y_minus = turn(down, "gy", -1), turn(up, "gy", 1)
        planes = []
        if source:
            _, source = lax.optimization_barrier(((down, up), source))
            slab_up, slab_down = chosen(choose_far, 128, place, *source)
            planes = [ring(slab_up, 2), ring(slab_down, -2)]
        ghosts = (x_plus, x_minus, y_plus, y_minus)
        specs = []
        for block, half_block in ((0, 0), (CZ // 8 - 1, HALF // 8 - 1)):
            specs.append(pl.BlockSpec((6, 8, LANES), lambda i, block=block: (0, block, 0)))
            specs += [pl.BlockSpec((8, LANES), lambda i, block=block: (block, 0))] * 2
            specs += [pl.BlockSpec((8, LANES), lambda i, block=half_block: (block, 0))] * 2
        z_low, z_high = pl.pallas_call(
            pack_z,
            grid=(1,),
            out_shape=(shape(16, LANES), shape(16, LANES)),
            in_specs=[SMEM] + specs,
            out_specs=[pl.BlockSpec((16, LANES), lambda i: (0, 0))] * 2,
            compiler_params=params(),
            name="pack_z",
        )(place, field, *ghosts, field, *ghosts)
        z_plus, z_minus = turn(z_low, "gz", -1), turn(z_high, "gz", 1)
        if source:
            (z_plus, z_minus), planes = lax.optimization_barrier(((z_plus, z_minus), planes))
        return ghosts + (z_plus, z_minus), planes

    up, down = chosen(choose_near, 64 * RING + 8, place, lookup, slab)
    received = [ring(up, 1), ring(down, -1)]
    for sweep_index in range(SWEEPS):
        final = sweep_index == SWEEPS - 1
        if final:
            up, down = chosen(choose_next, 64 * (RING - 1) + 8, place, *received)
            received += [ring(up, 1), ring(down, -1)]
            x_ghosts, _, _ = lax.optimization_barrier((x_ghosts, up, down))
        ghosts, planes = halo(field, *x_ghosts, received if final else [])
        received += planes
        scratch = [
            pltpu.VMEM((10, CZ + 2 * HALO, LANES), F32),
            pltpu.VMEM(((CZ + 1 + WINDOW) * PLANE + 8, LANES), F32),
            pltpu.VMEM(((CZ + MAXSEG) * PLANE, LANES), F32),
        ]
        inputs = [place, seg_len, field, drive, conduct, *ghosts, diagonal, solver]
        specs = [SMEM] * 2 + [VMEM] * 11
        if final:
            outs = (shape(6, CZ, LANES), plane_array)
        else:
            outs = (shape(6, CZ, LANES), plane_array, plane_array)
        result = pl.pallas_call(
            functools.partial(sweep, final),
            out_shape=outs,
            in_specs=specs,
            out_specs=[VMEM] * len(outs),
            scratch_shapes=scratch,
            compiler_params=params(),
            cost_estimate=cost(1 << 28, 4 * field_bytes),
            name="sweep",
        )(*inputs)
        if final:
            field, heat = result
        else:
            field, face_low, face_high = result
            x_ghosts = turn(face_low, "gx", -1), turn(face_high, "gx", 1)

    field_new = pl.pallas_call(
        finish_field,
        out_shape=shape(6, LANES, CZ),
        in_specs=[VMEM],
        out_specs=VMEM,
        compiler_params=params(),
        cost_estimate=cost(1 << 20, 2 * field_bytes),
        name="finish_field",
    )(field)
    heat_above, heat_below = turn(heat[:8], "gz", -1), turn(heat[CZ - 8 :], "gz", 1)
    heat_above, heat_below, field_new = lax.optimization_barrier(
        (heat_above, heat_below, field_new)
    )
    rows = slab_cap + 8
    outgoing = pl.pallas_call(
        pack_heat,
        out_shape=shape(owners, rows, LANES),
        in_specs=[SMEM] * 2 + [VMEM] * 3,
        out_specs=VMEM,
        scratch_shapes=[pltpu.VMEM((CZ + 16 + rows, LANES), F32)],
        compiler_params=params(),
        name="pack_heat",
    )(place, lookup, heat, heat_below, heat_above)
    arrived = lax.all_to_all(outgoing, ("gx", "gy"), split_axis=0, concat_axis=0, tiled=True)
    planes = slab_cap + 2 * RING
    factor, warm = pl.pallas_call(
        heat_step,
        out_shape=(shape(owners, slab_cap, LANES), shape(slab_cap, 4, 8, LANES)),
        in_specs=[SMEM] * 2 + [VMEM] * 8,
        out_specs=[VMEM] * 2,
        scratch_shapes=[
            pltpu.VMEM((2, planes, 4, 8, LANES), F32),
            pltpu.VMEM((planes, 4, 8, LANES), F32),
            pltpu.VMEM(((1 + rows) * owners, LANES), F32),
        ],
        compiler_params=params(),
        name="heat_step",
    )(place, lookup, slab, *received, arrived)
    returned = lax.all_to_all(factor, ("gx", "gy"), split_axis=0, concat_axis=0, tiled=True)
    renewed_heat_rise = pl.pallas_call(
        finish_slab,
        out_shape=shape(slab_cap, 32, LANES),
        in_specs=[SMEM, SMEM, VMEM],
        out_specs=VMEM,
        compiler_params=params(),
        name="finish_slab",
    )(place, lookup, warm)
    renewed_sigma_omega = pl.pallas_call(
        finish_conduct,
        out_shape=shape(LANES, CZ),
        in_specs=[SMEM] + [VMEM] * 2,
        out_specs=VMEM,
        scratch_shapes=[pltpu.VMEM((CZ + slab_cap, LANES), F32)],
        compiler_params=params(),
        name="finish_conduct",
    )(lookup, returned, sigma_omega_cellwise.reshape(LANES, CZ))
    return (
        field_new.reshape(6, CX, CY, CZ),
        renewed_heat_rise[None, None, None],
        renewed_sigma_omega.reshape(CX, CY, CZ),
    )


def solution(mesh):
    return jax.shard_map(
        body,
        mesh=mesh,
        in_specs=(
            P(None, "gx", "gy", "gz"),
            P(None, "gx", "gy", "gz"),
            P("gx", "gy", "gz"),
            P("gx", "gy", "gz", None, None, None),
            P("gx", "gy", "gz", None, None),
            P("gx", "gy", "gz", None),
            P("gz", None),
            P("gx", "gy", "gz", None, None, None),
            P("gx", "gy", "gz", None, None, None),
        ),
        out_specs=(
            P(None, "gx", "gy", "gz"),
            P("gx", "gy", "gz", None, None, None),
            P("gx", "gy", "gz"),
        ),
        check_vma=False,
    )
```

```python
import functools

import jax
import jax.numpy as jnp
from jax import lax
from jax.experimental import pallas as pl
from jax.experimental.pallas import tpu as pltpu
from jax.sharding import PartitionSpec as P

SWEEPS = 2
SECTIONS = 4

mass_shift = 1.0
solver_scale = 0.2
coupling_scale = 0.05
time_step = 2.5
heat_drop = 0.15

CX, CY, CZ = 8, 16, 256
LANES = CX * CY
PLANE = 24
WINDOW = 21
MAXSEG = 19
F32 = jnp.float32
HALO = 8
CHUNK = 128
XP_PLUS, XP_MINUS = 6, 7
X_BITS, Y_BITS = 112, 15
RING = SECTIONS
HALF = CZ // 2
N_X, N_Y, N_Z = 4, 8, 8
OWNERS = N_X * N_Y
CORNER = (0, 1, 16, 17)
VMEM = pl.BlockSpec(memory_space=pltpu.VMEM)
SMEM = pl.BlockSpec(memory_space=pltpu.SMEM)
HBM = pl.BlockSpec(memory_space=pltpu.HBM)


def params(mib=24):
    return pltpu.CompilerParams(vmem_limit_bytes=mib << 20)


def cost(flops, moved):
    return pl.CostEstimate(flops=flops, bytes_accessed=moved, transcendentals=0)


def lane_of(value):
    return lax.broadcasted_iota(jnp.int32, value.shape, value.ndim - 1)


def ahead(value, by):
    shift = (-by) % LANES
    return value if shift == 0 else pltpu.roll(value, shift, value.ndim - 1)


def x_slot(slot):
    return 16 * slot


def y_slot(slot):
    return slot


def x_next(value, halo, slot):
    lane = lane_of(value)
    return jnp.where(lane & X_BITS == X_BITS, ahead(halo, x_slot(slot) - X_BITS), ahead(value, 16))


def x_before(value, halo, slot):
    lane = lane_of(value)
    return jnp.where(lane & X_BITS == 0, ahead(halo, x_slot(slot)), ahead(value, -16))


def y_next(value, halo, slot):
    lane = lane_of(value)
    return jnp.where(lane & Y_BITS == Y_BITS, ahead(halo, y_slot(slot) - Y_BITS), ahead(value, 1))


def y_before(value, halo, slot):
    lane = lane_of(value)
    return jnp.where(lane & Y_BITS == 0, ahead(halo, y_slot(slot)), ahead(value, -1))


def x_faces(parts):
    lane = lane_of(parts[0])
    own = lane & X_BITS
    first = jnp.zeros_like(parts[0])
    last = first
    for slot, part in enumerate(parts):
        mine = own == x_slot(slot)
        first = jnp.where(mine, ahead(part, -x_slot(slot)), first)
        last = jnp.where(mine, ahead(part, X_BITS - x_slot(slot)), last)
    return first, last


def y_faces(parts):
    lane = lane_of(parts[0])
    own = lane & Y_BITS
    first = jnp.zeros_like(parts[0])
    last = first
    for slot, part in enumerate(parts):
        mine = own == y_slot(slot)
        first = jnp.where(mine, ahead(part, -y_slot(slot)), first)
        last = jnp.where(mine, ahead(part, Y_BITS - y_slot(slot)), last)
    return first, last


def sides(place):
    x, y, z = place[0], place[1], place[2]
    return x > 0, x < N_X - 1, y > 0, y < N_Y - 1, z > 0, z < N_Z - 1


def own_slab(place):
    owner = place[0] * N_Y + place[1]
    slab = place[2] * OWNERS + owner
    last = OWNERS * N_Z - 1
    return owner, (slab > 0, slab < last, slab > 1, slab < last - 1)


def kept(flag, value):
    return jnp.where(flag, value, jnp.zeros_like(value))


def to_planes(source, index, target):
    for half in range(CZ // LANES):
        lanes = slice(half * LANES, (half + 1) * LANES)
        target[index, lanes, :] = source[index, :, lanes].T


def prepare_field(field, planes, first, last, loaded, sems):
    copies = [pltpu.make_async_copy(field.at[c], loaded.at[c], sems.at[c]) for c in range(6)]
    for copy in copies:
        copy.start()
    for comp in range(6):
        copies[comp].wait()
        to_planes(loaded, comp, planes)

    def chunk(i, carry):
        rows = pl.ds(pl.multiple_of(i * CHUNK, CHUNK), CHUNK)
        low, high = x_faces([planes[comp, rows, :] for comp in range(6)])
        first[rows, :] = low
        last[rows, :] = high
        return carry

    lax.fori_loop(0, CZ // CHUNK, chunk, 0)


def prepare_rest(
    drive, conduct, diagonal, warm, rates, solver,
    drive_planes, conduct_planes, diagonal_spread, slab, solver_here,
    drive_in, conduct_in, diagonal_in, slab_in, sems,
):
    copies = [pltpu.make_async_copy(warm, slab_in.at[0], sems.at[0])]
    copies.append(pltpu.make_async_copy(rates, slab_in.at[1], sems.at[1]))
    copies.append(pltpu.make_async_copy(drive, drive_in, sems.at[2]))
    copies.append(pltpu.make_async_copy(conduct, conduct_in, sems.at[3]))
    copies.append(pltpu.make_async_copy(diagonal, diagonal_in, sems.at[4]))
    parts = 4
    size = solver.shape[0] // parts
    for part in range(parts):
        at = pl.ds(part * size, size)
        copies.append(pltpu.make_async_copy(solver.at[at], solver_here.at[at], sems.at[5 + part]))
    for copy in copies:
        copy.start()
    batch = 4
    for which in range(2):
        copies[which].wait()
        for base in range(0, slab.shape[0], batch):
            value = slab_in[which, base : base + batch].reshape(4 * batch, 8, LANES)
            slab[base : base + batch, which] = swap_tiles(value).reshape(batch, 4, 8, LANES)
    for copy in copies[2:5]:
        copy.wait()
    for comp in range(6):
        to_planes(drive_in, comp, drive_planes)
    to_planes(conduct_in, 0, conduct_planes)
    turned = solver_scale * diagonal_in[...].T
    for s in range(diagonal_spread.shape[0]):
        diagonal_spread[s] = jnp.broadcast_to(turned[:, s : s + 1], diagonal_spread.shape[1:])
    for copy in copies[5:]:
        copy.wait()


def pack_y(place, field, x_plus, x_minus, down, up):
    flags = sides(place)

    def chunk(i, carry):
        parts = []
        for base in (0, HALF):
            rows = pl.ds(pl.multiple_of(base + i * CHUNK, CHUNK), CHUNK)
            parts += [field[comp, rows, :] for comp in range(6)]
            parts += [kept(flags[1], x_plus[rows, :]), kept(flags[0], x_minus[rows, :])]
        low, high = y_faces(parts)
        rows = pl.ds(pl.multiple_of(i * CHUNK, CHUNK), CHUNK)
        down[rows, :] = low
        up[rows, :] = high
        return carry

    lax.fori_loop(0, HALF // CHUNK, chunk, 0)


def choose_near(place, lookup, slab, up, down):
    count = lookup[own_slab(place)[0]]
    for depth in range(RING):
        at = slice(64 * depth, 64 * (depth + 1))
        up[at, :] = slab[jnp.maximum(count - 1 - depth, 0)].reshape(64, LANES)
        down[at, :] = slab[depth].reshape(64, LANES)
    count = jnp.full((8, LANES), count, jnp.int32).astype(F32)
    up[-8:, :] = count
    down[-8:, :] = count


def choose_next(place, below, above, up, down):
    near = own_slab(place)[1]
    size = 64 * (RING - 1)
    up[:size, :] = kept(near[0], below[:size, :])
    down[:size, :] = kept(near[1], above[:size, :])
    up[-8:, :] = below[-8:, :]
    down[-8:, :] = above[-8:, :]


def planes_of(message, count, flag):
    return [
        kept(flag, message[64 * d : 64 * (d + 1), :]).reshape(8, 8, LANES)
        for d in range(count)
    ]


def choose_far(place, below1, above1, below2, above2, up, down):
    near = own_slab(place)[1]
    for one, two, out, flag in ((below1, below2, up, near[0]), (above1, above2, down, near[1])):
        first = planes_of(one, 2, flag)
        second = planes_of(two, 1, flag)
        out[0:64, :] = first[0].reshape(64, LANES)
        out[64:128, :] = jnp.where(one[-8:, :] > 1.5, first[1], second[0]).reshape(64, LANES)


def beyond(one, two, three, near, far):
    a, b, c = planes_of(one, 4, near), planes_of(two, 3, near), planes_of(three, 2, far)
    first, second = one[-8:, :], two[-8:, :]
    two_left = jnp.where(second > 1.5, b[1], c[0])
    three_left = jnp.where(second > 2.5, b[2], jnp.where(second > 1.5, c[0], c[1]))
    return (
        a[0],
        jnp.where(first > 1.5, a[1], b[0]),
        jnp.where(first > 2.5, a[2], jnp.where(first > 1.5, b[0], two_left)),
        jnp.where(
            first > 3.5,
            a[3],
            jnp.where(first > 2.5, b[0], jnp.where(first > 1.5, two_left, three_left)),
        ),
    )


def y_rows(message, row, count, upper):
    value = message[row : row + count, :]
    return ahead(value, 8) if upper else value


def pack_z(place, *refs):
    flags = sides(place)
    lows, highs, (first, last) = refs[:5], refs[5:10], refs[10:]
    for (field, xp, xm, yp, ym), row, out in ((lows, 0, first), (highs, 7, last)):
        for comp in range(6):
            out[comp : comp + 1, :] = field[comp, row : row + 1, :]
        out[6:7, :] = kept(flags[1], xp[row : row + 1, :])
        out[7:8, :] = kept(flags[0], xm[row : row + 1, :])
        out[8:9, :] = kept(flags[3], y_rows(yp, row, 1, row > 0))
        out[9:10, :] = kept(flags[2], y_rows(ym, row, 1, row > 0))
        out[10:16, :] = jnp.zeros((6, LANES), F32)


def curl_chunk(wide, part):
    ex, ey, ez = wide[3 * part], wide[3 * part + 1], wide[3 * part + 2]
    xp, xm, yp, ym = wide[6], wide[7], wide[8], wide[9]
    sx, sy, sz = 3 * part, 3 * part + 1, 3 * part + 2

    def here(v):
        return v[8 : 8 + CHUNK]

    def up(v):
        return v[9 : 9 + CHUNK]

    def down(v):
        return v[7 : 7 + CHUNK]

    upper = [v[8:] for v in (ex, ey, xm, ym)]
    ex_xm = x_before(upper[0], upper[2], sx)
    ey_ym = y_before(upper[1], upper[3], sy)
    ex_xm_up, ex_xm = ex_xm[1 : 1 + CHUNK], ex_xm[:CHUNK]
    ey_ym_up, ey_ym = ey_ym[1 : 1 + CHUNK], ey_ym[:CHUNK]
    lower = [v[: 8 + CHUNK] for v in (ez, xp, yp)]
    ez_xp = x_next(lower[0], lower[1], sz)
    ez_yp = y_next(lower[0], lower[2], sz)
    ez_xp_down, ez_xp = down(ez_xp), ez_xp[8:]
    ez_yp_down, ez_yp = down(ez_yp), ez_yp[8:]
    xp0, xm0, yp0, ym0 = here(xp), here(xm), here(yp), here(ym)
    ex0, ey0, ez0 = here(ex), here(ey), here(ez)
    ex_yp = y_next(ex0, yp0, sx)
    ex_ym = y_before(ex0, ym0, sx)
    ex_xm_yp = x_before(ex_yp, y_next(xm0, yp0, XP_MINUS), sx)
    ey_xp = x_next(ey0, xp0, sy)
    ey_xm = x_before(ey0, xm0, sy)
    ey_xp_ym = x_next(ey_ym, y_before(xp0, ym0, XP_PLUS), sy)
    ez_xm = x_before(ez0, xm0, sz)
    ez_ym = y_before(ez0, ym0, sz)
    kx = 4.0 * ex0 - ex_yp - ex_ym - up(ex) - down(ex)
    kx = kx + (ey_xp - ey0 - ey_xp_ym + ey_ym) + (ez_xp - ez0 - ez_xp_down + down(ez))
    ky = 4.0 * ey0 - ey_xp - ey_xm - up(ey) - down(ey)
    ky = ky + (ex_yp - ex0 - ex_xm_yp + ex_xm) + (ez_yp - ez0 - ez_yp_down + down(ez))
    kz = 4.0 * ez0 - ez_xp - ez_xm - ez_yp - ez_ym
    kz = kz + (up(ex) - ex0 - ex_xm_up + ex_xm) + (up(ey) - ey0 - ey_ym_up + ey_ym)
    return (kx, ky, kz), (ex0, ey0, ez0)


def sweep(last_sweep, place, seg_len, field, drive, conduct, xp, xm, yp, ym, zp, zm, diagonal, solver, *rest):
    if last_sweep:
        field_out, heat_out, ext, columns, solved = rest
    else:
        field_out, first, last, ext, columns, solved = rest
    segs = solver.shape[0]
    flags = sides(place)

    for base in range(0, CZ, CHUNK):
        rows = slice(base, base + CHUNK)
        to = slice(base + HALO, base + HALO + CHUNK)
        for comp in range(6):
            ext[comp, to, :] = field[comp, rows, :]
        ext[6, to, :] = kept(flags[1], xp[rows, :])
        ext[7, to, :] = kept(flags[0], xm[rows, :])
        ext[8, to, :] = kept(flags[3], y_rows(yp, base % HALF, CHUNK, base >= HALF))
        ext[9, to, :] = kept(flags[2], y_rows(ym, base % HALF, CHUNK, base >= HALF))
    for comp in range(10):
        ext[comp, HALO - 1 : HALO, :] = kept(flags[4], zm[comp : comp + 1, :])
        ext[comp, HALO + CZ : HALO + CZ + 1, :] = kept(flags[5], zp[comp : comp + 1, :])

    columns[0:PLANE, :] = jnp.zeros((PLANE, LANES), F32)
    tail = columns.shape[0] - (CZ + 1) * PLANE
    columns[(CZ + 1) * PLANE :, :] = jnp.zeros((tail, LANES), F32)

    def residual(i, carry):
        base = pl.multiple_of(i * CHUNK, CHUNK)
        rows = pl.ds(base, CHUNK)
        wide = [ext[comp, pl.ds(base, CHUNK + 2 * HALO), :] for comp in range(10)]
        curl_real, real = curl_chunk(wide, 0)
        curl_imag, imag = curl_chunk(wide, 1)
        sigma = conduct[0, rows, :]
        for axis in range(3):
            both = (
                curl_real[axis] + mass_shift * real[axis] - sigma * imag[axis],
                curl_imag[axis] + mass_shift * imag[axis] + sigma * real[axis],
            )
            for part in range(2):
                comp = 3 * part + axis
                rest_of = drive[comp, rows, :] - both[part]
                for q in range(4):
                    at = (base + 1) * PLANE + comp * 4 + q
                    columns[pl.ds(at, CHUNK, stride=PLANE), :] = ahead(rest_of, CORNER[q])
        return carry

    lax.fori_loop(0, CZ // CHUNK, residual, 0, unroll=True)

    row_of = lax.broadcasted_iota(jnp.int32, (512, LANES), 0)
    start = jnp.int32(0)
    for s in range(segs):
        length = seg_len[s]
        window = columns[pl.ds(pl.multiple_of(start * PLANE, 8), 512), :]
        window = jnp.where(row_of < (length + 2) * PLANE, window, 0.0).astype(jnp.bfloat16)
        product = jnp.dot(solver[s], window, preferred_element_type=F32)
        scaled = diagonal[s] * window.astype(F32)
        result = coupling_scale * product + scaled
        to = pl.ds(pl.multiple_of(start * PLANE, 8), MAXSEG * PLANE)
        solved[to, :] = result[PLANE : (MAXSEG + 1) * PLANE, :]
        start = start + length

    def update(i, carry):
        base = pl.multiple_of(i * CHUNK, CHUNK)
        rows = pl.ds(base, CHUNK)
        lane = lax.broadcasted_iota(jnp.int32, (CHUNK, LANES), 1)
        parts = []
        for comp in range(6):
            add = jnp.zeros((CHUNK, LANES), F32)
            for q in range(4):
                piece = solved[pl.ds(base * PLANE + comp * 4 + q, CHUNK, stride=PLANE), :]
                add = jnp.where(lane & 17 == CORNER[q], ahead(piece, -CORNER[q]), add)
            part = field[comp, rows, :] + add
            field_out[comp, rows, :] = part
            parts.append(part)
        if last_sweep:
            total = parts[0] * parts[0]
            for part in parts[1:]:
                total = total + part * part
            heat_out[rows, :] = 0.5 * conduct[0, rows, :] * total
        else:
            low, high = x_faces(parts)
            first[rows, :] = low
            last[rows, :] = high
        return carry

    lax.fori_loop(0, CZ // CHUNK, update, 0, unroll=True)


def finish_field(planes, out):
    for comp in range(6):
        for half in range(CZ // LANES):
            lanes = slice(half * LANES, (half + 1) * LANES)
            out[comp, :, lanes] = planes[comp, lanes, :].T


def pack_heat(place, lookup, heat, below, above, out, ext):
    flags = sides(place)
    ext[0:8, :] = kept(flags[4], below[...])
    ext[8 : 8 + CZ, :] = heat[...]
    ext[8 + CZ : 16 + CZ, :] = kept(flags[5], above[...])
    ext[16 + CZ :, :] = jnp.zeros((ext.shape[0] - 16 - CZ, LANES), F32)
    start = 8 - (RING - 1)
    for owner in range(out.shape[0]):
        out[owner] = ext[pl.ds(start, out.shape[1]), :]
        start = start + lookup[owner]


def swap_tiles(value):
    row = lax.broadcasted_iota(jnp.int32, value.shape, value.ndim - 2)
    lane = lane_of(value)
    axis = value.ndim - 2
    for k in range(3):
        step = 1 << k
        row_bit = (row >> k) & 1
        lane_bit = (lane >> (4 + k)) & 1
        up = ahead(pltpu.roll(value, 8 - step, axis), -16 * step)
        down = up if step == 4 else ahead(pltpu.roll(value, step, axis), 16 * step)
        value = jnp.where(row_bit == lane_bit, value, jnp.where(row_bit == 0, up, down))
    return value


def heat_step(place, lookup, slab, below1, above1, below2, above2, below3, above3, arrived, factor_out, warm_out, temp, rates, joule):
    owner, near = own_slab(place)
    count = lookup[owner]
    planes = temp.shape[1]
    owners = arrived.shape[0]
    for plane in range(planes - 2 * RING):
        temp[0, plane + RING] = slab[plane, 0]
        rates[plane + RING] = slab[plane, 1]
    lower = beyond(below1, below2, below3, near[0], near[2])
    upper = beyond(above1, above2, above3, near[1], near[3])
    for depth in range(RING):
        for at, plane in ((RING - 1 - depth, lower[depth]), (RING + count + depth, upper[depth])):
            temp[0, at] = plane[:4]
            rates[at] = plane[4:]
    for owner in range(owners):
        joule[pl.ds(owners + owner, arrived.shape[1], stride=owners), :] = arrived[owner]

    group = 2
    section = time_step / (SECTIONS * SECTIONS)

    def one(step, now, before, base):
        value = temp[now, pl.ds(base - 1, group + 2)]
        mid = value[1:-1]
        lane = lane_of(mid)
        row = lax.broadcasted_iota(jnp.int32, mid.shape, 2)
        none = jnp.zeros_like(mid[:, :1])
        gx_up = jnp.concatenate([mid[:, 1:], none], axis=1)
        gx_down = jnp.concatenate([none, mid[:, :-1]], axis=1)
        gy_up = jnp.where(row == 7, 0.0, pltpu.roll(mid, 7, 2))
        gy_down = jnp.where(row == 0, 0.0, pltpu.roll(mid, 1, 2))
        total = ahead(jnp.where(lane < 16, gx_up, mid), 16)
        total = total + ahead(jnp.where(lane >= 112, gx_down, mid), -16)
        total = total + jnp.where(lane & 15 == 15, ahead(gy_up, -15), ahead(mid, 1))
        total = total + jnp.where(lane & 15 == 0, ahead(gy_down, 15), ahead(mid, -1))
        total = total + value[:-2] + value[2:]
        heat = joule[pl.ds(base * owners, group * owners), :].reshape(group, 4, 8, LANES)
        rate = rates[pl.ds(base, group)] * (total - 6.0 * mid) + heat
        if step == 1:
            temp[before, pl.ds(base, group)] = mid + section * rate
        else:
            old = temp[before, pl.ds(base, group)]
            temp[before, pl.ds(base, group)] = 2.0 * mid - old + 2.0 * section * rate

    for step in range(1, SECTIONS + 1):
        now, before = (step - 1) % 2, step % 2

        for base in range(step, planes - step, group):
            one(step, now, before, base)
    final = SECTIONS % 2
    for plane in range(warm_out.shape[0]):
        result = temp[final, plane + RING]
        warm_out[plane] = result
        joule[plane * owners : (plane + 1) * owners, :] = jnp.exp(-heat_drop * result).reshape(owners, LANES)
    for owner in range(owners):
        factor_out[owner] = joule[pl.ds(owner, factor_out.shape[1], stride=owners), :]


def finish_slab(place, lookup, warm, out):
    count = lookup[own_slab(place)[0]]
    batch = 4
    for base in range(0, out.shape[0], batch):
        value = swap_tiles(warm[base : base + batch].reshape(4 * batch, 8, LANES))
        value = value.reshape(batch, 32, LANES)
        for plane in range(batch):
            out[base + plane] = kept(count > base + plane, value[plane])


def finish_conduct(lookup, returned, conduct, out, rows):
    start = 0
    for owner in range(returned.shape[0]):
        rows[pl.ds(start, returned.shape[1]), :] = returned[owner]
        start = start + lookup[owner]
    for half in range(CZ // LANES):
        lanes = slice(half * LANES, (half + 1) * LANES)
        out[:, lanes] = conduct[:, lanes] * rows[half * LANES : (half + 1) * LANES, :].T


def in_hbm(value):
    return pltpu.with_memory_space_constraint(value, pltpu.HBM)


def shape(*dims):
    return jax.ShapeDtypeStruct(dims, F32)


def body(
    earlier_edge_voltage,
    coil_drive_current,
    sigma_omega_cellwise,
    subdomain_inverse_full,
    subdomain_inverse_main,
    subdomain_layer_counts,
    heat_layer_lookup,
    warming_amount,
    heat_spreading_coef,
):
    count_x, count_y, count_z = (lax.axis_size(axis) for axis in ("gx", "gy", "gz"))
    owners = count_x * count_y
    segs = subdomain_layer_counts.shape[3]
    slab_cap = warming_amount.shape[3]

    def turn(value, axis, step):
        count = lax.axis_size(axis)
        return lax.ppermute(value, axis, [(i, (i + step) % count) for i in range(count)])

    def device(slab):
        return (slab % owners) * count_z + slab // owners

    def ring(value, step):
        total = owners * count_z
        pairs = [(device(i), device((i + step) % total)) for i in range(total)]
        return lax.ppermute(value, ("gx", "gy", "gz"), pairs)

    place = jnp.stack([lax.axis_index(axis) for axis in ("gx", "gy", "gz")]).astype(jnp.int32)
    seg_len = subdomain_layer_counts[0, 0, 0]
    lookup = heat_layer_lookup[0]

    field_bytes = 6 * CZ * LANES * 4
    plane_array = shape(CZ, LANES)
    field, face_low, face_high = pl.pallas_call(
        prepare_field,
        out_shape=(shape(6, CZ, LANES), plane_array, plane_array),
        in_specs=[HBM],
        out_specs=[VMEM] * 3,
        scratch_shapes=[pltpu.VMEM((6, LANES, CZ), F32), pltpu.SemaphoreType.DMA((6,))],
        compiler_params=params(),
        cost_estimate=cost(1 << 20, 2 * field_bytes),
        name="prepare_field",
    )(in_hbm(earlier_edge_voltage.reshape(6, LANES, CZ)))
    x_ghosts = turn(face_low, "gx", -1), turn(face_high, "gx", 1)
    solver = subdomain_inverse_full[0, 0, 0]
    drive, conduct, diagonal, slab, solver = pl.pallas_call(
        prepare_rest,
        out_shape=(
            shape(6, CZ, LANES),
            shape(1, CZ, LANES),
            shape(segs, 512, LANES),
            shape(slab_cap, 2, 4, 8, LANES),
            jax.ShapeDtypeStruct(solver.shape, solver.dtype),
        ),
        in_specs=[HBM] * 6,
        out_specs=[VMEM] * 5,
        scratch_shapes=[
            pltpu.VMEM((6, LANES, CZ), F32),
            pltpu.VMEM((1, LANES, CZ), F32),
            pltpu.VMEM((segs, 512), F32),
            pltpu.VMEM((2, slab_cap, 32, LANES), F32),
            pltpu.SemaphoreType.DMA((9,)),
        ],
        compiler_params=params(),
        cost_estimate=cost(1 << 20, 16 * field_bytes),
        name="prepare_rest",
    )(
        in_hbm(coil_drive_current.reshape(6, LANES, CZ)),
        in_hbm(sigma_omega_cellwise.reshape(1, LANES, CZ)),
        in_hbm(subdomain_inverse_main[0, 0, 0]),
        in_hbm(warming_amount[0, 0, 0]),
        in_hbm(heat_spreading_coef[0, 0, 0]),
        in_hbm(solver),
    )
    x_ghosts, drive, conduct, diagonal, slab, solver = lax.optimization_barrier(
        (x_ghosts, drive, conduct, diagonal, slab, solver)
    )

    def chosen(kernel, rows, *inputs):
        small = inputs[1].ndim == 1
        return pl.pallas_call(
            kernel,
            out_shape=(shape(rows, LANES),) * 2,
            in_specs=[SMEM] * (1 + small) + [VMEM] * (len(inputs) - 1 - small),
            out_specs=[VMEM] * 2,
            compiler_params=params(),
            name=kernel.__name__,
        )(*inputs)

    def halo(field, x_plus, x_minus, source):
        message = shape(HALF, LANES)
        down, up = pl.pallas_call(
            pack_y,
            out_shape=(message, message),
            in_specs=[SMEM] + [VMEM] * 3,
            out_specs=[VMEM] * 2,
            compiler_params=params(),
            cost_estimate=cost(1 << 20, field_bytes),
            name="pack_y",
        )(place, field, x_plus, x_minus)
        y_plus, y_minus = turn(down, "gy", -1), turn(up, "gy", 1)
        planes = []
        if source:
            _, source = lax.optimization_barrier(((down, up), source))
            slab_up, slab_down = chosen(choose_far, 128, place, *source)
            planes = [ring(slab_up, 2), ring(slab_down, -2)]
        ghosts = (x_plus, x_minus, y_plus, y_minus)
        specs = []
        for block, half_block in ((0, 0), (CZ // 8 - 1, HALF // 8 - 1)):
            specs.append(pl.BlockSpec((6, 8, LANES), lambda i, block=block: (0, block, 0)))
            specs += [pl.BlockSpec((8, LANES), lambda i, block=block: (block, 0))] * 2
            specs += [pl.BlockSpec((8, LANES), lambda i, block=half_block: (block, 0))] * 2
        z_low, z_high = pl.pallas_call(
            pack_z,
            grid=(1,),
            out_shape=(shape(16, LANES), shape(16, LANES)),
            in_specs=[SMEM] + specs,
            out_specs=[pl.BlockSpec((16, LANES), lambda i: (0, 0))] * 2,
            compiler_params=params(),
            name="pack_z",
        )(place, field, *ghosts, field, *ghosts)
        z_plus, z_minus = turn(z_low, "gz", -1), turn(z_high, "gz", 1)
        if source:
            (z_plus, z_minus), planes = lax.optimization_barrier(((z_plus, z_minus), planes))
        return ghosts + (z_plus, z_minus), planes

    up, down = chosen(choose_near, 64 * RING + 8, place, lookup, slab)
    received = [ring(up, 1), ring(down, -1)]
    for sweep_index in range(SWEEPS):
        final = sweep_index == SWEEPS - 1
        if final:
            up, down = chosen(choose_next, 64 * (RING - 1) + 8, place, *received)
            received += [ring(up, 1), ring(down, -1)]
            x_ghosts, _, _ = lax.optimization_barrier((x_ghosts, up, down))
        ghosts, planes = halo(field, *x_ghosts, received if final else [])
        received += planes
        scratch = [
            pltpu.VMEM((10, CZ + 2 * HALO, LANES), F32),
            pltpu.VMEM(((CZ + 1 + WINDOW) * PLANE + 8, LANES), F32),
            pltpu.VMEM(((CZ + MAXSEG) * PLANE, LANES), F32),
        ]
        inputs = [place, seg_len, field, drive, conduct, *ghosts, diagonal, solver]
        specs = [SMEM] * 2 + [VMEM] * 11
        if final:
            outs = (shape(6, CZ, LANES), plane_array)
        else:
            outs = (shape(6, CZ, LANES), plane_array, plane_array)
        result = pl.pallas_call(
            functools.partial(sweep, final),
            out_shape=outs,
            in_specs=specs,
            out_specs=[VMEM] * len(outs),
            scratch_shapes=scratch,
            compiler_params=params(),
            cost_estimate=cost(1 << 28, 4 * field_bytes),
            name="sweep",
        )(*inputs)
        if final:
            field, heat = result
        else:
            field, face_low, face_high = result
            x_ghosts = turn(face_low, "gx", -1), turn(face_high, "gx", 1)

    field_new = pl.pallas_call(
        finish_field,
        out_shape=shape(6, LANES, CZ),
        in_specs=[VMEM],
        out_specs=VMEM,
        compiler_params=params(),
        cost_estimate=cost(1 << 20, 2 * field_bytes),
        name="finish_field",
    )(field)
    heat_above, heat_below = turn(heat[:8], "gz", -1), turn(heat[CZ - 8 :], "gz", 1)
    heat_above, heat_below, field_new = lax.optimization_barrier(
        (heat_above, heat_below, field_new)
    )
    rows = slab_cap + 8
    outgoing = pl.pallas_call(
        pack_heat,
        out_shape=shape(owners, rows, LANES),
        in_specs=[SMEM] * 2 + [VMEM] * 3,
        out_specs=VMEM,
        scratch_shapes=[pltpu.VMEM((CZ + 16 + rows, LANES), F32)],
        compiler_params=params(),
        name="pack_heat",
    )(place, lookup, heat, heat_below, heat_above)
    arrived = lax.all_to_all(outgoing, ("gx", "gy"), split_axis=0, concat_axis=0, tiled=True)
    planes = slab_cap + 2 * RING
    factor, warm = pl.pallas_call(
        heat_step,
        out_shape=(shape(owners, slab_cap, LANES), shape(slab_cap, 4, 8, LANES)),
        in_specs=[SMEM] * 2 + [VMEM] * 8,
        out_specs=[VMEM] * 2,
        scratch_shapes=[
            pltpu.VMEM((2, planes, 4, 8, LANES), F32),
            pltpu.VMEM((planes, 4, 8, LANES), F32),
            pltpu.VMEM(((1 + rows) * owners, LANES), F32),
        ],
        compiler_params=params(),
        name="heat_step",
    )(place, lookup, slab, *received, arrived)
    returned = lax.all_to_all(factor, ("gx", "gy"), split_axis=0, concat_axis=0, tiled=True)
    renewed_heat_rise = pl.pallas_call(
        finish_slab,
        out_shape=shape(slab_cap, 32, LANES),
        in_specs=[SMEM, SMEM, VMEM],
        out_specs=VMEM,
        compiler_params=params(),
        name="finish_slab",
    )(place, lookup, warm)
    renewed_sigma_omega = pl.pallas_call(
        finish_conduct,
        out_shape=shape(LANES, CZ),
        in_specs=[SMEM] + [VMEM] * 2,
        out_specs=VMEM,
        scratch_shapes=[pltpu.VMEM((CZ + slab_cap, LANES), F32)],
        compiler_params=params(),
        name="finish_conduct",
    )(lookup, returned, sigma_omega_cellwise.reshape(LANES, CZ))
    return (
        field_new.reshape(6, CX, CY, CZ),
        renewed_heat_rise[None, None, None],
        renewed_sigma_omega.reshape(CX, CY, CZ),
    )


def solution(mesh):
    return jax.shard_map(
        body,
        mesh=mesh,
        in_specs=(
            P(None, "gx", "gy", "gz"),
            P(None, "gx", "gy", "gz"),
            P("gx", "gy", "gz"),
            P("gx", "gy", "gz", None, None, None),
            P("gx", "gy", "gz", None, None),
            P("gx", "gy", "gz", None),
            P("gz", None),
            P("gx", "gy", "gz", None, None, None),
            P("gx", "gy", "gz", None, None, None),
        ),
        out_specs=(
            P(None, "gx", "gy", "gz"),
            P("gx", "gy", "gz", None, None, None),
            P("gx", "gy", "gz"),
        ),
        check_vma=False,
    )
```
